32 devices in a mesh: dp: 8 (over y, x, core), ctx: 4 (over z).
Axes of the slice: x: 2, y: 2, z: 4, core: 2. Of those that a mesh axis runs over, the one named last changes fastest.
Arguments:
- inputs: bfloat16 [4096, 8192], P('ctx', 'dp'), may hold values from -6 to 6
- cotangent: bfloat16 [4096, 8192], P('ctx', 'dp'), may hold values from -6 to 6
- residue: float32 [8192], P('dp'), may hold values from -0.6 to 0.6
- decay: float32 [8192], P('dp'), may hold values from 7.324219e-05 to 0.05
- skip_gain: float32 [8192], P('dp'), may hold values from -4 to 4
- band_blocks: int32 [8, 4], P('dp'), may hold values from 0 to 3, each once within a row
Outputs:
- layer_out: bfloat16 [4096, 8192], P('ctx', 'dp')
- input_grad: bfloat16 [4096, 8192], P('ctx', 'dp')
- skip_grad: float32 [8192], P(('dp', 'ctx'))
- residue_grad: float32 [8192], P(('dp', 'ctx'))
- decay_grad: float32 [8192], P(('dp', 'ctx'))
The draws below stay inside these ranges and needn't reach their ends.
Inputs may be any that keep to these rules, and one draw needn't show every extreme that they name: Each row of band_blocks holds each of 0 to 3 exactly once.
All inputs are finite; a program needn't handle non-finite values.
Results may differ from the reference program's by a relative error of at most 0.0019.
Values may be sent and summed in bfloat16 or wider, within the bound.
A program may use at most 128 MiB of HBM per device.

```python
import math
import jax
import jax.numpy as jnp
from jax import lax

C = 8192
TOK_DEV = 1024
CG = 256
CD = 1024
SEQ = 4096
N_DP = 8
N_CTX = 4


def steps_of(own_key, extent, shards, smallest, largest):
    gain = 1.0
    for axis_at, shards_of in shards:
        draws = jax.random.uniform(jax.random.fold_in(jax.random.fold_in(own_key, 6), axis_at), (shards_of,), jnp.float32, smallest / len(shards), largest / len(shards))
        gain = gain * jnp.repeat(jnp.exp(draws), extent[axis_at] // shards_of).reshape((-1,) + (1,) * (len(extent) - 1 - axis_at))
    return gain


def centred(own_key, dims, spread, bound, split=(), kind=jnp.bfloat16):
    drawn = spread * jax.random.normal(own_key, dims, jnp.float32)
    if split:
        drawn = drawn * steps_of(own_key, dims, split, -0.22, 0.18)
    return jnp.clip(drawn, -bound, bound).astype(kind)


def setup_inputs(seed: int = 0) -> dict:
    streams_of = jax.random.split(jax.random.key(seed), 7)
    return {
        "inputs": centred(streams_of[0], (SEQ, C), 1.0, 6.0, ((0, 4), (1, 8))),
        "cotangent": centred(streams_of[1], (SEQ, C), 1.0, 6.0, ((0, 4), (1, 8))),
        "residue": centred(streams_of[2], (C,), 0.15, 0.6, ((0, 8),), jnp.float32),
        "decay": jnp.clip(jnp.exp(math.log(0.05) - 6.5260067 * jax.random.uniform(streams_of[3], (C,), jnp.float32) ** steps_of(streams_of[3], (C,), ((0, 8),), -0.2, 0.2)), 7.324219041038305e-05, 0.05),
        "skip_gain": centred(streams_of[4], (C,), 1.0, 4.0, ((0, 8),), jnp.float32),
        "band_blocks": jax.vmap(lambda own: jax.random.permutation(own, N_CTX))(jax.random.split(streams_of[5], N_DP)).reshape((N_DP, N_CTX)).astype(jnp.int32),
    }


def compose(earlier_pair, later_pair):
    return (earlier_pair[0] * later_pair[0], earlier_pair[1] * later_pair[0] + later_pair[1])

def causal_sum(values, decay_rate):
    factors = jnp.broadcast_to(jnp.exp(-decay_rate)[None, :], values.shape)
    return lax.associative_scan(compose, (factors, values))[1]

def filtered(values, decay_rate, lengths):
    summed = causal_sum(values, decay_rate)
    shifted_index = jnp.arange(SEQ, dtype=jnp.int32)[:, None] - lengths[None, :]
    earlier = jnp.take_along_axis(summed, jnp.maximum(shifted_index, 0).astype(jnp.int32), axis=0)
    earlier = jnp.where(shifted_index >= 0, earlier, jnp.zeros_like(earlier))
    return summed - jnp.exp(-decay_rate * lengths.astype(jnp.float32))[None, :] * earlier

def reference(inputs, cotangent, residue, decay, skip_gain, band_blocks):
    lengths = jnp.repeat(((band_blocks.reshape(-1) + 1) * TOK_DEV).astype(jnp.int32), CG, total_repeat_length=C)

    def layer(values, res_arg, decay_arg, skip_arg, slab_lengths):
        return skip_arg[None, :] * values + res_arg[None, :] * filtered(values, decay_arg, slab_lengths)

    def one_slab(pack):
        values = pack[0].astype(jnp.float32)
        upstream = pack[1].astype(jnp.float32)
        res_s, dec_s, skip_s, len_s = (pack[2], pack[3], pack[4], pack[5])

        def local_layer(v, r, d, k):
            return layer(v, r, d, k, len_s)
        result, pullback = jax.vjp(local_layer, values, res_s, dec_s, skip_s)
        grad_in, grad_res, grad_decay, grad_skip = pullback(upstream)
        stacked = jnp.stack([grad_skip, grad_res, grad_decay * dec_s])
        return (result.astype(jnp.bfloat16), grad_in.astype(jnp.bfloat16), stacked)
    slab_in = jnp.transpose(inputs.reshape(SEQ, N_DP, CD), (1, 0, 2))
    slab_ct = jnp.transpose(cotangent.reshape(SEQ, N_DP, CD), (1, 0, 2))
    outputs, grads_in, stacked = lax.map(one_slab, (slab_in, slab_ct, residue.reshape(N_DP, CD), decay.reshape(N_DP, CD), skip_gain.reshape(N_DP, CD), lengths.reshape(N_DP, CD)))
    outputs = jnp.transpose(outputs, (1, 0, 2)).reshape(SEQ, C)
    grads_in = jnp.transpose(grads_in, (1, 0, 2)).reshape(SEQ, C)
    grads = jnp.transpose(stacked, (1, 0, 2)).reshape(3, C)
    return (outputs, grads_in, grads[0], grads[1], grads[2])
```

```python
import functools
import jax
import jax.numpy as jnp
from jax import lax
from jax.experimental import pallas as pl
from jax.experimental.pallas import tpu as pltpu
from jax.sharding import PartitionSpec as P


def prefix(value, axis, join, neutral, backward):
    count, mine = (lax.axis_size(axis), lax.axis_index(axis))
    pieces = jax.tree.map(lambda part: lax.all_gather(part, axis), value)
    if backward:
        pieces = jax.tree.map(lambda part: part[::-1], pieces)
        mine = count - 1 - mine
    total = jax.tree.map(
        lambda part, zero: jnp.full_like(part, 0) + jnp.asarray(zero, part.dtype), value, neutral
    )

    def turn(position, total):
        longer = join(total, jax.tree.map(lambda part: part[position], pieces))
        return jax.tree.map(lambda new, old: jnp.where(position < mine, new, old), longer, total)

    return lax.fori_loop(0, count - 1, turn, total)


def compose(earlier_pair, later_pair):
    return (earlier_pair[0] * later_pair[0], earlier_pair[1] * later_pair[0] + later_pair[1])


def chain_step(earlier_pair, later_pair):
    return (earlier_pair[0] * later_pair[1] + later_pair[0], earlier_pair[1] * later_pair[1])


def local_scan(values, decay_rate, backward):
    factors = jnp.broadcast_to(jnp.exp(-decay_rate)[None, :], values.shape)
    return lax.associative_scan(compose, (factors, values), reverse=backward)[1]


def slot_groups(bands, ctx_rank, direction):
    group_count = bands.shape[0]
    slot_index = jnp.arange(group_count, dtype=jnp.int32)
    distance = (slot_index - ctx_rank) * direction
    matches = bands[None, :] + 1 == distance[:, None]
    return jnp.sum(jnp.where(matches, slot_index[None, :], 0), axis=1)


def pick(shaped, order):
    blocks = [
        lax.dynamic_index_in_dim(shaped, order[at], 1, keepdims=True)
        for at in range(order.shape[0])
    ]
    return jnp.concatenate(blocks, axis=1)


def outgoing(values, slot_group, group_count, group_width):
    shaped = values.reshape(values.shape[0], group_count, group_width)
    return pick(shaped, slot_group)


def incoming(received, source, in_range):
    picked = pick(received, source)
    picked = jnp.where(in_range[None, :, None], picked, jnp.zeros((), picked.dtype))
    return picked.reshape(picked.shape[0], -1)


def body(inputs, cotangent, residue, decay, skip_gain, band_blocks):
    values = inputs.astype(jnp.float32)
    upstream = cotangent.astype(jnp.float32)
    bands = band_blocks[0]
    block_rows, channels = values.shape
    group_count = bands.shape[0]
    group_width = channels // group_count
    ctx_rank = lax.axis_index("ctx")
    offsets = jnp.arange(block_rows, dtype=jnp.float32)[:, None]
    lengths = jnp.repeat(
        (bands + 1) * block_rows, group_width, total_repeat_length=channels
    ).astype(jnp.float32)
    band_tail = jnp.exp(-decay * lengths)[None, :]
    block_decay = jnp.exp(-decay * block_rows)
    lead_decay = jnp.exp(-decay[None, :] * (offsets + 1.0))
    trail_decay = jnp.exp(-decay[None, :] * (block_rows - offsets))
    zero_state = jnp.zeros_like(decay)
    unit_state = jnp.ones_like(decay)
    inside = local_scan(values, decay, False)
    before, _ = prefix(
        (inside[-1], block_decay), "ctx", chain_step, (zero_state, unit_state), False
    )
    carried = inside + lead_decay * before[None, :]
    send_fwd = slot_groups(bands, ctx_rank, 1)
    source_fwd = ctx_rank - bands - 1
    valid_fwd = source_fwd >= 0
    source_fwd = jnp.clip(source_fwd, 0, group_count - 1)
    inside_back = local_scan(upstream, decay, True)
    after, _ = prefix(
        (inside_back[0], block_decay), "ctx", chain_step, (zero_state, unit_state), True
    )
    back_carried = inside_back + trail_decay * after[None, :]
    send_bwd = slot_groups(bands, ctx_rank, -1)
    source_bwd = ctx_rank + bands + 1
    valid_bwd = source_bwd < group_count
    source_bwd = jnp.clip(source_bwd, 0, group_count - 1)
    received = lax.all_to_all(
        outgoing(carried, send_fwd, group_count, group_width),
        "ctx",
        split_axis=1,
        concat_axis=1,
        tiled=True,
    )
    far_state = incoming(received, source_fwd, valid_fwd)
    received_back = lax.all_to_all(
        outgoing(back_carried, send_bwd, group_count, group_width),
        "ctx",
        split_axis=1,
        concat_axis=1,
        tiled=True,
    )
    near_state = incoming(received_back, source_bwd, valid_bwd)
    truncated = carried - band_tail * far_state
    layer_out = (skip_gain[None, :] * values + residue[None, :] * truncated).astype(jnp.bfloat16)
    back_truncated = back_carried - band_tail * near_state
    input_grad = (skip_gain[None, :] * upstream + residue[None, :] * back_truncated).astype(
        jnp.bfloat16
    )
    position = ctx_rank.astype(jnp.float32) * block_rows + offsets
    weighted = upstream * truncated
    moment = jnp.sum(position * weighted, axis=0) - jnp.sum(
        position * values * back_truncated, axis=0
    )
    grad_terms = jnp.stack(
        [jnp.sum(values * upstream, axis=0), jnp.sum(weighted, axis=0), -decay * residue * moment]
    )
    share_width = channels // lax.axis_size("ctx")
    summed = lax.psum(grad_terms, "ctx")
    own_share = lax.dynamic_slice_in_dim(summed, ctx_rank * share_width, share_width, 1)
    return (layer_out, input_grad, own_share[0], own_share[1], own_share[2])


MESH = pl.DeviceIdType.MESH
LANES = 128
ROWS = 8
PAIR = 2 * ROWS
PIECES = 4
UNROLL = 4


def greet(count, me):
    barrier = pltpu.get_barrier_semaphore()
    for step in range(1, count):
        pl.semaphore_signal(
            barrier,
            inc=1,
            device_id={"ctx": lax.rem(me + step, count)},
            device_id_type=MESH,
        )
    return lambda: pl.semaphore_wait(barrier, count - 1)


def pieces_of(count, slot):
    return PIECES if slot == count - 2 else 1


def pair_at(step):
    return pl.ds(pl.multiple_of(step * PAIR, PAIR), PAIR)


def banded_kernel(
    count,
    bands,
    x_hbm,
    c_hbm,
    residue_ref,
    decay_ref,
    skip_ref,
    out_hbm,
    grad_hbm,
    total_ref,
    x_all,
    c_all,
    xs,
    cs,
    far_x,
    far_c,
    ends,
    far_ends,
    outs,
    grads,
    sums,
    got,
    load_sem,
    store_sem,
    x_send,
    x_recv,
    c_send,
    c_recv,
    e_send,
    e_recv,
    s_send,
    s_recv,
):
    me = lax.axis_index("ctx")
    _, rows, width = x_all.shape
    shape = (ROWS, width)
    steps = rows // PAIR

    def load(source, target, at, group):
        lanes = pl.ds(group * width, width)
        return pltpu.make_async_copy(
            source.at[:, lanes], target.at[group], load_sem.at[at, group]
        )

    for at, (source, target) in enumerate(((x_hbm, x_all), (c_hbm, c_all))):
        for group in range(count):
            load(source, target, at, group).start()
    all_here = greet(count, me)
    groups = []
    for slot in range(count):
        group = jnp.int32(0)
        for other in range(count):
            group = jnp.where(bands[other] == slot, other, group)
        groups.append(group)

    def pack(whole, packed):
        def turn(step, _):
            at = pair_at(step)
            for slot in range(count):
                packed[slot, at, :] = whole[groups[slot], at, :]
            return 0

        lax.fori_loop(0, steps, turn, 0, unroll=UNROLL)

    for at, (source, target, packed) in enumerate(((x_hbm, x_all, xs), (c_hbm, c_all, cs))):
        for group in range(count):
            load(source, target, at, group).wait()
        pack(target, packed)

    first_sem = [sum(pieces_of(count, s) for s in range(slot)) for slot in range(count)]

    def x_copy(slot, piece):
        size = rows // pieces_of(count, slot)
        at = pl.ds(piece * size, size)
        sem = first_sem[slot] + piece
        return pltpu.make_async_remote_copy(
            src_ref=xs.at[slot, at],
            dst_ref=far_x.at[slot, at],
            send_sem=x_send.at[sem],
            recv_sem=x_recv.at[sem],
            device_id={"ctx": lax.rem(me + slot + 1, count)},
            device_id_type=MESH,
        )

    def c_copy(slot, piece):
        size = rows // pieces_of(count, slot)
        at = pl.ds(rows - (piece + 1) * size, size)
        sem = first_sem[slot] + piece
        return pltpu.make_async_remote_copy(
            src_ref=cs.at[slot, at],
            dst_ref=far_c.at[slot, at],
            send_sem=c_send.at[sem],
            recv_sem=c_recv.at[sem],
            device_id={"ctx": lax.rem(me + count - slot - 1, count)},
            device_id_type=MESH,
        )

    def small_copy(source, target, send, recv, step):
        return pltpu.make_async_remote_copy(
            src_ref=source,
            dst_ref=target,
            send_sem=send.at[step],
            recv_sem=recv.at[step],
            device_id={"ctx": lax.rem(me + step + 1, count)},
            device_id_type=MESH,
        )

    def end_copy(step):
        return small_copy(ends, far_ends.at[me], e_send, e_recv, step)

    def share_copy(slot, step):
        at = slot * (count - 1) + step
        return pltpu.make_async_remote_copy(
            src_ref=sums.at[slot],
            dst_ref=got.at[step, slot],
            send_sem=s_send.at[at],
            recv_sem=s_recv.at[at],
            device_id={"ctx": lax.rem(me + step + 1, count)},
            device_id_type=MESH,
        )

    def store(slot, piece, backward):
        pieces = pieces_of(count, slot)
        size = rows // pieces
        source, target = (grads, grad_hbm) if backward else (outs, out_hbm)
        at = pl.ds(rows - (piece + 1) * size if backward else piece * size, size)
        sem = store_sem.at[int(backward), first_sem[slot] + piece]
        return pltpu.make_async_copy(source.at[slot, at], target.at[slot, at], sem)

    def send(slot):
        for piece in range(pieces_of(count, slot)):
            pl.when(me + slot + 1 < count)(lambda: x_copy(slot, piece).start())
            pl.when(me >= slot + 1)(lambda: c_copy(slot, piece).start())

    all_here()
    send(0)

    level = lax.broadcasted_iota(jnp.int32, shape, 0)
    depth = level.astype(jnp.float32)
    zero = jnp.zeros(shape, jnp.float32)
    for slot in range(count):
        rate = decay_ref[groups[slot]]
        leap_pair = jnp.broadcast_to(jnp.exp(-rate * PAIR), shape)

        def turn(step, held):
            ahead = xs[slot, pair_at(step), :].astype(jnp.float32)
            back = cs[slot, pair_at(steps - 1 - step), :].astype(jnp.float32)
            parts = (ahead[:ROWS], ahead[ROWS:], back[:ROWS], back[ROWS:])
            return tuple(old * leap_pair + new for old, new in zip(held, parts))

        upper, lower, back_upper, back_lower = lax.fori_loop(
            0, steps, turn, (zero,) * 4, unroll=UNROLL
        )
        last = upper * jnp.exp(-rate * (PAIR - 1 - depth)) + lower * jnp.exp(
            -rate * (ROWS - 1 - depth)
        )
        first = back_upper * jnp.exp(-rate * depth) + back_lower * jnp.exp(
            -rate * (ROWS + depth)
        )
        ends[slot, 0:1, :] = jnp.sum(last, axis=0, keepdims=True)
        ends[slot, 1:2, :] = jnp.sum(first, axis=0, keepdims=True)
    for step in range(count - 1):
        end_copy(step).start()
    for slot in range(1, count - 1):
        send(slot)
    for step in range(count - 1):
        end_copy(step).wait()

    def scan(tile, hops):
        for hop, factor in hops:
            tile = tile + factor * pltpu.roll(tile, hop, 0)
        return tile

    def work(slot):
        band = slot + 1
        has_before = me >= band
        has_after = me + band < count
        reach = slot < count - 1
        rate = decay_ref[groups[slot]]
        residue_row = residue_ref[groups[slot]]
        carry = jnp.zeros((1, width), jnp.float32)
        back_carry = carry
        for other in range(count):
            apart = me - 1 - other
            kept = jnp.logical_and(apart >= 0, apart < band)
            factor = jnp.exp(-rate * (jnp.maximum(apart, 0) * rows).astype(jnp.float32))
            carry = carry + jnp.where(kept, factor * far_ends[other, slot, 0:1, :], 0.0)
            apart = other - me - 1
            kept = jnp.logical_and(apart >= 0, apart < band)
            factor = jnp.exp(-rate * (jnp.maximum(apart, 0) * rows).astype(jnp.float32))
            back_carry = back_carry + jnp.where(
                kept, factor * far_ends[other, slot, 1:2, :], 0.0
            )
        tail = jnp.broadcast_to(jnp.exp(-rate * float(band * rows)), shape)
        leap = jnp.broadcast_to(jnp.exp(-rate * ROWS), shape)
        residue = jnp.broadcast_to(residue_row, shape)
        skip = jnp.broadcast_to(skip_ref[groups[slot]], shape)
        lead = jnp.exp(-rate * (depth + 1.0))
        trail = jnp.exp(-rate * (ROWS - depth))
        fwd = [
            (hop, jnp.where(level >= hop, jnp.exp(-rate * hop), 0.0)) for hop in (1, 2, 4)
        ]
        bwd = [
            (ROWS - hop, jnp.where(level < ROWS - hop, jnp.exp(-rate * hop), 0.0))
            for hop in (1, 2, 4)
        ]

        def forward(step, state):
            carry, s_skip, s_w, s_tw = state
            at = pair_at(step)
            base = (step * PAIR).astype(jnp.float32)
            x = xs[slot, at, :].astype(jnp.float32)
            c = cs[slot, at, :].astype(jnp.float32)
            if reach:
                far = far_x[slot, at, :].astype(jnp.float32)
            made = []
            for half in range(2):
                part = slice(half * ROWS, (half + 1) * ROWS)
                fresh = x[part]
                if reach:
                    fresh = fresh - jnp.where(has_before, tail * far[part], 0.0)
                local = scan(fresh, fwd)
                truncated = local + lead * carry
                carry = leap * carry + jnp.broadcast_to(local[ROWS - 1 :], shape)
                made.append(skip * x[part] + residue * truncated)
                w = c[part] * truncated
                s_skip = s_skip + x[part] * c[part]
                s_w = s_w + w
                s_tw = s_tw + (base + half * ROWS) * w
            outs[slot, at, :] = jnp.concatenate(made, axis=0).astype(outs.dtype)
            return carry, s_skip, s_w, s_tw

        def backward(step, state):
            carry, unused, s_v, s_tv = state
            at = pair_at(steps - 1 - step)
            base = ((steps - 1 - step) * PAIR).astype(jnp.float32)
            x = xs[slot, at, :].astype(jnp.float32)
            c = cs[slot, at, :].astype(jnp.float32)
            if reach:
                far = far_c[slot, at, :].astype(jnp.float32)
            made = [None, None]
            for half in (1, 0):
                part = slice(half * ROWS, (half + 1) * ROWS)
                fresh = c[part]
                if reach:
                    fresh = fresh - jnp.where(has_after, tail * far[part], 0.0)
                local = scan(fresh, bwd)
                truncated = local + trail * carry
                carry = leap * carry + jnp.broadcast_to(local[:1], shape)
                made[half] = skip * c[part] + residue * truncated
                v = x[part] * truncated
                s_v = s_v + v
                s_tv = s_tv + (base + half * ROWS) * v
            grads[slot, at, :] = jnp.concatenate(made, axis=0).astype(grads.dtype)
            return carry, unused, s_v, s_tv

        ahead = (jnp.broadcast_to(carry, shape), zero, zero, zero)
        back = (jnp.broadcast_to(back_carry, shape), zero, zero, zero)
        pieces = pieces_of(count, slot)

        def run(backwards, state):
            for piece in range(pieces):
                span = (piece * steps // pieces, (piece + 1) * steps // pieces)
                if reach and backwards:
                    pl.when(has_after)(lambda: c_copy(slot, piece).wait_recv())
                elif reach:
                    pl.when(has_before)(lambda: x_copy(slot, piece).wait_recv())
                turn = backward if backwards else forward
                state = lax.fori_loop(*span, turn, state, unroll=UNROLL)
                store(slot, piece, backwards).start()
            return state

        if not reach or 2 * band < count:
            ahead = run(False, ahead)
            back = run(True, back)
            close(slot, rate, residue_row, ahead, back)
            return None
        ready = lax.cond(has_after, lambda: run(False, ahead), lambda: run(True, back))

        def rest():
            late = lax.cond(has_after, lambda: run(True, back), lambda: run(False, ahead))
            pick = lambda left, right: tuple(
                jnp.where(has_after, one, two) for one, two in zip(left, right)
            )
            close(slot, rate, residue_row, pick(ready, late), pick(late, ready))

        return rest

    def close(slot, rate, residue_row, ahead, back):
        _, s_skip, s_w, s_tw = ahead
        _, _, s_v, s_tv = back
        offset = depth + (me * rows).astype(jnp.float32)
        moment = (s_tw - s_tv) + offset * (s_w - s_v)
        sums[slot, 0:1, :] = jnp.sum(s_skip, axis=0, keepdims=True)
        sums[slot, 1:2, :] = jnp.sum(s_w, axis=0, keepdims=True)
        sums[slot, 2:3, :] = (
            -rate * residue_row * jnp.sum(moment, axis=0, keepdims=True)
        )
        for step in range(count - 1):
            share_copy(slot, step).start()

    sums[...] = jnp.zeros_like(sums)
    work(count - 1)
    pending = [work(slot) for slot in range(count - 1)]
    for rest in pending:
        if rest is not None:
            rest()

    for slot in range(count):
        for piece in range(pieces_of(count, slot)):
            store(slot, piece, False).wait()
            store(slot, piece, True).wait()
    for slot in range(count):
        total = sums[slot]
        for step in range(count - 1):
            share_copy(slot, step).wait()
            total = total + got[step, slot]
        total_ref[slot] = total
    for slot in range(count - 1):
        for piece in range(pieces_of(count, slot)):
            pl.when(me + slot + 1 < count)(lambda: x_copy(slot, piece).wait_send())
            pl.when(me >= slot + 1)(lambda: c_copy(slot, piece).wait_send())


def place_kernel(bands, out, grad, total, out_ref, grad_ref, skip_ref, residue_ref, decay_ref):
    out_ref[...] = out[0]
    grad_ref[...] = grad[0]
    own = total[bands[lax.axis_index("ctx")]]
    skip_ref[...] = own[0:1]
    residue_ref[...] = own[1:2]
    decay_ref[...] = own[2:3]


def place(bands, outs, grads, totals):
    count, rows, width = outs.shape
    slot = pl.BlockSpec((1, rows, width), lambda g, r, bands: (bands[g], r, 0))
    block = pl.BlockSpec((rows, width), lambda g, r, bands: (r, g))
    one = pl.BlockSpec((1, width), lambda g, r, bands: (0, 0))
    whole = jax.ShapeDtypeStruct((rows, count * width), outs.dtype)
    small = jax.ShapeDtypeStruct((1, width), totals.dtype)
    return pl.pallas_call(
        place_kernel,
        grid_spec=pltpu.PrefetchScalarGridSpec(
            num_scalar_prefetch=1,
            grid=(count, 1),
            in_specs=[
                slot,
                slot,
                pl.BlockSpec(totals.shape, lambda g, r, bands: (0, 0, 0)),
            ],
            out_specs=[block, block, one, one, one],
        ),
        out_shape=(whole, whole, small, small, small),
        name="place",
    )(bands, outs, grads, totals)


def banded(count, inputs, cotangent, residue, decay, skip_gain, band_blocks):
    rows, channels = inputs.shape
    width = channels // count
    bands = band_blocks[0]
    anywhere = pl.BlockSpec(memory_space=pl.ANY)
    inside = pl.BlockSpec(memory_space=pltpu.VMEM)
    flows = sum(pieces_of(count, slot) for slot in range(count))
    many = pltpu.SemaphoreType.DMA((flows,))
    few = pltpu.SemaphoreType.DMA((count - 1,))
    some = pltpu.SemaphoreType.DMA((count * (count - 1),))
    packed = pltpu.VMEM((count, rows, width), inputs.dtype)
    far = pltpu.VMEM((count - 1, rows, width), inputs.dtype)
    outs, grads, totals = pl.pallas_call(
        functools.partial(banded_kernel, count),
        in_specs=[
            pl.BlockSpec(memory_space=pltpu.SMEM),
            anywhere,
            anywhere,
            inside,
            inside,
            inside,
        ],
        out_specs=[anywhere, anywhere, inside],
        out_shape=(
            jax.ShapeDtypeStruct((count, rows, width), inputs.dtype),
            jax.ShapeDtypeStruct((count, rows, width), inputs.dtype),
            jax.ShapeDtypeStruct((count, ROWS // 2, width), jnp.float32),
        ),
        scratch_shapes=[
            packed,
            packed,
            packed,
            packed,
            far,
            far,
            pltpu.VMEM((count, 2, width), jnp.float32),
            pltpu.VMEM((count, count, 2, width), jnp.float32),
            packed,
            packed,
            pltpu.VMEM((count, ROWS // 2, width), jnp.float32),
            pltpu.VMEM((count - 1, count, ROWS // 2, width), jnp.float32),
            pltpu.SemaphoreType.DMA((2, count)),
            pltpu.SemaphoreType.DMA((2, flows)),
            many,
            many,
            many,
            many,
            few,
            few,
            some,
            some,
        ],
        compiler_params=pltpu.CompilerParams(collective_id=0, has_side_effects=True),
        name="banded",
    )(
        bands,
        inputs,
        cotangent,
        *(part.reshape(count, 1, width) for part in (residue, decay, skip_gain)),
    )
    layer_out, input_grad, *sums = place(bands, outs, grads, totals)
    return (layer_out, input_grad, *(part.reshape(width) for part in sums))


def local_body(count, inputs, cotangent, residue, decay, skip_gain, band_blocks):
    rows, channels = inputs.shape
    groups = band_blocks.shape[1]
    fits = groups == count and count > 1 and rows % (PAIR * PIECES) == 0
    if fits and channels % (groups * LANES) == 0:
        return banded(count, inputs, cotangent, residue, decay, skip_gain, band_blocks)
    return body(inputs, cotangent, residue, decay, skip_gain, band_blocks)


def solution(mesh):
    placed = (P("ctx", "dp"), P("ctx", "dp"), P("dp"), P("dp"), P("dp"), P("dp", None))
    return jax.shard_map(
        functools.partial(local_body, mesh.shape["ctx"]),
        mesh=mesh,
        in_specs=placed,
        out_specs=(
            P("ctx", "dp"),
            P("ctx", "dp"),
            P(("dp", "ctx")),
            P(("dp", "ctx")),
            P(("dp", "ctx")),
        ),
        check_vma=False,
    )
```

```python
import functools
import jax
import jax.numpy as jnp
from jax import lax
from jax.experimental import pallas as pl
from jax.experimental.pallas import tpu as pltpu
from jax.sharding import PartitionSpec as P


def prefix(value, axis, join, neutral, backward):
    count, mine = (lax.axis_size(axis), lax.axis_index(axis))
    pieces = jax.tree.map(lambda part: lax.all_gather(part, axis), value)
    if backward:
        pieces = jax.tree.map(lambda part: part[::-1], pieces)
        mine = count - 1 - mine
    total = jax.tree.map(
        lambda part, zero: jnp.full_like(part, 0) + jnp.asarray(zero, part.dtype), value, neutral
    )

    def turn(position, total):
        longer = join(total, jax.tree.map(lambda part: part[position], pieces))
        return jax.tree.map(lambda new, old: jnp.where(position < mine, new, old), longer, total)

    return lax.fori_loop(0, count - 1, turn, total)


def compose(earlier_pair, later_pair):
    return (earlier_pair[0] * later_pair[0], earlier_pair[1] * later_pair[0] + later_pair[1])


def chain_step(earlier_pair, later_pair):
    return (earlier_pair[0] * later_pair[1] + later_pair[0], earlier_pair[1] * later_pair[1])


def local_scan(values, decay_rate, backward):
    factors = jnp.broadcast_to(jnp.exp(-decay_rate)[None, :], values.shape)
    return lax.associative_scan(compose, (factors, values), reverse=backward)[1]


def slot_groups(bands, ctx_rank, direction):
    group_count = bands.shape[0]
    slot_index = jnp.arange(group_count, dtype=jnp.int32)
    distance = (slot_index - ctx_rank) * direction
    matches = bands[None, :] + 1 == distance[:, None]
    return jnp.sum(jnp.where(matches, slot_index[None, :], 0), axis=1)


def pick(shaped, order):
    blocks = [
        lax.dynamic_index_in_dim(shaped, order[at], 1, keepdims=True)
        for at in range(order.shape[0])
    ]
    return jnp.concatenate(blocks, axis=1)


def outgoing(values, slot_group, group_count, group_width):
    shaped = values.reshape(values.shape[0], group_count, group_width)
    return pick(shaped, slot_group)


def incoming(received, source, in_range):
    picked = pick(received, source)
    picked = jnp.where(in_range[None, :, None], picked, jnp.zeros((), picked.dtype))
    return picked.reshape(picked.shape[0], -1)


def body(inputs, cotangent, residue, decay, skip_gain, band_blocks):
    values = inputs.astype(jnp.float32)
    upstream = cotangent.astype(jnp.float32)
    bands = band_blocks[0]
    block_rows, channels = values.shape
    group_count = bands.shape[0]
    group_width = channels // group_count
    ctx_rank = lax.axis_index("ctx")
    offsets = jnp.arange(block_rows, dtype=jnp.float32)[:, None]
    lengths = jnp.repeat(
        (bands + 1) * block_rows, group_width, total_repeat_length=channels
    ).astype(jnp.float32)
    band_tail = jnp.exp(-decay * lengths)[None, :]
    block_decay = jnp.exp(-decay * block_rows)
    lead_decay = jnp.exp(-decay[None, :] * (offsets + 1.0))
    trail_decay = jnp.exp(-decay[None, :] * (block_rows - offsets))
    zero_state = jnp.zeros_like(decay)
    unit_state = jnp.ones_like(decay)
    inside = local_scan(values, decay, False)
    before, _ = prefix(
        (inside[-1], block_decay), "ctx", chain_step, (zero_state, unit_state), False
    )
    carried = inside + lead_decay * before[None, :]
    send_fwd = slot_groups(bands, ctx_rank, 1)
    source_fwd = ctx_rank - bands - 1
    valid_fwd = source_fwd >= 0
    source_fwd = jnp.clip(source_fwd, 0, group_count - 1)
    inside_back = local_scan(upstream, decay, True)
    after, _ = prefix(
        (inside_back[0], block_decay), "ctx", chain_step, (zero_state, unit_state), True
    )
    back_carried = inside_back + trail_decay * after[None, :]
    send_bwd = slot_groups(bands, ctx_rank, -1)
    source_bwd = ctx_rank + bands + 1
    valid_bwd = source_bwd < group_count
    source_bwd = jnp.clip(source_bwd, 0, group_count - 1)
    received = lax.all_to_all(
        outgoing(carried, send_fwd, group_count, group_width),
        "ctx",
        split_axis=1,
        concat_axis=1,
        tiled=True,
    )
    far_state = incoming(received, source_fwd, valid_fwd)
    received_back = lax.all_to_all(
        outgoing(back_carried, send_bwd, group_count, group_width),
        "ctx",
        split_axis=1,
        concat_axis=1,
        tiled=True,
    )
    near_state = incoming(received_back, source_bwd, valid_bwd)
    truncated = carried - band_tail * far_state
    layer_out = (skip_gain[None, :] * values + residue[None, :] * truncated).astype(jnp.bfloat16)
    back_truncated = back_carried - band_tail * near_state
    input_grad = (skip_gain[None, :] * upstream + residue[None, :] * back_truncated).astype(
        jnp.bfloat16
    )
    position = ctx_rank.astype(jnp.float32) * block_rows + offsets
    weighted = upstream * truncated
    moment = jnp.sum(position * weighted, axis=0) - jnp.sum(
        position * values * back_truncated, axis=0
    )
    grad_terms = jnp.stack(
        [jnp.sum(values * upstream, axis=0), jnp.sum(weighted, axis=0), -decay * residue * moment]
    )
    share_width = channels // lax.axis_size("ctx")
    summed = lax.psum(grad_terms, "ctx")
    own_share = lax.dynamic_slice_in_dim(summed, ctx_rank * share_width, share_width, 1)
    return (layer_out, input_grad, own_share[0], own_share[1], own_share[2])


MESH = pl.DeviceIdType.MESH
LANES = 128
ROWS = 8
PAIR = 2 * ROWS
PIECES = 8
UNROLL = 4
SCOPED = 51_500_000


def greet(count, me):
    barrier = pltpu.get_barrier_semaphore()
    for step in range(1, count):
        pl.semaphore_signal(
            barrier,
            inc=1,
            device_id={"ctx": lax.rem(me + step, count)},
            device_id_type=MESH,
        )
    return lambda: pl.semaphore_wait(barrier, count - 1)


def parts_of(slot, backward):
    if backward:
        return {0: (2, 4, 1, 1), 1: (2, 6)}.get(slot, (8,))
    return {1: (4, 2, 2)}.get(slot, (2, 6))


def kept_back(slot, backward):
    if backward:
        return 2 if slot == 0 else 0
    return 1 if slot == 1 else 0


def piece_rows(rows, slot, backward, piece):
    parts = parts_of(slot, backward)
    size = rows * parts[piece] // PIECES
    start = rows * sum(parts[:piece]) // PIECES
    return (rows - start - size if backward else start, size)


def piece_at(slot, backward, piece):
    return sum(len(parts_of(before, backward)) for before in range(slot)) + piece


def flow_count(count, backward):
    return sum(len(parts_of(slot, backward)) for slot in range(count - 1))


def pair_at(step):
    return pl.ds(pl.multiple_of(step * PAIR, PAIR), PAIR)


def banded_kernel(
    count,
    bands_hbm,
    x_hbm,
    c_hbm,
    residue_hbm,
    decay_hbm,
    skip_hbm,
    outs,
    grads,
    own_ref,
    bands,
    residue_ref,
    decay_ref,
    skip_ref,
    x_first,
    x_rest,
    c_first,
    c_rest,
    xs,
    cs,
    far_x,
    far_c,
    ends,
    far_ends,
    sums,
    got,
    totals,
    blank,
    small_sem,
    load_sem,
    x_send,
    x_recv,
    c_send,
    c_recv,
    e_send,
    e_recv,
    s_send,
    s_recv,
):
    me = lax.axis_index("ctx")
    _, rows, width = xs.shape
    shape = (ROWS, width)
    first = x_first.shape[1]

    all_here = greet(count, me)

    small = [
        pltpu.make_async_copy(source, target, small_sem.at[at])
        for at, (source, target) in enumerate(
            (
                (bands_hbm, bands),
                (decay_hbm, decay_ref),
                (residue_hbm, residue_ref),
                (skip_hbm, skip_ref),
            )
        )
    ]
    small[0].start()
    chunks = (
        (c_hbm, rows - first, c_first, cs),
        (x_hbm, 0, x_first, xs),
        (c_hbm, 0, c_rest, cs),
        (x_hbm, first, x_rest, xs),
    )

    def load(chunk, group):
        source, start, target, _ = chunks[chunk]
        lanes = pl.ds(group * width, width)
        return pltpu.make_async_copy(
            source.at[pl.ds(start, target.shape[1]), lanes],
            target.at[group],
            load_sem.at[chunk, group],
        )

    for chunk in range(len(chunks)):
        for group in range(count):
            load(chunk, group).start()
    for copy in small[1:]:
        copy.start()
    small[0].wait()
    groups = []
    for slot in range(count):
        group = jnp.int32(0)
        for other in range(count):
            group = jnp.where(bands[other] == slot, other, group)
        groups.append(group)

    def pack(chunk):
        _, start, whole, packed = chunks[chunk]
        for group in range(count):
            load(chunk, group).wait()

        def turn(step, _):
            to = pl.ds(pl.multiple_of(start + step * PAIR, PAIR), PAIR)
            for slot in range(count):
                packed[slot, to, :] = whole[groups[slot], pair_at(step), :]
            return 0

        lax.fori_loop(0, whole.shape[1] // PAIR, turn, 0, unroll=UNROLL)

    def has_source(slot, backward):
        return me + slot + 1 < count if backward else me >= slot + 1

    def flow(slot, backward, piece):
        start, size = piece_rows(rows, slot, backward, piece)
        at = pl.ds(start, size)
        sem = piece_at(slot, backward, piece)
        source, target, sends, recvs = (
            (cs, far_c, c_send, c_recv) if backward else (xs, far_x, x_send, x_recv)
        )
        to = me + count - slot - 1 if backward else me + slot + 1
        return pltpu.make_async_remote_copy(
            src_ref=source.at[slot, at],
            dst_ref=target.at[slot, at],
            send_sem=sends.at[sem],
            recv_sem=recvs.at[sem],
            device_id={"ctx": lax.rem(to, count)},
            device_id_type=MESH,
        )

    def each_piece(slots, backward, pick, act):
        for slot in slots:
            sends_it = has_source(slot, not backward)
            for piece in pick(slot, len(parts_of(slot, backward))):
                pl.when(sends_it)(lambda: act(flow(slot, backward, piece)))

    def send(slots, backward, pick):
        each_piece(slots, backward, pick, lambda copy: copy.start())

    def small_copy(source, target, sends, recvs, step):
        return pltpu.make_async_remote_copy(
            src_ref=source,
            dst_ref=target,
            send_sem=sends.at[step],
            recv_sem=recvs.at[step],
            device_id={"ctx": lax.rem(me + step + 1, count)},
            device_id_type=MESH,
        )

    def end_copy(step):
        return small_copy(ends, far_ends.at[me], e_send, e_recv, step)

    def share_copy(step):
        return small_copy(sums, got.at[step], s_send, s_recv, step)

    middle = tuple(range(2, count - 1))
    up_order = middle[::-1] + (0, 1)
    down_order = (1,) + middle + (0,)
    pack(0)
    all_here()
    send((1, 0), True, lambda slot, many: (0,))
    pack(1)
    send(middle[::-1] + (0,), False, lambda slot, many: (0,))
    pack(2)
    pack(3)
    for copy in small[1:]:
        copy.wait()

    level = lax.broadcasted_iota(jnp.int32, shape, 0)
    depth = level.astype(jnp.float32)
    blank[...] = jnp.zeros(shape, jnp.float32)
    zero = blank[...]
    steps = rows // PAIR
    ends[...] = jnp.zeros_like(ends)
    for slot in range(count):
        rate = decay_ref[groups[slot]]
        leap_pair = jnp.broadcast_to(jnp.exp(-rate * PAIR), shape)
        wide_pair = leap_pair * float(PAIR)
        weighted = {0: (0, 1), 1: (2, 3)}.get(slot, ())

        def turn(step, state):
            held, moments = state
            ahead = xs[slot, pair_at(step), :].astype(jnp.float32)
            back = cs[slot, pair_at(steps - 1 - step), :].astype(jnp.float32)
            parts = (ahead[:ROWS], ahead[ROWS:], back[:ROWS], back[ROWS:])
            moments = tuple(
                moment * leap_pair + held[at] * wide_pair
                for moment, at in zip(moments, weighted)
            )
            return (
                tuple(old * leap_pair + new for old, new in zip(held, parts)),
                moments,
            )

        held, moments = lax.fori_loop(
            0, steps, turn, ((zero,) * 4, (zero,) * len(weighted)), unroll=UNROLL
        )
        apart = (PAIR - 1 - depth, ROWS - 1 - depth, depth, ROWS + depth)
        factors = [jnp.exp(-rate * far) for far in apart]
        scaled = [one * factor for one, factor in zip(held, factors)]
        ends[slot, 0:1, :] = jnp.sum(scaled[0] + scaled[1], axis=0, keepdims=True)
        ends[slot, 1:2, :] = jnp.sum(scaled[2] + scaled[3], axis=0, keepdims=True)
        if weighted:
            both = zero
            for moment, at in zip(moments, weighted):
                both = both + factors[at] * moment + apart[at] * scaled[at]
            ends[slot, 2:3, :] = jnp.sum(both, axis=0, keepdims=True)
    for step in range(count - 1):
        end_copy(step).start()

    def later(slot, backward):
        many = len(parts_of(slot, backward))
        begun = backward and slot < 2 or not backward and slot != 1
        return (1 if begun else 0, many - kept_back(slot, backward))

    send(down_order, True, lambda slot, many: range(*later(slot, True)))
    send(up_order, False, lambda slot, many: range(*later(slot, False)))

    for slot in range(count - 1):
        for backward, far in ((False, far_x), (True, far_c)):

            @pl.when(jnp.logical_not(has_source(slot, backward)))
            def _():
                def clear(step, _):
                    far[slot, pair_at(step), :] = jnp.zeros((PAIR, width), far.dtype)
                    return 0

                lax.fori_loop(0, steps, clear, 0, unroll=UNROLL)

    for step in range(count - 1):
        end_copy(step).wait()

    def scan(tile, hops):
        for hop, turn, factor in hops:
            tile = tile + factor * pltpu.roll(tile, turn, 0)
        return tile

    def scan_both(tile, moment, hops):
        for hop, turn, factor in hops:
            moved = pltpu.roll(tile, turn, 0)
            moment = moment + factor * (pltpu.roll(moment, turn, 0) + float(hop) * moved)
            tile = tile + factor * moved
        return tile, moment

    def run(slot, backward, mode):
        band = slot + 1
        reach = slot < count - 1
        one = mode == "one"
        rate = decay_ref[groups[slot]]
        start = jnp.zeros((1, width), jnp.float32)
        start_moment = start
        row = int(backward)
        for other in range(count):
            apart = other - me - 1 if backward else me - 1 - other
            kept = jnp.logical_and(apart >= 0, apart < band)
            span = (jnp.maximum(apart, 0) * rows).astype(jnp.float32)
            factor = jnp.exp(-rate * span)
            end = far_ends[other, slot, row : row + 1, :]
            start = start + jnp.where(kept, factor * end, 0.0)
            if one:
                moment = far_ends[other, slot, 2:3, :] + span * end
                start_moment = start_moment + jnp.where(kept, factor * moment, 0.0)
        tail_row = jnp.exp(-rate * float(band * rows))
        tail = jnp.broadcast_to(tail_row, shape)
        far_tail = jnp.broadcast_to(tail_row * float(band * rows), shape)
        leap = jnp.broadcast_to(jnp.exp(-rate * ROWS), shape)
        wide = leap * float(ROWS)
        residue = jnp.broadcast_to(residue_ref[groups[slot]], shape)
        skip = jnp.broadcast_to(skip_ref[groups[slot]], shape)
        ahead = ROWS - depth if backward else depth + 1.0
        lead = jnp.exp(-rate * ahead)
        lead_moment = lead * ahead
        hops = []
        for hop in (1, 2, 4):
            inside = level < ROWS - hop if backward else level >= hop
            factor = jnp.where(inside, jnp.exp(-rate * hop), 0.0)
            hops.append((hop, ROWS - hop if backward else hop, factor))
        source, other_side = (cs, xs) if backward else (xs, cs)
        target = grads if backward else outs
        far_ref = far_c if backward else far_x
        edge = slice(0, 1) if backward else slice(ROWS - 1, ROWS)

        def turn(step, state):
            carry, moment_carry, s_skip, s_w, s_m = state
            if backward:
                step = steps - 1 - step
            at = pair_at(step)
            base = (step * PAIR).astype(jnp.float32)
            values = source[slot, at, :].astype(jnp.float32)
            if mode != "none":
                others = other_side[slot, at, :].astype(jnp.float32)
            if reach:
                far = far_ref[slot, at, :].astype(jnp.float32)
            made = [None, None]
            for half in (1, 0) if backward else (0, 1):
                part = slice(half * ROWS, (half + 1) * ROWS)
                fresh = values[part]
                if reach:
                    fresh = fresh - tail * far[part]
                if one:
                    local, local_moment = scan_both(fresh, -far_tail * far[part], hops)
                    moment = local_moment + lead * moment_carry + lead_moment * carry
                    moment_carry = (
                        leap * moment_carry
                        + wide * carry
                        + jnp.broadcast_to(local_moment[edge], shape)
                    )
                else:
                    local = scan(fresh, hops)
                truncated = local + lead * carry
                carry = leap * carry + jnp.broadcast_to(local[edge], shape)
                made[half] = skip * values[part] + residue * truncated
                if mode != "none":
                    w = others[part] * truncated
                    s_w = s_w + w
                if one:
                    s_m = s_m + others[part] * moment
                elif mode == "two":
                    s_m = s_m + (base + half * ROWS) * w
                if one or mode == "two" and not backward:
                    s_skip = s_skip + values[part] * others[part]
            target[slot, at, :] = jnp.concatenate(made, axis=0).astype(target.dtype)
            return carry, moment_carry, s_skip, s_w, s_m

        state = (
            zero + jnp.broadcast_to(start, shape),
            zero + jnp.broadcast_to(start_moment, shape),
            zero,
            zero,
            zero,
        )
        done = 0
        parts = parts_of(slot, backward) if reach else (PIECES,)
        for piece, part in enumerate(parts):
            if reach:
                pl.when(has_source(slot, backward))(
                    lambda: flow(slot, backward, piece).wait_recv()
                )
            span = (done * steps // PIECES, (done + part) * steps // PIECES)
            state = lax.fori_loop(*span, turn, state, unroll=UNROLL)
            done += part
        return state[2:]

    def close(slot, s_skip, s_w, moment):
        scale = -decay_ref[groups[slot]] * residue_ref[groups[slot]]
        sums[slot, 0:1, :] = jnp.sum(s_skip, axis=0, keepdims=True)
        sums[slot, 1:2, :] = jnp.sum(s_w, axis=0, keepdims=True)
        sums[slot, 2:3, :] = scale * jnp.sum(moment, axis=0, keepdims=True)

    def both_sides(slot):
        s_skip, s_w, s_tw = run(slot, False, "two")
        _, s_v, s_tv = run(slot, True, "two")
        offset = depth + (me * rows).astype(jnp.float32)
        close(slot, s_skip, s_w, (s_tw - s_tv) + offset * (s_w - s_v))

    sums[...] = jnp.zeros_like(sums)
    both_sides(count - 1)
    close(0, *run(0, False, "one"))
    for slot in middle:
        both_sides(slot)
    close(1, *run(1, True, "one"))
    for step in range(count - 1):
        share_copy(step).start()
    send((0,), True, lambda slot, many: range(many - kept_back(slot, True), many))
    send((1,), False, lambda slot, many: range(many - kept_back(slot, False), many))

    @pl.when(has_source(0, True))
    def _():
        run(1, False, "none")
        run(0, True, "none")

    @pl.when(jnp.logical_not(has_source(0, True)))
    def _():
        run(0, True, "none")
        run(1, False, "none")

    for step in range(count - 1):
        share_copy(step).wait()
    for slot in range(count):
        total = sums[slot]
        for step in range(count - 1):
            total = total + got[step, slot]
        totals[slot] = total
    own_ref[...] = totals[bands[me]]
    for backward in (False, True):
        each_piece(
            range(count - 1),
            backward,
            lambda slot, many: range(many),
            lambda copy: copy.wait_send(),
        )


def place_kernel(
    bands, outs, grads, own, out_hbm, grad_hbm, skip_hbm, residue_hbm, decay_hbm, sems, own_sems
):
    count, _, width = outs.shape
    copies = []
    for group in range(count):
        slot = bands[group]
        lanes = pl.ds(group * width, width)
        for side, (source, target) in enumerate(((outs, out_hbm), (grads, grad_hbm))):
            copies.append(
                pltpu.make_async_copy(
                    source.at[slot], target.at[:, lanes], sems.at[side, group]
                )
            )
    for row, target in enumerate((skip_hbm, residue_hbm, decay_hbm)):
        copies.append(
            pltpu.make_async_copy(own.at[pl.ds(row, 1)], target, own_sems.at[row])
        )
    for copy in copies:
        copy.start()
    for copy in copies:
        copy.wait()


def place(bands, outs, grads, own):
    count, rows, width = outs.shape
    inside = pl.BlockSpec(memory_space=pltpu.VMEM)
    anywhere = pl.BlockSpec(memory_space=pl.ANY)
    whole = jax.ShapeDtypeStruct((rows, count * width), outs.dtype)
    small = jax.ShapeDtypeStruct((1, width), own.dtype)
    return pl.pallas_call(
        place_kernel,
        in_specs=[pl.BlockSpec(memory_space=pltpu.SMEM), inside, inside, inside],
        out_specs=[anywhere] * 5,
        out_shape=(whole, whole, small, small, small),
        scratch_shapes=[
            pltpu.SemaphoreType.DMA((2, count)),
            pltpu.SemaphoreType.DMA((3,)),
        ],
        compiler_params=pltpu.CompilerParams(vmem_limit_bytes=SCOPED),
        name="place",
    )(bands, outs, grads, own)


def banded(count, inputs, cotangent, residue, decay, skip_gain, band_blocks):
    rows, channels = inputs.shape
    width = channels // count
    first = rows * 2 // PIECES
    bands = band_blocks[0]
    anywhere = pl.BlockSpec(memory_space=pl.ANY)
    inside = pl.BlockSpec(memory_space=pltpu.VMEM)
    x_flows = pltpu.SemaphoreType.DMA((flow_count(count, False),))
    c_flows = pltpu.SemaphoreType.DMA((flow_count(count, True),))
    few = pltpu.SemaphoreType.DMA((count - 1,))
    kind = inputs.dtype
    packed = pltpu.VMEM((count, rows, width), kind)
    far = pltpu.VMEM((count - 1, rows, width), kind)
    row = pltpu.VMEM((count, 1, width), jnp.float32)
    four = ROWS // 2
    outs, grads, own = pl.pallas_call(
        functools.partial(banded_kernel, count),
        in_specs=[anywhere] * 6,
        out_specs=[inside, inside, inside],
        out_shape=(
            jax.ShapeDtypeStruct((count, rows, width), kind),
            jax.ShapeDtypeStruct((count, rows, width), kind),
            jax.ShapeDtypeStruct((four, width), jnp.float32),
        ),
        scratch_shapes=[
            pltpu.SMEM((count,), jnp.int32),
            row,
            row,
            row,
            pltpu.VMEM((count, first, width), kind),
            pltpu.VMEM((count, rows - first, width), kind),
            pltpu.VMEM((count, first, width), kind),
            pltpu.VMEM((count, rows - first, width), kind),
            packed,
            packed,
            far,
            far,
            pltpu.VMEM((count, four, width), jnp.float32),
            pltpu.VMEM((count, count, four, width), jnp.float32),
            pltpu.VMEM((count, four, width), jnp.float32),
            pltpu.VMEM((count - 1, count, four, width), jnp.float32),
            pltpu.VMEM((count, four, width), jnp.float32),
            pltpu.VMEM((ROWS, width), jnp.float32),
            pltpu.SemaphoreType.DMA((4,)),
            pltpu.SemaphoreType.DMA((4, count)),
            x_flows,
            x_flows,
            c_flows,
            c_flows,
            few,
            few,
            few,
            few,
        ],
        compiler_params=pltpu.CompilerParams(
            collective_id=0, has_side_effects=True, vmem_limit_bytes=SCOPED
        ),
        name="banded",
    )(
        bands,
        inputs,
        cotangent,
        *(part.reshape(count, 1, width) for part in (residue, decay, skip_gain)),
    )
    layer_out, input_grad, *sums = place(bands, outs, grads, own)
    return (layer_out, input_grad, *(part.reshape(width) for part in sums))


def local_body(count, inputs, cotangent, residue, decay, skip_gain, band_blocks):
    rows, channels = inputs.shape
    groups = band_blocks.shape[1]
    fits = groups == count and count > 2 and rows % (PAIR * PIECES * UNROLL) == 0
    if fits and channels % (groups * LANES) == 0:
        return banded(count, inputs, cotangent, residue, decay, skip_gain, band_blocks)
    return body(inputs, cotangent, residue, decay, skip_gain, band_blocks)


def solution(mesh):
    placed = (P("ctx", "dp"), P("ctx", "dp"), P("dp"), P("dp"), P("dp"), P("dp", None))
    return jax.shard_map(
        functools.partial(local_body, mesh.shape["ctx"]),
        mesh=mesh,
        in_specs=placed,
        out_specs=(
            P("ctx", "dp"),
            P("ctx", "dp"),
            P(("dp", "ctx")),
            P(("dp", "ctx")),
            P(("dp", "ctx")),
        ),
        check_vma=False,
    )
```

```python
import functools
import jax
import jax.numpy as jnp
from jax import lax
from jax.experimental import pallas as pl
from jax.experimental.pallas import tpu as pltpu
from jax.sharding import PartitionSpec as P


def prefix(value, axis, join, neutral, backward):
    count, mine = (lax.axis_size(axis), lax.axis_index(axis))
    pieces = jax.tree.map(lambda part: lax.all_gather(part, axis), value)
    if backward:
        pieces = jax.tree.map(lambda part: part[::-1], pieces)
        mine = count - 1 - mine
    total = jax.tree.map(
        lambda part, zero: jnp.full_like(part, 0) + jnp.asarray(zero, part.dtype), value, neutral
    )

    def turn(position, total):
        longer = join(total, jax.tree.map(lambda part: part[position], pieces))
        return jax.tree.map(lambda new, old: jnp.where(position < mine, new, old), longer, total)

    return lax.fori_loop(0, count - 1, turn, total)


def compose(earlier_pair, later_pair):
    return (earlier_pair[0] * later_pair[0], earlier_pair[1] * later_pair[0] + later_pair[1])


def chain_step(earlier_pair, later_pair):
    return (earlier_pair[0] * later_pair[1] + later_pair[0], earlier_pair[1] * later_pair[1])


def local_scan(values, decay_rate, backward):
    factors = jnp.broadcast_to(jnp.exp(-decay_rate)[None, :], values.shape)
    return lax.associative_scan(compose, (factors, values), reverse=backward)[1]


def slot_groups(bands, ctx_rank, direction):
    group_count = bands.shape[0]
    slot_index = jnp.arange(group_count, dtype=jnp.int32)
    distance = (slot_index - ctx_rank) * direction
    matches = bands[None, :] + 1 == distance[:, None]
    return jnp.sum(jnp.where(matches, slot_index[None, :], 0), axis=1)


def pick(shaped, order):
    blocks = [
        lax.dynamic_index_in_dim(shaped, order[at], 1, keepdims=True)
        for at in range(order.shape[0])
    ]
    return jnp.concatenate(blocks, axis=1)


def outgoing(values, slot_group, group_count, group_width):
    shaped = values.reshape(values.shape[0], group_count, group_width)
    return pick(shaped, slot_group)


def incoming(received, source, in_range):
    picked = pick(received, source)
    picked = jnp.where(in_range[None, :, None], picked, jnp.zeros((), picked.dtype))
    return picked.reshape(picked.shape[0], -1)


def body(inputs, cotangent, residue, decay, skip_gain, band_blocks):
    values = inputs.astype(jnp.float32)
    upstream = cotangent.astype(jnp.float32)
    bands = band_blocks[0]
    block_rows, channels = values.shape
    group_count = bands.shape[0]
    group_width = channels // group_count
    ctx_rank = lax.axis_index("ctx")
    offsets = jnp.arange(block_rows, dtype=jnp.float32)[:, None]
    lengths = jnp.repeat(
        (bands + 1) * block_rows, group_width, total_repeat_length=channels
    ).astype(jnp.float32)
    band_tail = jnp.exp(-decay * lengths)[None, :]
    block_decay = jnp.exp(-decay * block_rows)
    lead_decay = jnp.exp(-decay[None, :] * (offsets + 1.0))
    trail_decay = jnp.exp(-decay[None, :] * (block_rows - offsets))
    zero_state = jnp.zeros_like(decay)
    unit_state = jnp.ones_like(decay)
    inside = local_scan(values, decay, False)
    before, _ = prefix(
        (inside[-1], block_decay), "ctx", chain_step, (zero_state, unit_state), False
    )
    carried = inside + lead_decay * before[None, :]
    send_fwd = slot_groups(bands, ctx_rank, 1)
    source_fwd = ctx_rank - bands - 1
    valid_fwd = source_fwd >= 0
    source_fwd = jnp.clip(source_fwd, 0, group_count - 1)
    inside_back = local_scan(upstream, decay, True)
    after, _ = prefix(
        (inside_back[0], block_decay), "ctx", chain_step, (zero_state, unit_state), True
    )
    back_carried = inside_back + trail_decay * after[None, :]
    send_bwd = slot_groups(bands, ctx_rank, -1)
    source_bwd = ctx_rank + bands + 1
    valid_bwd = source_bwd < group_count
    source_bwd = jnp.clip(source_bwd, 0, group_count - 1)
    received = lax.all_to_all(
        outgoing(carried, send_fwd, group_count, group_width),
        "ctx",
        split_axis=1,
        concat_axis=1,
        tiled=True,
    )
    far_state = incoming(received, source_fwd, valid_fwd)
    received_back = lax.all_to_all(
        outgoing(back_carried, send_bwd, group_count, group_width),
        "ctx",
        split_axis=1,
        concat_axis=1,
        tiled=True,
    )
    near_state = incoming(received_back, source_bwd, valid_bwd)
    truncated = carried - band_tail * far_state
    layer_out = (skip_gain[None, :] * values + residue[None, :] * truncated).astype(jnp.bfloat16)
    back_truncated = back_carried - band_tail * near_state
    input_grad = (skip_gain[None, :] * upstream + residue[None, :] * back_truncated).astype(
        jnp.bfloat16
    )
    position = ctx_rank.astype(jnp.float32) * block_rows + offsets
    weighted = upstream * truncated
    moment = jnp.sum(position * weighted, axis=0) - jnp.sum(
        position * values * back_truncated, axis=0
    )
    grad_terms = jnp.stack(
        [jnp.sum(values * upstream, axis=0), jnp.sum(weighted, axis=0), -decay * residue * moment]
    )
    share_width = channels // lax.axis_size("ctx")
    summed = lax.psum(grad_terms, "ctx")
    own_share = lax.dynamic_slice_in_dim(summed, ctx_rank * share_width, share_width, 1)
    return (layer_out, input_grad, own_share[0], own_share[1], own_share[2])


MESH = pl.DeviceIdType.MESH
LANES = 128
ROWS = 8
PAIR = 2 * ROWS
PIECES = 8
UNROLL = 4
SCOPED = 48_000_000


def greet(count, me):
    barrier = pltpu.get_barrier_semaphore()
    for step in range(1, count):
        pl.semaphore_signal(
            barrier,
            inc=1,
            device_id={"ctx": lax.rem(me + step, count)},
            device_id_type=MESH,
        )
    return lambda: pl.semaphore_wait(barrier, count - 1)


def parts_of(slot, backward):
    if backward:
        return {0: (2, 4, 1, 1), 1: (2, 6)}.get(slot, (8,))
    return {1: (4, 2, 2)}.get(slot, (2, 6))


def kept_back(slot, backward):
    if backward:
        return 2 if slot == 0 else 0
    return 1 if slot == 1 else 0


def piece_rows(rows, slot, backward, piece):
    parts = parts_of(slot, backward)
    size = rows * parts[piece] // PIECES
    start = rows * sum(parts[:piece]) // PIECES
    return (rows - start - size if backward else start, size)


def piece_at(slot, backward, piece):
    return sum(len(parts_of(before, backward)) for before in range(slot)) + piece


def flow_count(count, backward):
    return sum(len(parts_of(slot, backward)) for slot in range(count - 1))


def pair_at(step):
    return pl.ds(pl.multiple_of(step * PAIR, PAIR), PAIR)


def banded_kernel(
    count,
    bands_hbm,
    x_hbm,
    c_hbm,
    residue_hbm,
    decay_hbm,
    skip_hbm,
    outs,
    grads,
    own_ref,
    bands,
    residue_ref,
    decay_ref,
    skip_ref,
    x_first,
    x_rest,
    c_first,
    c_rest,
    xs,
    cs,
    far_x,
    far_c,
    ends,
    far_ends,
    sums,
    got,
    totals,
    blank,
    small_sem,
    load_sem,
    x_send,
    x_recv,
    c_send,
    c_recv,
    e_send,
    e_recv,
    s_send,
    s_recv,
):
    me = lax.axis_index("ctx")
    _, rows, width = xs.shape
    shape = (ROWS, width)
    first = x_first.shape[1]

    all_here = greet(count, me)

    small = [
        pltpu.make_async_copy(source, target, small_sem.at[at])
        for at, (source, target) in enumerate(
            (
                (bands_hbm, bands),
                (decay_hbm, decay_ref),
                (residue_hbm, residue_ref),
                (skip_hbm, skip_ref),
            )
        )
    ]
    small[0].start()
    chunks = (
        (c_hbm, rows - first, c_first, cs),
        (x_hbm, 0, x_first, xs),
        (c_hbm, 0, c_rest, cs),
        (x_hbm, first, x_rest, xs),
    )

    def load(chunk, group):
        source, start, target, _ = chunks[chunk]
        lanes = pl.ds(group * width, width)
        return pltpu.make_async_copy(
            source.at[pl.ds(start, target.shape[1]), lanes],
            target.at[group],
            load_sem.at[chunk, group],
        )

    for chunk in range(len(chunks)):
        for group in range(count):
            load(chunk, group).start()
    for copy in small[1:]:
        copy.start()
    small[0].wait()
    groups = []
    for slot in range(count):
        group = jnp.int32(0)
        for other in range(count):
            group = jnp.where(bands[other] == slot, other, group)
        groups.append(group)

    def pack(chunk):
        _, start, whole, packed = chunks[chunk]
        for group in range(count):
            load(chunk, group).wait()

        def turn(step, _):
            to = pl.ds(pl.multiple_of(start + step * PAIR, PAIR), PAIR)
            for slot in range(count):
                packed[slot, to, :] = whole[groups[slot], pair_at(step), :]
            return 0

        lax.fori_loop(0, whole.shape[1] // PAIR, turn, 0, unroll=UNROLL)

    def has_source(slot, backward):
        return me + slot + 1 < count if backward else me >= slot + 1

    def flow(slot, backward, piece):
        start, size = piece_rows(rows, slot, backward, piece)
        at = pl.ds(start, size)
        sem = piece_at(slot, backward, piece)
        source, target, sends, recvs = (
            (cs, far_c, c_send, c_recv) if backward else (xs, far_x, x_send, x_recv)
        )
        to = me + count - slot - 1 if backward else me + slot + 1
        return pltpu.make_async_remote_copy(
            src_ref=source.at[slot, at],
            dst_ref=target.at[slot, at],
            send_sem=sends.at[sem],
            recv_sem=recvs.at[sem],
            device_id={"ctx": lax.rem(to, count)},
            device_id_type=MESH,
        )

    def each_piece(slots, backward, pick, act):
        for slot in slots:
            sends_it = has_source(slot, not backward)
            for piece in pick(slot, len(parts_of(slot, backward))):
                pl.when(sends_it)(lambda: act(flow(slot, backward, piece)))

    def send(slots, backward, pick):
        each_piece(slots, backward, pick, lambda copy: copy.start())

    def small_copy(source, target, sends, recvs, step):
        return pltpu.make_async_remote_copy(
            src_ref=source,
            dst_ref=target,
            send_sem=sends.at[step],
            recv_sem=recvs.at[step],
            device_id={"ctx": lax.rem(me + step + 1, count)},
            device_id_type=MESH,
        )

    def end_copy(step):
        return small_copy(ends, far_ends.at[me], e_send, e_recv, step)

    def share_copy(step):
        return small_copy(sums, got.at[step], s_send, s_recv, step)

    middle = tuple(range(2, count - 1))
    up_order = middle[::-1] + (0, 1)
    down_order = (1,) + middle + (0,)
    pack(0)
    all_here()
    send((1, 0), True, lambda slot, many: (0,))
    pack(1)
    send(middle[::-1] + (0,), False, lambda slot, many: (0,))
    pack(2)
    pack(3)
    for copy in small[1:]:
        copy.wait()

    level = lax.broadcasted_iota(jnp.int32, shape, 0)
    depth = level.astype(jnp.float32)
    blank[...] = jnp.zeros(shape, jnp.float32)
    zero = blank[...]
    steps = rows // PAIR
    ends[...] = jnp.zeros_like(ends)
    for slot in range(count):
        rate = decay_ref[groups[slot]]
        leap_pair = jnp.broadcast_to(jnp.exp(-rate * PAIR), shape)
        wide_pair = leap_pair * float(PAIR)
        weighted = {0: (0, 1), 1: (2, 3)}.get(slot, ())

        def turn(step, state):
            held, moments = state
            ahead = xs[slot, pair_at(step), :].astype(jnp.float32)
            back = cs[slot, pair_at(steps - 1 - step), :].astype(jnp.float32)
            parts = (ahead[:ROWS], ahead[ROWS:], back[:ROWS], back[ROWS:])
            moments = tuple(
                moment * leap_pair + held[at] * wide_pair
                for moment, at in zip(moments, weighted)
            )
            return (
                tuple(old * leap_pair + new for old, new in zip(held, parts)),
                moments,
            )

        held, moments = lax.fori_loop(
            0, steps, turn, ((zero,) * 4, (zero,) * len(weighted)), unroll=UNROLL
        )
        apart = (PAIR - 1 - depth, ROWS - 1 - depth, depth, ROWS + depth)
        factors = [jnp.exp(-rate * far) for far in apart]
        scaled = [one * factor for one, factor in zip(held, factors)]
        ends[slot, 0:1, :] = jnp.sum(scaled[0] + scaled[1], axis=0, keepdims=True)
        ends[slot, 1:2, :] = jnp.sum(scaled[2] + scaled[3], axis=0, keepdims=True)
        if weighted:
            both = zero
            for moment, at in zip(moments, weighted):
                both = both + factors[at] * moment + apart[at] * scaled[at]
            ends[slot, 2:3, :] = jnp.sum(both, axis=0, keepdims=True)
    for step in range(count - 1):
        end_copy(step).start()

    def later(slot, backward):
        many = len(parts_of(slot, backward))
        begun = backward and slot < 2 or not backward and slot != 1
        return (1 if begun else 0, many - kept_back(slot, backward))

    send(down_order, True, lambda slot, many: range(*later(slot, True)))
    send(up_order, False, lambda slot, many: range(*later(slot, False)))

    for slot in range(count - 1):
        for backward, far in ((False, far_x), (True, far_c)):

            @pl.when(jnp.logical_not(has_source(slot, backward)))
            def _():
                def clear(step, _):
                    far[slot, pair_at(step), :] = jnp.zeros((PAIR, width), far.dtype)
                    return 0

                lax.fori_loop(0, steps, clear, 0, unroll=UNROLL)

    for step in range(count - 1):
        end_copy(step).wait()

    def scan(tile, hops):
        for hop, turn, factor in hops:
            tile = tile + factor * pltpu.roll(tile, turn, 0)
        return tile

    def scan_both(tile, moment, hops):
        for hop, turn, factor in hops:
            moved = pltpu.roll(tile, turn, 0)
            moment = moment + factor * (pltpu.roll(moment, turn, 0) + float(hop) * moved)
            tile = tile + factor * moved
        return tile, moment

    def run(slot, backward, mode):
        band = slot + 1
        reach = slot < count - 1
        one = mode == "one"
        rate = decay_ref[groups[slot]]
        start = jnp.zeros((1, width), jnp.float32)
        start_moment = start
        row = int(backward)
        for other in range(count):
            apart = other - me - 1 if backward else me - 1 - other
            kept = jnp.logical_and(apart >= 0, apart < band)
            span = (jnp.maximum(apart, 0) * rows).astype(jnp.float32)
            factor = jnp.exp(-rate * span)
            end = far_ends[other, slot, row : row + 1, :]
            start = start + jnp.where(kept, factor * end, 0.0)
            if one:
                moment = far_ends[other, slot, 2:3, :] + span * end
                start_moment = start_moment + jnp.where(kept, factor * moment, 0.0)
        tail_row = jnp.exp(-rate * float(band * rows))
        tail = jnp.broadcast_to(tail_row, shape)
        far_tail = jnp.broadcast_to(tail_row * float(band * rows), shape)
        leap = jnp.broadcast_to(jnp.exp(-rate * ROWS), shape)
        wide = leap * float(ROWS)
        residue = jnp.broadcast_to(residue_ref[groups[slot]], shape)
        skip = jnp.broadcast_to(skip_ref[groups[slot]], shape)
        ahead = ROWS - depth if backward else depth + 1.0
        lead = jnp.exp(-rate * ahead)
        lead_moment = lead * ahead
        hops = []
        for hop in (1, 2, 4):
            inside = level < ROWS - hop if backward else level >= hop
            factor = jnp.where(inside, jnp.exp(-rate * hop), 0.0)
            hops.append((hop, ROWS - hop if backward else hop, factor))
        source, other_side = (cs, xs) if backward else (xs, cs)
        target = grads if backward else outs
        far_ref = far_c if backward else far_x
        edge = slice(0, 1) if backward else slice(ROWS - 1, ROWS)

        def turn(step, state):
            carry, moment_carry, s_skip, s_w, s_m = state
            if backward:
                step = steps - 1 - step
            at = pair_at(step)
            base = (step * PAIR).astype(jnp.float32)
            values = source[slot, at, :].astype(jnp.float32)
            if mode != "none":
                others = other_side[slot, at, :].astype(jnp.float32)
            if reach:
                far = far_ref[slot, at, :].astype(jnp.float32)
            made = [None, None]
            for half in (1, 0) if backward else (0, 1):
                part = slice(half * ROWS, (half + 1) * ROWS)
                fresh = values[part]
                if reach:
                    fresh = fresh - tail * far[part]
                if one:
                    local, local_moment = scan_both(fresh, -far_tail * far[part], hops)
                    moment = local_moment + lead * moment_carry + lead_moment * carry
                    moment_carry = (
                        leap * moment_carry
                        + wide * carry
                        + jnp.broadcast_to(local_moment[edge], shape)
                    )
                else:
                    local = scan(fresh, hops)
                truncated = local + lead * carry
                carry = leap * carry + jnp.broadcast_to(local[edge], shape)
                made[half] = skip * values[part] + residue * truncated
                if mode != "none":
                    w = others[part] * truncated
                    s_w = s_w + w
                if one:
                    s_m = s_m + others[part] * moment
                elif mode == "two":
                    s_m = s_m + (base + half * ROWS) * w
                if one or mode == "two" and not backward:
                    s_skip = s_skip + values[part] * others[part]
            target[slot, at, :] = jnp.concatenate(made, axis=0).astype(target.dtype)
            return carry, moment_carry, s_skip, s_w, s_m

        state = (
            zero + jnp.broadcast_to(start, shape),
            zero + jnp.broadcast_to(start_moment, shape),
            zero,
            zero,
            zero,
        )
        done = 0
        parts = parts_of(slot, backward) if reach else (PIECES,)
        for piece, part in enumerate(parts):
            if reach:
                pl.when(has_source(slot, backward))(
                    lambda: flow(slot, backward, piece).wait_recv()
                )
            span = (done * steps // PIECES, (done + part) * steps // PIECES)
            state = lax.fori_loop(*span, turn, state, unroll=UNROLL)
            done += part
        return state[2:]

    def close(slot, s_skip, s_w, moment):
        scale = -decay_ref[groups[slot]] * residue_ref[groups[slot]]
        sums[slot, 0:1, :] = jnp.sum(s_skip, axis=0, keepdims=True)
        sums[slot, 1:2, :] = jnp.sum(s_w, axis=0, keepdims=True)
        sums[slot, 2:3, :] = scale * jnp.sum(moment, axis=0, keepdims=True)

    def both_sides(slot):
        s_skip, s_w, s_tw = run(slot, False, "two")
        _, s_v, s_tv = run(slot, True, "two")
        offset = depth + (me * rows).astype(jnp.float32)
        close(slot, s_skip, s_w, (s_tw - s_tv) + offset * (s_w - s_v))

    sums[...] = jnp.zeros_like(sums)
    both_sides(count - 1)
    close(0, *run(0, False, "one"))
    for slot in middle:
        both_sides(slot)
    close(1, *run(1, True, "one"))
    for step in range(count - 1):
        share_copy(step).start()
    send((0,), True, lambda slot, many: range(many - kept_back(slot, True), many))
    send((1,), False, lambda slot, many: range(many - kept_back(slot, False), many))

    @pl.when(has_source(0, True))
    def _():
        run(1, False, "none")
        run(0, True, "none")

    @pl.when(jnp.logical_not(has_source(0, True)))
    def _():
        run(0, True, "none")
        run(1, False, "none")

    for step in range(count - 1):
        share_copy(step).wait()
    for slot in range(count):
        total = sums[slot]
        for step in range(count - 1):
            total = total + got[step, slot]
        totals[slot] = total
    own_ref[...] = totals[bands[me]]
    for backward in (False, True):
        each_piece(
            range(count - 1),
            backward,
            lambda slot, many: range(many),
            lambda copy: copy.wait_send(),
        )


def place_kernel(
    bands, outs, grads, own, out_hbm, grad_hbm, skip_hbm, residue_hbm, decay_hbm, sems, own_sems
):
    count, _, width = outs.shape
    copies = []
    for group in range(count):
        slot = bands[group]
        lanes = pl.ds(group * width, width)
        for side, (source, target) in enumerate(((outs, out_hbm), (grads, grad_hbm))):
            copies.append(
                pltpu.make_async_copy(
                    source.at[slot], target.at[:, lanes], sems.at[side, group]
                )
            )
    for row, target in enumerate((skip_hbm, residue_hbm, decay_hbm)):
        copies.append(
            pltpu.make_async_copy(own.at[pl.ds(row, 1)], target, own_sems.at[row])
        )
    for copy in copies:
        copy.start()
    for copy in copies:
        copy.wait()


def in_hbm(*arrays):
    return [pltpu.with_memory_space_constraint(one, pltpu.HBM) for one in arrays]


def place(bands, outs, grads, own):
    count, rows, width = outs.shape
    inside = pl.BlockSpec(memory_space=pltpu.VMEM)
    anywhere = pl.BlockSpec(memory_space=pl.ANY)
    whole = jax.ShapeDtypeStruct((rows, count * width), outs.dtype)
    small = jax.ShapeDtypeStruct((1, width), own.dtype)
    return pl.pallas_call(
        place_kernel,
        in_specs=[pl.BlockSpec(memory_space=pltpu.SMEM), inside, inside, inside],
        out_specs=[anywhere] * 5,
        out_shape=(whole, whole, small, small, small),
        scratch_shapes=[
            pltpu.SemaphoreType.DMA((2, count)),
            pltpu.SemaphoreType.DMA((3,)),
        ],
        compiler_params=pltpu.CompilerParams(vmem_limit_bytes=SCOPED),
        name="place",
    )(*in_hbm(bands), outs, grads, own)


def banded(count, inputs, cotangent, residue, decay, skip_gain, band_blocks):
    rows, channels = inputs.shape
    width = channels // count
    first = rows * 2 // PIECES
    bands = band_blocks[0]
    anywhere = pl.BlockSpec(memory_space=pl.ANY)
    inside = pl.BlockSpec(memory_space=pltpu.VMEM)
    x_flows = pltpu.SemaphoreType.DMA((flow_count(count, False),))
    c_flows = pltpu.SemaphoreType.DMA((flow_count(count, True),))
    few = pltpu.SemaphoreType.DMA((count - 1,))
    kind = inputs.dtype
    packed = pltpu.VMEM((count, rows, width), kind)
    far = pltpu.VMEM((count - 1, rows, width), kind)
    row = pltpu.VMEM((count, 1, width), jnp.float32)
    four = ROWS // 2
    outs, grads, own = pl.pallas_call(
        functools.partial(banded_kernel, count),
        in_specs=[anywhere] * 6,
        out_specs=[inside, inside, inside],
        out_shape=(
            pltpu.VMEM((count, rows, width), kind),
            pltpu.VMEM((count, rows, width), kind),
            pltpu.VMEM((four, width), jnp.float32),
        ),
        scratch_shapes=[
            pltpu.SMEM((count,), jnp.int32),
            row,
            row,
            row,
            pltpu.VMEM((count, first, width), kind),
            pltpu.VMEM((count, rows - first, width), kind),
            pltpu.VMEM((count, first, width), kind),
            pltpu.VMEM((count, rows - first, width), kind),
            packed,
            packed,
            far,
            far,
            pltpu.VMEM((count, four, width), jnp.float32),
            pltpu.VMEM((count, count, four, width), jnp.float32),
            pltpu.VMEM((count, four, width), jnp.float32),
            pltpu.VMEM((count - 1, count, four, width), jnp.float32),
            pltpu.VMEM((count, four, width), jnp.float32),
            pltpu.VMEM((ROWS, width), jnp.float32),
            pltpu.SemaphoreType.DMA((4,)),
            pltpu.SemaphoreType.DMA((4, count)),
            x_flows,
            x_flows,
            c_flows,
            c_flows,
            few,
            few,
            few,
            few,
        ],
        compiler_params=pltpu.CompilerParams(
            collective_id=0, has_side_effects=True, vmem_limit_bytes=SCOPED
        ),
        name="banded",
    )(
        *in_hbm(
            bands,
            inputs,
            cotangent,
            *(part.reshape(count, 1, width) for part in (residue, decay, skip_gain)),
        )
    )
    layer_out, input_grad, *sums = place(bands, outs, grads, own)
    return (layer_out, input_grad, *(part.reshape(width) for part in sums))


def local_body(count, inputs, cotangent, residue, decay, skip_gain, band_blocks):
    rows, channels = inputs.shape
    groups = band_blocks.shape[1]
    fits = groups == count and count > 2 and rows % (PAIR * PIECES * UNROLL) == 0
    if fits and channels % (groups * LANES) == 0:
        return banded(count, inputs, cotangent, residue, decay, skip_gain, band_blocks)
    return body(inputs, cotangent, residue, decay, skip_gain, band_blocks)


def solution(mesh):
    placed = (P("ctx", "dp"), P("ctx", "dp"), P("dp"), P("dp"), P("dp"), P("dp", None))
    return jax.shard_map(
        functools.partial(local_body, mesh.shape["ctx"]),
        mesh=mesh,
        in_specs=placed,
        out_specs=(
            P("ctx", "dp"),
            P("ctx", "dp"),
            P(("dp", "ctx")),
            P(("dp", "ctx")),
            P(("dp", "ctx")),
        ),
        check_vma=False,
    )
```

```python
import functools
import jax
import jax.numpy as jnp
from jax import lax
from jax.experimental import pallas as pl
from jax.experimental.pallas import tpu as pltpu
from jax.sharding import PartitionSpec as P


def prefix(value, axis, join, neutral, backward):
    count, mine = (lax.axis_size(axis), lax.axis_index(axis))
    pieces = jax.tree.map(lambda part: lax.all_gather(part, axis), value)
    if backward:
        pieces = jax.tree.map(lambda part: part[::-1], pieces)
        mine = count - 1 - mine
    total = jax.tree.map(
        lambda part, zero: jnp.full_like(part, 0) + jnp.asarray(zero, part.dtype), value, neutral
    )

    def turn(position, total):
        longer = join(total, jax.tree.map(lambda part: part[position], pieces))
        return jax.tree.map(lambda new, old: jnp.where(position < mine, new, old), longer, total)

    return lax.fori_loop(0, count - 1, turn, total)


def compose(earlier_pair, later_pair):
    return (earlier_pair[0] * later_pair[0], earlier_pair[1] * later_pair[0] + later_pair[1])


def chain_step(earlier_pair, later_pair):
    return (earlier_pair[0] * later_pair[1] + later_pair[0], earlier_pair[1] * later_pair[1])


def local_scan(values, decay_rate, backward):
    factors = jnp.broadcast_to(jnp.exp(-decay_rate)[None, :], values.shape)
    return lax.associative_scan(compose, (factors, values), reverse=backward)[1]


def slot_groups(bands, ctx_rank, direction):
    group_count = bands.shape[0]
    slot_index = jnp.arange(group_count, dtype=jnp.int32)
    distance = (slot_index - ctx_rank) * direction
    matches = bands[None, :] + 1 == distance[:, None]
    return jnp.sum(jnp.where(matches, slot_index[None, :], 0), axis=1)


def pick(shaped, order):
    blocks = [
        lax.dynamic_index_in_dim(shaped, order[at], 1, keepdims=True)
        for at in range(order.shape[0])
    ]
    return jnp.concatenate(blocks, axis=1)


def outgoing(values, slot_group, group_count, group_width):
    shaped = values.reshape(values.shape[0], group_count, group_width)
    return pick(shaped, slot_group)


def incoming(received, source, in_range):
    picked = pick(received, source)
    picked = jnp.where(in_range[None, :, None], picked, jnp.zeros((), picked.dtype))
    return picked.reshape(picked.shape[0], -1)


def body(inputs, cotangent, residue, decay, skip_gain, band_blocks):
    values = inputs.astype(jnp.float32)
    upstream = cotangent.astype(jnp.float32)
    bands = band_blocks[0]
    block_rows, channels = values.shape
    group_count = bands.shape[0]
    group_width = channels // group_count
    ctx_rank = lax.axis_index("ctx")
    offsets = jnp.arange(block_rows, dtype=jnp.float32)[:, None]
    lengths = jnp.repeat(
        (bands + 1) * block_rows, group_width, total_repeat_length=channels
    ).astype(jnp.float32)
    band_tail = jnp.exp(-decay * lengths)[None, :]
    block_decay = jnp.exp(-decay * block_rows)
    lead_decay = jnp.exp(-decay[None, :] * (offsets + 1.0))
    trail_decay = jnp.exp(-decay[None, :] * (block_rows - offsets))
    zero_state = jnp.zeros_like(decay)
    unit_state = jnp.ones_like(decay)
    inside = local_scan(values, decay, False)
    before, _ = prefix(
        (inside[-1], block_decay), "ctx", chain_step, (zero_state, unit_state), False
    )
    carried = inside + lead_decay * before[None, :]
    send_fwd = slot_groups(bands, ctx_rank, 1)
    source_fwd = ctx_rank - bands - 1
    valid_fwd = source_fwd >= 0
    source_fwd = jnp.clip(source_fwd, 0, group_count - 1)
    inside_back = local_scan(upstream, decay, True)
    after, _ = prefix(
        (inside_back[0], block_decay), "ctx", chain_step, (zero_state, unit_state), True
    )
    back_carried = inside_back + trail_decay * after[None, :]
    send_bwd = slot_groups(bands, ctx_rank, -1)
    source_bwd = ctx_rank + bands + 1
    valid_bwd = source_bwd < group_count
    source_bwd = jnp.clip(source_bwd, 0, group_count - 1)
    received = lax.all_to_all(
        outgoing(carried, send_fwd, group_count, group_width),
        "ctx",
        split_axis=1,
        concat_axis=1,
        tiled=True,
    )
    far_state = incoming(received, source_fwd, valid_fwd)
    received_back = lax.all_to_all(
        outgoing(back_carried, send_bwd, group_count, group_width),
        "ctx",
        split_axis=1,
        concat_axis=1,
        tiled=True,
    )
    near_state = incoming(received_back, source_bwd, valid_bwd)
    truncated = carried - band_tail * far_state
    layer_out = (skip_gain[None, :] * values + residue[None, :] * truncated).astype(jnp.bfloat16)
    back_truncated = back_carried - band_tail * near_state
    input_grad = (skip_gain[None, :] * upstream + residue[None, :] * back_truncated).astype(
        jnp.bfloat16
    )
    position = ctx_rank.astype(jnp.float32) * block_rows + offsets
    weighted = upstream * truncated
    moment = jnp.sum(position * weighted, axis=0) - jnp.sum(
        position * values * back_truncated, axis=0
    )
    grad_terms = jnp.stack(
        [jnp.sum(values * upstream, axis=0), jnp.sum(weighted, axis=0), -decay * residue * moment]
    )
    share_width = channels // lax.axis_size("ctx")
    summed = lax.psum(grad_terms, "ctx")
    own_share = lax.dynamic_slice_in_dim(summed, ctx_rank * share_width, share_width, 1)
    return (layer_out, input_grad, own_share[0], own_share[1], own_share[2])


MESH = pl.DeviceIdType.MESH
LANES = 128
ROWS = 8
PAIR = 2 * ROWS
PIECES = 8
UNROLL = 4
SCOPED = 48_000_000


def greet(count, me):
    barrier = pltpu.get_barrier_semaphore()
    for step in range(1, count):
        pl.semaphore_signal(
            barrier,
            inc=1,
            device_id={"ctx": lax.rem(me + step, count)},
            device_id_type=MESH,
        )
    return lambda: pl.semaphore_wait(barrier, count - 1)


def parts_of(slot, backward):
    if backward:
        return {0: (2, 4, 1, 1), 1: (2, 6)}.get(slot, (8,))
    return {1: (4, 2, 2)}.get(slot, (2, 6))


def kept_back(slot, backward):
    if backward:
        return 2 if slot == 0 else 0
    return 1 if slot == 1 else 0


def piece_rows(rows, slot, backward, piece):
    parts = parts_of(slot, backward)
    size = rows * parts[piece] // PIECES
    start = rows * sum(parts[:piece]) // PIECES
    return (rows - start - size if backward else start, size)


def piece_at(slot, backward, piece):
    return sum(len(parts_of(before, backward)) for before in range(slot)) + piece


def flow_count(count, backward):
    return sum(len(parts_of(slot, backward)) for slot in range(count - 1))


def end_row(slot, backward):
    return 0 if backward and slot == 0 else slot + 1


def pair_at(step):
    return pl.ds(pl.multiple_of(step * PAIR, PAIR), PAIR)


def banded_kernel(
    count,
    bands_hbm,
    x_hbm,
    c_hbm,
    residue_hbm,
    decay_hbm,
    skip_hbm,
    outs,
    grads,
    own_ref,
    bands,
    residue_ref,
    decay_ref,
    skip_ref,
    x_first,
    x_rest,
    c_first,
    c_rest,
    xs,
    cs,
    far_x,
    far_c,
    ends,
    far_ends,
    sums,
    shares,
    got,
    blank,
    small_sem,
    load_sem,
    x_send,
    x_recv,
    c_send,
    c_recv,
    e_send,
    e_recv,
    s_send,
    s_recv,
):
    me = lax.axis_index("ctx")
    _, rows, width = xs.shape
    shape = (ROWS, width)
    first = x_first.shape[1]

    all_here = greet(count, me)

    small = [
        pltpu.make_async_copy(source, target, small_sem.at[at])
        for at, (source, target) in enumerate(
            (
                (bands_hbm, bands),
                (decay_hbm, decay_ref),
                (residue_hbm, residue_ref),
                (skip_hbm, skip_ref),
            )
        )
    ]
    small[0].start()
    chunks = (
        (c_hbm, rows - first, c_first, cs),
        (x_hbm, 0, x_first, xs),
        (c_hbm, 0, c_rest, cs),
        (x_hbm, first, x_rest, xs),
    )

    def load(chunk, group):
        source, start, target, _ = chunks[chunk]
        lanes = pl.ds(group * width, width)
        return pltpu.make_async_copy(
            source.at[pl.ds(start, target.shape[1]), lanes],
            target.at[group],
            load_sem.at[chunk, group],
        )

    for chunk in range(len(chunks)):
        for group in range(count):
            load(chunk, group).start()
    for copy in small[1:]:
        copy.start()
    small[0].wait()
    groups = []
    for slot in range(count):
        group = jnp.int32(0)
        for other in range(count):
            group = jnp.where(bands[other] == slot, other, group)
        groups.append(group)

    def pack(chunk):
        _, start, whole, packed = chunks[chunk]
        for group in range(count):
            load(chunk, group).wait()

        def turn(step, _):
            to = pl.ds(pl.multiple_of(start + step * PAIR, PAIR), PAIR)
            for slot in range(count):
                packed[slot, to, :] = whole[groups[slot], pair_at(step), :]
            return 0

        lax.fori_loop(0, whole.shape[1] // PAIR, turn, 0, unroll=UNROLL)

    def has_source(slot, backward):
        return me + slot + 1 < count if backward else me >= slot + 1

    def flow(slot, backward, piece):
        start, size = piece_rows(rows, slot, backward, piece)
        at = pl.ds(start, size)
        sem = piece_at(slot, backward, piece)
        source, target, sends, recvs = (
            (cs, far_c, c_send, c_recv) if backward else (xs, far_x, x_send, x_recv)
        )
        to = me + count - slot - 1 if backward else me + slot + 1
        return pltpu.make_async_remote_copy(
            src_ref=source.at[slot, at],
            dst_ref=target.at[slot, at],
            send_sem=sends.at[sem],
            recv_sem=recvs.at[sem],
            device_id={"ctx": lax.rem(to, count)},
            device_id_type=MESH,
        )

    def each_piece(slots, backward, pick, act):
        for slot in slots:
            sends_it = has_source(slot, not backward)
            for piece in pick(slot, len(parts_of(slot, backward))):
                pl.when(sends_it)(lambda: act(flow(slot, backward, piece)))

    def send(slots, backward, pick):
        each_piece(slots, backward, pick, lambda copy: copy.start())

    def end_copy(far, backward):
        first_row = end_row(far - 1, backward)
        if far == 1 or far == 2 and backward:
            first_row = far - 1
        at = pl.ds(first_row, count + 1 - first_row)
        side = int(backward)
        to = me + count - far if backward else me + far
        return pltpu.make_async_remote_copy(
            src_ref=ends.at[side, at],
            dst_ref=far_ends.at[side, far - 1, at],
            send_sem=e_send.at[side, far - 1],
            recv_sem=e_recv.at[side, far - 1],
            device_id={"ctx": lax.rem(to, count)},
            device_id_type=MESH,
        )

    def each_end(act_send, act_receive):
        for far in range(1, count):
            for backward in (False, True):
                if act_send is not None:
                    pl.when(has_source(far - 1, not backward))(
                        lambda: act_send(end_copy(far, backward))
                    )
                if act_receive is not None:
                    pl.when(has_source(far - 1, backward))(
                        lambda: act_receive(end_copy(far, backward))
                    )

    def share_copy(step):
        to = lax.rem(me + step + 1, count)
        return pltpu.make_async_remote_copy(
            src_ref=shares.at[step],
            dst_ref=got.at[step],
            send_sem=s_send.at[step],
            recv_sem=s_recv.at[step],
            device_id={"ctx": to},
            device_id_type=MESH,
        )

    middle = tuple(range(2, count - 1))
    up_order = middle[::-1] + (0, 1)
    down_order = (1,) + middle + (0,)
    pack(0)
    all_here()
    send((1, 0), True, lambda slot, many: (0,))
    pack(1)
    send(middle[::-1] + (0,), False, lambda slot, many: (0,))
    pack(2)
    pack(3)
    for copy in small[1:]:
        copy.wait()

    level = lax.broadcasted_iota(jnp.int32, shape, 0)
    depth = level.astype(jnp.float32)
    blank[...] = jnp.zeros(shape, jnp.float32)
    zero = blank[...]
    steps = rows // PAIR
    for slot in range(count):
        rate = decay_ref[groups[slot]]
        leap_pair = jnp.broadcast_to(jnp.exp(-rate * PAIR), shape)
        wide_pair = leap_pair * float(PAIR)
        weighted = {0: (0, 1), 1: (2, 3)}.get(slot, ())

        def turn(step, state):
            held, moments = state
            ahead = xs[slot, pair_at(step), :].astype(jnp.float32)
            back = cs[slot, pair_at(steps - 1 - step), :].astype(jnp.float32)
            parts = (ahead[:ROWS], ahead[ROWS:], back[:ROWS], back[ROWS:])
            moments = tuple(
                moment * leap_pair + held[at] * wide_pair
                for moment, at in zip(moments, weighted)
            )
            return (
                tuple(old * leap_pair + new for old, new in zip(held, parts)),
                moments,
            )

        held, moments = lax.fori_loop(
            0, steps, turn, ((zero,) * 4, (zero,) * len(weighted)), unroll=UNROLL
        )
        apart = (PAIR - 1 - depth, ROWS - 1 - depth, depth, ROWS + depth)
        factors = [jnp.exp(-rate * far) for far in apart]
        scaled = [one * factor for one, factor in zip(held, factors)]
        for side in range(2):
            both = scaled[2 * side] + scaled[2 * side + 1]
            ends[side, end_row(slot, side)] = jnp.sum(both, axis=0, keepdims=True)
        if weighted:
            both = zero
            for moment, at in zip(moments, weighted):
                both = both + factors[at] * moment + apart[at] * scaled[at]
            ends[slot, slot] = jnp.sum(both, axis=0, keepdims=True)
    each_end(lambda copy: copy.start(), None)

    def later(slot, backward):
        many = len(parts_of(slot, backward))
        begun = backward and slot < 2 or not backward and slot != 1
        return (1 if begun else 0, many - kept_back(slot, backward))

    send(down_order, True, lambda slot, many: range(*later(slot, True)))
    send(up_order, False, lambda slot, many: range(*later(slot, False)))

    for slot in range(count - 1):
        for backward, far in ((False, far_x), (True, far_c)):

            @pl.when(jnp.logical_not(has_source(slot, backward)))
            def _():
                def clear(step, _):
                    far[slot, pair_at(step), :] = jnp.zeros((PAIR, width), far.dtype)
                    return 0

                lax.fori_loop(0, steps, clear, 0, unroll=UNROLL)

    each_end(lambda copy: copy.wait_send(), lambda copy: copy.wait_recv())

    def scan(tile, hops):
        for hop, turn, factor in hops:
            tile = tile + factor * pltpu.roll(tile, turn, 0)
        return tile

    def scan_both(tile, moment, hops):
        for hop, turn, factor in hops:
            moved = pltpu.roll(tile, turn, 0)
            moment = moment + factor * (pltpu.roll(moment, turn, 0) + float(hop) * moved)
            tile = tile + factor * moved
        return tile, moment

    def run(slot, backward, mode):
        band = slot + 1
        reach = slot < count - 1
        one = mode == "one"
        rate = decay_ref[groups[slot]]
        start = jnp.zeros((1, width), jnp.float32)
        start_moment = start
        side = int(backward)
        for apart in range(min(band, count - 1)):
            kept = has_source(apart, backward)
            span = float(apart * rows)
            factor = jnp.exp(-rate * span)
            end = far_ends[side, apart, end_row(slot, backward)]
            start = start + jnp.where(kept, factor * end, 0.0)
            if one:
                moment = far_ends[side, apart, slot] + span * end
                start_moment = start_moment + jnp.where(kept, factor * moment, 0.0)
        tail_row = jnp.exp(-rate * float(band * rows))
        tail = jnp.broadcast_to(tail_row, shape)
        far_tail = jnp.broadcast_to(tail_row * float(band * rows), shape)
        leap = jnp.broadcast_to(jnp.exp(-rate * ROWS), shape)
        wide = leap * float(ROWS)
        residue = jnp.broadcast_to(residue_ref[groups[slot]], shape)
        skip = jnp.broadcast_to(skip_ref[groups[slot]], shape)
        ahead = ROWS - depth if backward else depth + 1.0
        lead = jnp.exp(-rate * ahead)
        lead_moment = lead * ahead
        hops = []
        for hop in (1, 2, 4):
            inside = level < ROWS - hop if backward else level >= hop
            factor = jnp.where(inside, jnp.exp(-rate * hop), 0.0)
            hops.append((hop, ROWS - hop if backward else hop, factor))
        source, other_side = (cs, xs) if backward else (xs, cs)
        target = grads if backward else outs
        far_ref = far_c if backward else far_x
        edge = slice(0, 1) if backward else slice(ROWS - 1, ROWS)

        def turn(step, state):
            carry, moment_carry, s_skip, s_w, s_m = state
            if backward:
                step = steps - 1 - step
            at = pair_at(step)
            base = (step * PAIR).astype(jnp.float32)
            values = source[slot, at, :].astype(jnp.float32)
            if mode != "none":
                others = other_side[slot, at, :].astype(jnp.float32)
            if reach:
                far = far_ref[slot, at, :].astype(jnp.float32)
            made = [None, None]
            for half in (1, 0) if backward else (0, 1):
                part = slice(half * ROWS, (half + 1) * ROWS)
                fresh = values[part]
                if reach:
                    fresh = fresh - tail * far[part]
                if one:
                    local, local_moment = scan_both(fresh, -far_tail * far[part], hops)
                    moment = local_moment + lead * moment_carry + lead_moment * carry
                    moment_carry = (
                        leap * moment_carry
                        + wide * carry
                        + jnp.broadcast_to(local_moment[edge], shape)
                    )
                else:
                    local = scan(fresh, hops)
                truncated = local + lead * carry
                carry = leap * carry + jnp.broadcast_to(local[edge], shape)
                made[half] = skip * values[part] + residue * truncated
                if mode != "none":
                    w = others[part] * truncated
                    s_w = s_w + w
                if one:
                    s_m = s_m + others[part] * moment
                elif mode == "two":
                    s_m = s_m + (base + half * ROWS) * w
                if one or mode == "two" and not backward:
                    s_skip = s_skip + values[part] * others[part]
            target[slot, at, :] = jnp.concatenate(made, axis=0).astype(target.dtype)
            return carry, moment_carry, s_skip, s_w, s_m

        state = (
            zero + jnp.broadcast_to(start, shape),
            zero + jnp.broadcast_to(start_moment, shape),
            zero,
            zero,
            zero,
        )
        done = 0
        parts = parts_of(slot, backward) if reach else (PIECES,)
        for piece, part in enumerate(parts):
            if reach:
                pl.when(has_source(slot, backward))(
                    lambda: flow(slot, backward, piece).wait_recv()
                )
            span = (done * steps // PIECES, (done + part) * steps // PIECES)
            state = lax.fori_loop(*span, turn, state, unroll=UNROLL)
            done += part
        return state[2:]

    def close(slot, s_skip, s_w, moment):
        scale = -decay_ref[groups[slot]] * residue_ref[groups[slot]]
        sums[slot, 0] = jnp.sum(s_skip, axis=0, keepdims=True)
        sums[slot, 1] = jnp.sum(s_w, axis=0, keepdims=True)
        sums[slot, 2] = scale * jnp.sum(moment, axis=0, keepdims=True)

    def both_sides(slot):
        s_skip, s_w, s_tw = run(slot, False, "two")
        _, s_v, s_tv = run(slot, True, "two")
        offset = depth + (me * rows).astype(jnp.float32)
        close(slot, s_skip, s_w, (s_tw - s_tv) + offset * (s_w - s_v))

    both_sides(count - 1)
    for slot in middle[::-1]:
        both_sides(slot)

    @pl.when(has_source(0, False))
    def _():
        close(1, *run(1, True, "one"))
        close(0, *run(0, False, "one"))

    @pl.when(jnp.logical_not(has_source(0, False)))
    def _():
        close(0, *run(0, False, "one"))
        close(1, *run(1, True, "one"))

    for step in range(count - 1):
        share = sums[bands[lax.rem(me + step + 1, count)]]
        shares[step] = share
        share_copy(step).start()
    send((0,), True, lambda slot, many: range(many - kept_back(slot, True), many))
    send((1,), False, lambda slot, many: range(many - kept_back(slot, False), many))

    @pl.when(has_source(0, True))
    def _():
        run(1, False, "none")
        run(0, True, "none")

    @pl.when(jnp.logical_not(has_source(0, True)))
    def _():
        run(0, True, "none")
        run(1, False, "none")

    for step in range(count - 1):
        share_copy(step).wait()
    total = sums[bands[me]]
    for step in range(count - 1):
        total = total + got[step]
    own_ref[...] = total
    for backward in (False, True):
        each_piece(
            range(count - 1),
            backward,
            lambda slot, many: range(many),
            lambda copy: copy.wait_send(),
        )


def place_kernel(
    bands, outs, grads, own, out_hbm, grad_hbm, skip_hbm, residue_hbm, decay_hbm, sems, own_sems
):
    count, _, width = outs.shape
    copies = []
    for group in range(count):
        slot = bands[group]
        lanes = pl.ds(group * width, width)
        for side, (source, target) in enumerate(((outs, out_hbm), (grads, grad_hbm))):
            copies.append(
                pltpu.make_async_copy(
                    source.at[slot], target.at[:, lanes], sems.at[side, group]
                )
            )
    for row, target in enumerate((skip_hbm, residue_hbm, decay_hbm)):
        copies.append(pltpu.make_async_copy(own.at[row], target, own_sems.at[row]))
    for copy in copies:
        copy.start()
    for copy in copies:
        copy.wait()


def in_hbm(*arrays):
    return [pltpu.with_memory_space_constraint(one, pltpu.HBM) for one in arrays]


def place(bands, outs, grads, own):
    count, rows, width = outs.shape
    inside = pl.BlockSpec(memory_space=pltpu.VMEM)
    anywhere = pl.BlockSpec(memory_space=pl.ANY)
    whole = jax.ShapeDtypeStruct((rows, count * width), outs.dtype)
    small = jax.ShapeDtypeStruct((1, width), own.dtype)
    return pl.pallas_call(
        place_kernel,
        in_specs=[pl.BlockSpec(memory_space=pltpu.SMEM), inside, inside, inside],
        out_specs=[anywhere] * 5,
        out_shape=(whole, whole, small, small, small),
        scratch_shapes=[
            pltpu.SemaphoreType.DMA((2, count)),
            pltpu.SemaphoreType.DMA((3,)),
        ],
        compiler_params=pltpu.CompilerParams(vmem_limit_bytes=SCOPED),
        name="place",
    )(*in_hbm(bands), outs, grads, own)


def banded(count, inputs, cotangent, residue, decay, skip_gain, band_blocks):
    rows, channels = inputs.shape
    width = channels // count
    first = rows * 2 // PIECES
    bands = band_blocks[0]
    anywhere = pl.BlockSpec(memory_space=pl.ANY)
    inside = pl.BlockSpec(memory_space=pltpu.VMEM)
    x_flows = pltpu.SemaphoreType.DMA((flow_count(count, False),))
    c_flows = pltpu.SemaphoreType.DMA((flow_count(count, True),))
    few = pltpu.SemaphoreType.DMA((count - 1,))
    kind = inputs.dtype
    packed = pltpu.VMEM((count, rows, width), kind)
    far = pltpu.VMEM((count - 1, rows, width), kind)
    row = pltpu.VMEM((count, 1, width), jnp.float32)
    ends = pltpu.SemaphoreType.DMA((2, count - 1))
    outs, grads, own = pl.pallas_call(
        functools.partial(banded_kernel, count),
        in_specs=[anywhere] * 6,
        out_specs=[inside, inside, inside],
        out_shape=(
            pltpu.VMEM((count, rows, width), kind),
            pltpu.VMEM((count, rows, width), kind),
            pltpu.VMEM((3, 1, width), jnp.float32),
        ),
        scratch_shapes=[
            pltpu.SMEM((count,), jnp.int32),
            row,
            row,
            row,
            pltpu.VMEM((count, first, width), kind),
            pltpu.VMEM((count, rows - first, width), kind),
            pltpu.VMEM((count, first, width), kind),
            pltpu.VMEM((count, rows - first, width), kind),
            packed,
            packed,
            far,
            far,
            pltpu.VMEM((2, count + 1, 1, width), jnp.float32),
            pltpu.VMEM((2, count - 1, count + 1, 1, width), jnp.float32),
            pltpu.VMEM((count, 3, 1, width), jnp.float32),
            pltpu.VMEM((count - 1, 3, 1, width), jnp.float32),
            pltpu.VMEM((count - 1, 3, 1, width), jnp.float32),
            pltpu.VMEM((ROWS, width), jnp.float32),
            pltpu.SemaphoreType.DMA((4,)),
            pltpu.SemaphoreType.DMA((4, count)),
            x_flows,
            x_flows,
            c_flows,
            c_flows,
            ends,
            ends,
            few,
            few,
        ],
        compiler_params=pltpu.CompilerParams(
            collective_id=0, has_side_effects=True, vmem_limit_bytes=SCOPED
        ),
        name="banded",
    )(
        *in_hbm(
            bands,
            inputs,
            cotangent,
            *(part.reshape(count, 1, width) for part in (residue, decay, skip_gain)),
        )
    )
    layer_out, input_grad, *sums = place(bands, outs, grads, own)
    return (layer_out, input_grad, *(part.reshape(width) for part in sums))


def local_body(count, inputs, cotangent, residue, decay, skip_gain, band_blocks):
    rows, channels = inputs.shape
    groups = band_blocks.shape[1]
    fits = groups == count and count > 2 and rows % (PAIR * PIECES * UNROLL) == 0
    if fits and channels % (groups * LANES) == 0:
        return banded(count, inputs, cotangent, residue, decay, skip_gain, band_blocks)
    return body(inputs, cotangent, residue, decay, skip_gain, band_blocks)


def solution(mesh):
    placed = (P("ctx", "dp"), P("ctx", "dp"), P("dp"), P("dp"), P("dp"), P("dp", None))
    return jax.shard_map(
        functools.partial(local_body, mesh.shape["ctx"]),
        mesh=mesh,
        in_specs=placed,
        out_specs=(
            P("ctx", "dp"),
            P("ctx", "dp"),
            P(("dp", "ctx")),
            P(("dp", "ctx")),
            P(("dp", "ctx")),
        ),
        check_vma=False,
    )
```

```python
import functools
import jax
import jax.numpy as jnp
from jax import lax
from jax.experimental import pallas as pl
from jax.experimental.pallas import tpu as pltpu
from jax.sharding import PartitionSpec as P


def prefix(value, axis, join, neutral, backward):
    count, mine = (lax.axis_size(axis), lax.axis_index(axis))
    pieces = jax.tree.map(lambda part: lax.all_gather(part, axis), value)
    if backward:
        pieces = jax.tree.map(lambda part: part[::-1], pieces)
        mine = count - 1 - mine
    total = jax.tree.map(
        lambda part, zero: jnp.full_like(part, 0) + jnp.asarray(zero, part.dtype), value, neutral
    )

    def turn(position, total):
        longer = join(total, jax.tree.map(lambda part: part[position], pieces))
        return jax.tree.map(lambda new, old: jnp.where(position < mine, new, old), longer, total)

    return lax.fori_loop(0, count - 1, turn, total)


def compose(earlier_pair, later_pair):
    return (earlier_pair[0] * later_pair[0], earlier_pair[1] * later_pair[0] + later_pair[1])


def chain_step(earlier_pair, later_pair):
    return (earlier_pair[0] * later_pair[1] + later_pair[0], earlier_pair[1] * later_pair[1])


def local_scan(values, decay_rate, backward):
    factors = jnp.broadcast_to(jnp.exp(-decay_rate)[None, :], values.shape)
    return lax.associative_scan(compose, (factors, values), reverse=backward)[1]


def slot_groups(bands, ctx_rank, direction):
    group_count = bands.shape[0]
    slot_index = jnp.arange(group_count, dtype=jnp.int32)
    distance = (slot_index - ctx_rank) * direction
    matches = bands[None, :] + 1 == distance[:, None]
    return jnp.sum(jnp.where(matches, slot_index[None, :], 0), axis=1)


def pick(shaped, order):
    blocks = [
        lax.dynamic_index_in_dim(shaped, order[at], 1, keepdims=True)
        for at in range(order.shape[0])
    ]
    return jnp.concatenate(blocks, axis=1)


def outgoing(values, slot_group, group_count, group_width):
    shaped = values.reshape(values.shape[0], group_count, group_width)
    return pick(shaped, slot_group)


def incoming(received, source, in_range):
    picked = pick(received, source)
    picked = jnp.where(in_range[None, :, None], picked, jnp.zeros((), picked.dtype))
    return picked.reshape(picked.shape[0], -1)


def body(inputs, cotangent, residue, decay, skip_gain, band_blocks):
    values = inputs.astype(jnp.float32)
    upstream = cotangent.astype(jnp.float32)
    bands = band_blocks[0]
    block_rows, channels = values.shape
    group_count = bands.shape[0]
    group_width = channels // group_count
    ctx_rank = lax.axis_index("ctx")
    offsets = jnp.arange(block_rows, dtype=jnp.float32)[:, None]
    lengths = jnp.repeat(
        (bands + 1) * block_rows, group_width, total_repeat_length=channels
    ).astype(jnp.float32)
    band_tail = jnp.exp(-decay * lengths)[None, :]
    block_decay = jnp.exp(-decay * block_rows)
    lead_decay = jnp.exp(-decay[None, :] * (offsets + 1.0))
    trail_decay = jnp.exp(-decay[None, :] * (block_rows - offsets))
    zero_state = jnp.zeros_like(decay)
    unit_state = jnp.ones_like(decay)
    inside = local_scan(values, decay, False)
    before, _ = prefix(
        (inside[-1], block_decay), "ctx", chain_step, (zero_state, unit_state), False
    )
    carried = inside + lead_decay * before[None, :]
    send_fwd = slot_groups(bands, ctx_rank, 1)
    source_fwd = ctx_rank - bands - 1
    valid_fwd = source_fwd >= 0
    source_fwd = jnp.clip(source_fwd, 0, group_count - 1)
    inside_back = local_scan(upstream, decay, True)
    after, _ = prefix(
        (inside_back[0], block_decay), "ctx", chain_step, (zero_state, unit_state), True
    )
    back_carried = inside_back + trail_decay * after[None, :]
    send_bwd = slot_groups(bands, ctx_rank, -1)
    source_bwd = ctx_rank + bands + 1
    valid_bwd = source_bwd < group_count
    source_bwd = jnp.clip(source_bwd, 0, group_count - 1)
    received = lax.all_to_all(
        outgoing(carried, send_fwd, group_count, group_width),
        "ctx",
        split_axis=1,
        concat_axis=1,
        tiled=True,
    )
    far_state = incoming(received, source_fwd, valid_fwd)
    received_back = lax.all_to_all(
        outgoing(back_carried, send_bwd, group_count, group_width),
        "ctx",
        split_axis=1,
        concat_axis=1,
        tiled=True,
    )
    near_state = incoming(received_back, source_bwd, valid_bwd)
    truncated = carried - band_tail * far_state
    layer_out = (skip_gain[None, :] * values + residue[None, :] * truncated).astype(jnp.bfloat16)
    back_truncated = back_carried - band_tail * near_state
    input_grad = (skip_gain[None, :] * upstream + residue[None, :] * back_truncated).astype(
        jnp.bfloat16
    )
    position = ctx_rank.astype(jnp.float32) * block_rows + offsets
    weighted = upstream * truncated
    moment = jnp.sum(position * weighted, axis=0) - jnp.sum(
        position * values * back_truncated, axis=0
    )
    grad_terms = jnp.stack(
        [jnp.sum(values * upstream, axis=0), jnp.sum(weighted, axis=0), -decay * residue * moment]
    )
    share_width = channels // lax.axis_size("ctx")
    summed = lax.psum(grad_terms, "ctx")
    own_share = lax.dynamic_slice_in_dim(summed, ctx_rank * share_width, share_width, 1)
    return (layer_out, input_grad, own_share[0], own_share[1], own_share[2])


MESH = pl.DeviceIdType.MESH
LANES = 128
ROWS = 8
PAIR = 2 * ROWS
PIECES = 8
UNROLL = 4
SCOPED = 48_000_000


def greet(count, me):
    barrier = pltpu.get_barrier_semaphore()
    for step in range(1, count):
        pl.semaphore_signal(
            barrier,
            inc=1,
            device_id={"ctx": lax.rem(me + step, count)},
            device_id_type=MESH,
        )
    return lambda: pl.semaphore_wait(barrier, count - 1)


def parts_of(slot, backward):
    if backward:
        return {0: (4, 3, 1), 1: (2, 6)}.get(slot, (8,))
    return {0: (2, 6), 1: (6, 1, 1)}.get(slot, (8,))


def kept_back(slot, backward):
    return 2 if slot == (0 if backward else 1) else 0


def piece_rows(rows, slot, backward, piece):
    parts = parts_of(slot, backward)
    size = rows * parts[piece] // PIECES
    start = rows * sum(parts[:piece]) // PIECES
    return (rows - start - size if backward else start, size)


def piece_at(slot, backward, piece):
    return sum(len(parts_of(before, backward)) for before in range(slot)) + piece


def flow_count(count, backward):
    return sum(len(parts_of(slot, backward)) for slot in range(count - 1))


def end_row(slot, backward):
    return 0 if backward and slot == 0 else slot + 1


def pair_at(step):
    return pl.ds(pl.multiple_of(step * PAIR, PAIR), PAIR)


def banded_kernel(
    count,
    bands_hbm,
    x_hbm,
    c_hbm,
    residue_hbm,
    decay_hbm,
    skip_hbm,
    outs,
    grads,
    own_ref,
    order_ref,
    bands,
    residue_ref,
    decay_ref,
    skip_ref,
    x_first,
    x_rest,
    c_first,
    c_rest,
    xs,
    cs,
    far_x,
    far_c,
    ends,
    far_ends,
    sums,
    shares,
    got,
    blank,
    small_sem,
    load_sem,
    x_send,
    x_recv,
    c_send,
    c_recv,
    e_send,
    e_recv,
    s_send,
    s_recv,
):
    me = lax.axis_index("ctx")
    _, rows, width = xs.shape
    shape = (ROWS, width)
    first = x_first.shape[1]

    all_here = greet(count, me)

    small = [
        pltpu.make_async_copy(source, target, small_sem.at[at])
        for at, (source, target) in enumerate(
            (
                (bands_hbm, bands),
                (decay_hbm, decay_ref),
                (residue_hbm, residue_ref),
                (skip_hbm, skip_ref),
            )
        )
    ]
    small[0].start()
    chunks = (
        (c_hbm, rows - first, c_first, cs),
        (x_hbm, 0, x_first, xs),
        (c_hbm, 0, c_rest, cs),
        (x_hbm, first, x_rest, xs),
    )

    def load(chunk, group):
        source, start, target, _ = chunks[chunk]
        lanes = pl.ds(group * width, width)
        return pltpu.make_async_copy(
            source.at[pl.ds(start, target.shape[1]), lanes],
            target.at[group],
            load_sem.at[chunk, group],
        )

    for chunk in range(len(chunks)):
        for group in range(count):
            load(chunk, group).start()
    for copy in small[1:]:
        copy.start()
    small[0].wait()
    groups = []
    for slot in range(count):
        group = jnp.int32(0)
        for other in range(count):
            group = jnp.where(bands[other] == slot, other, group)
        groups.append(group)

    def pack(chunk):
        _, start, whole, packed = chunks[chunk]
        for group in range(count):
            load(chunk, group).wait()

        def turn(step, _):
            to = pl.ds(pl.multiple_of(start + step * PAIR, PAIR), PAIR)
            for slot in range(count):
                packed[slot, to, :] = whole[groups[slot], pair_at(step), :]
            return 0

        lax.fori_loop(0, whole.shape[1] // PAIR, turn, 0, unroll=UNROLL)

    def has_source(slot, backward):
        return me + slot + 1 < count if backward else me >= slot + 1

    def flow(slot, backward, piece):
        start, size = piece_rows(rows, slot, backward, piece)
        at = pl.ds(start, size)
        sem = piece_at(slot, backward, piece)
        source, target, sends, recvs = (
            (cs, far_c, c_send, c_recv) if backward else (xs, far_x, x_send, x_recv)
        )
        to = me + count - slot - 1 if backward else me + slot + 1
        return pltpu.make_async_remote_copy(
            src_ref=source.at[slot, at],
            dst_ref=target.at[slot, at],
            send_sem=sends.at[sem],
            recv_sem=recvs.at[sem],
            device_id={"ctx": lax.rem(to, count)},
            device_id_type=MESH,
        )

    def send(slot, backward, pieces, asked=True):
        sends_it = jnp.logical_and(has_source(slot, not backward), asked)
        for piece in pieces:
            pl.when(sends_it)(lambda: flow(slot, backward, piece).start())

    def pieces_of(slot, backward):
        return tuple(range(len(parts_of(slot, backward))))

    def end_copy(far, backward):
        first_row = end_row(far - 1, backward)
        if far == 1 or far == 2 and backward:
            first_row = far - 1
        at = pl.ds(first_row, count + 1 - first_row)
        side = int(backward)
        to = me + count - far if backward else me + far
        return pltpu.make_async_remote_copy(
            src_ref=ends.at[side, at],
            dst_ref=far_ends.at[side, far - 1, at],
            send_sem=e_send.at[side, far - 1],
            recv_sem=e_recv.at[side, far - 1],
            device_id={"ctx": lax.rem(to, count)},
            device_id_type=MESH,
        )

    def each_end(act_send, act_receive):
        for far in range(1, count):
            for backward in (False, True):
                if act_send is not None:
                    pl.when(has_source(far - 1, not backward))(
                        lambda: act_send(end_copy(far, backward))
                    )
                if act_receive is not None:
                    pl.when(has_source(far - 1, backward))(
                        lambda: act_receive(end_copy(far, backward))
                    )

    def share_copy(step):
        to = lax.rem(me + step + 1, count)
        return pltpu.make_async_remote_copy(
            src_ref=shares.at[step],
            dst_ref=got.at[step],
            send_sem=s_send.at[step],
            recv_sem=s_recv.at[step],
            device_id={"ctx": to},
            device_id_type=MESH,
        )

    middle = tuple(range(2, count - 1))
    lowest, highest = me == 0, me == count - 1
    outer = jnp.logical_or(lowest, highest)
    keeps_up, keeps_down = me == 1, me == count - 2
    pack(0)
    all_here()
    send(1, True, (0,), jnp.logical_not(highest))
    pack(1)
    send(0, False, (0,))
    pack(2)
    pack(3)
    for copy in small[1:]:
        copy.wait()

    level = lax.broadcasted_iota(jnp.int32, shape, 0)
    depth = level.astype(jnp.float32)
    blank[...] = jnp.zeros(shape, jnp.float32)
    zero = blank[...]
    steps = rows // PAIR
    for slot in range(count):
        rate = decay_ref[groups[slot]]
        leap_pair = jnp.broadcast_to(jnp.exp(-rate * PAIR), shape)
        wide_pair = leap_pair * float(PAIR)
        weighted = {0: (0, 1), 1: (2, 3)}.get(slot, ())

        def turn(step, state):
            held, moments = state
            ahead = xs[slot, pair_at(step), :].astype(jnp.float32)
            back = cs[slot, pair_at(steps - 1 - step), :].astype(jnp.float32)
            parts = (ahead[:ROWS], ahead[ROWS:], back[:ROWS], back[ROWS:])
            moments = tuple(
                moment * leap_pair + held[at] * wide_pair
                for moment, at in zip(moments, weighted)
            )
            return (
                tuple(old * leap_pair + new for old, new in zip(held, parts)),
                moments,
            )

        held, moments = lax.fori_loop(
            0, steps, turn, ((zero,) * 4, (zero,) * len(weighted)), unroll=UNROLL
        )
        apart = (PAIR - 1 - depth, ROWS - 1 - depth, depth, ROWS + depth)
        factors = [jnp.exp(-rate * far) for far in apart]
        scaled = [one * factor for one, factor in zip(held, factors)]
        for side in range(2):
            both = scaled[2 * side] + scaled[2 * side + 1]
            ends[side, end_row(slot, side)] = jnp.sum(both, axis=0, keepdims=True)
        if weighted:
            both = zero
            for moment, at in zip(moments, weighted):
                both = both + factors[at] * moment + apart[at] * scaled[at]
            ends[slot, slot] = jnp.sum(both, axis=0, keepdims=True)
    each_end(lambda copy: copy.start(), None)

    def ends_here():
        each_end(lambda copy: copy.wait_send(), lambda copy: copy.wait_recv())

    pl.when(outer)(ends_here)
    last_up = pieces_of(1, False)[-kept_back(1, False) :]
    last_down = pieces_of(0, True)[-kept_back(0, True) :]
    send(1, True, (0,), highest)
    send(1, True, pieces_of(1, True)[1:])
    for slot in middle:
        send(slot, True, pieces_of(slot, True))
    send(0, True, pieces_of(0, True)[: -len(last_down)])
    send(0, True, last_down, jnp.logical_not(keeps_down))
    for slot in middle[::-1]:
        send(slot, False, pieces_of(slot, False))
    send(0, False, pieces_of(0, False)[1:])
    send(1, False, pieces_of(1, False)[: -len(last_up)])
    send(1, False, last_up, jnp.logical_not(keeps_up))

    for slot in range(count - 1):
        for backward, far in ((False, far_x), (True, far_c)):

            @pl.when(jnp.logical_not(has_source(slot, backward)))
            def _():
                def clear(step, _):
                    far[slot, pair_at(step), :] = jnp.zeros((PAIR, width), far.dtype)
                    return 0

                lax.fori_loop(0, steps, clear, 0, unroll=UNROLL)

    pl.when(jnp.logical_not(outer))(ends_here)

    def scan(tile, hops):
        for hop, turn, factor in hops:
            tile = tile + factor * pltpu.roll(tile, turn, 0)
        return tile

    def scan_both(tile, moment, hops):
        for hop, turn, factor in hops:
            moved = pltpu.roll(tile, turn, 0)
            moment = moment + factor * (pltpu.roll(moment, turn, 0) + float(hop) * moved)
            tile = tile + factor * moved
        return tile, moment

    def run(slot, backward, mode):
        band = slot + 1
        reach = slot < count - 1
        one = mode == "one"
        rate = decay_ref[groups[slot]]
        start = jnp.zeros((1, width), jnp.float32)
        start_moment = start
        side = int(backward)
        for apart in range(min(band, count - 1)):
            kept = has_source(apart, backward)
            span = float(apart * rows)
            factor = jnp.exp(-rate * span)
            end = far_ends[side, apart, end_row(slot, backward)]
            start = start + jnp.where(kept, factor * end, 0.0)
            if one:
                moment = far_ends[side, apart, slot] + span * end
                start_moment = start_moment + jnp.where(kept, factor * moment, 0.0)
        tail_row = jnp.exp(-rate * float(band * rows))
        tail = jnp.broadcast_to(tail_row, shape)
        far_tail = jnp.broadcast_to(tail_row * float(band * rows), shape)
        leap = jnp.broadcast_to(jnp.exp(-rate * ROWS), shape)
        wide = leap * float(ROWS)
        residue = jnp.broadcast_to(residue_ref[groups[slot]], shape)
        skip = jnp.broadcast_to(skip_ref[groups[slot]], shape)
        ahead = ROWS - depth if backward else depth + 1.0
        lead = jnp.exp(-rate * ahead)
        lead_moment = lead * ahead
        hops = []
        for hop in (1, 2, 4):
            inside = level < ROWS - hop if backward else level >= hop
            factor = jnp.where(inside, jnp.exp(-rate * hop), 0.0)
            hops.append((hop, ROWS - hop if backward else hop, factor))
        source, other_side = (cs, xs) if backward else (xs, cs)
        target = grads if backward else outs
        far_ref = far_c if backward else far_x
        edge = slice(0, 1) if backward else slice(ROWS - 1, ROWS)

        def turn(step, state):
            carry, moment_carry, s_skip, s_w, s_m = state
            if backward:
                step = steps - 1 - step
            at = pair_at(step)
            base = (step * PAIR).astype(jnp.float32)
            values = source[slot, at, :].astype(jnp.float32)
            if mode != "none":
                others = other_side[slot, at, :].astype(jnp.float32)
            if reach:
                far = far_ref[slot, at, :].astype(jnp.float32)
            made = [None, None]
            for half in (1, 0) if backward else (0, 1):
                part = slice(half * ROWS, (half + 1) * ROWS)
                fresh = values[part]
                if reach:
                    fresh = fresh - tail * far[part]
                if one:
                    local, local_moment = scan_both(fresh, -far_tail * far[part], hops)
                    moment = local_moment + lead * moment_carry + lead_moment * carry
                    moment_carry = (
                        leap * moment_carry
                        + wide * carry
                        + jnp.broadcast_to(local_moment[edge], shape)
                    )
                else:
                    local = scan(fresh, hops)
                truncated = local + lead * carry
                carry = leap * carry + jnp.broadcast_to(local[edge], shape)
                made[half] = skip * values[part] + residue * truncated
                if mode != "none":
                    w = others[part] * truncated
                    s_w = s_w + w
                if one:
                    s_m = s_m + others[part] * moment
                elif mode == "two":
                    s_m = s_m + (base + half * ROWS) * w
                if one or mode == "two" and not backward:
                    s_skip = s_skip + values[part] * others[part]
            target[slot, at, :] = jnp.concatenate(made, axis=0).astype(target.dtype)
            return carry, moment_carry, s_skip, s_w, s_m

        state = (
            zero + jnp.broadcast_to(start, shape),
            zero + jnp.broadcast_to(start_moment, shape),
            zero,
            zero,
            zero,
        )
        done = 0
        parts = parts_of(slot, backward) if reach else (PIECES,)
        for piece, part in enumerate(parts):
            if reach:
                pl.when(has_source(slot, backward))(
                    lambda: flow(slot, backward, piece).wait_recv()
                )
            span = (done * steps // PIECES, (done + part) * steps // PIECES)
            state = lax.fori_loop(*span, turn, state, unroll=UNROLL)
            done += part
        return state[2:]

    def close(slot, s_skip, s_w, moment):
        scale = -decay_ref[groups[slot]] * residue_ref[groups[slot]]
        sums[slot, 0] = jnp.sum(s_skip, axis=0, keepdims=True)
        sums[slot, 1] = jnp.sum(s_w, axis=0, keepdims=True)
        sums[slot, 2] = scale * jnp.sum(moment, axis=0, keepdims=True)

    def both_sides(slot):
        s_skip, s_w, s_tw = run(slot, False, "two")
        _, s_v, s_tv = run(slot, True, "two")
        offset = depth + (me * rows).astype(jnp.float32)
        close(slot, s_skip, s_w, (s_tw - s_tv) + offset * (s_w - s_v))

    both_sides(count - 1)
    for slot in middle[::-1]:
        both_sides(slot)

    @pl.when(has_source(0, False))
    def _():
        close(1, *run(1, True, "one"))
        close(0, *run(0, False, "one"))

    @pl.when(jnp.logical_not(has_source(0, False)))
    def _():
        close(0, *run(0, False, "one"))
        close(1, *run(1, True, "one"))

    for step in range(count - 1):
        share = sums[bands[lax.rem(me + step + 1, count)]]
        shares[step] = share
        share_copy(step).start()
    send(0, True, last_down, keeps_down)
    send(1, False, last_up, keeps_up)

    @pl.when(has_source(0, True))
    def _():
        run(1, False, "none")
        run(0, True, "none")

    @pl.when(jnp.logical_not(has_source(0, True)))
    def _():
        run(0, True, "none")
        run(1, False, "none")

    for step in range(count - 1):
        share_copy(step).wait()
    total = sums[bands[me]]
    for step in range(count - 1):
        total = total + got[step]
    own_ref[...] = total
    for group in range(count):
        order_ref[group] = bands[group]
    for backward in (False, True):
        for slot in range(count - 1):
            for piece in pieces_of(slot, backward):
                pl.when(has_source(slot, not backward))(
                    lambda: flow(slot, backward, piece).wait_send()
                )


def place_kernel(
    bands, outs, grads, own, out_hbm, grad_hbm, skip_hbm, residue_hbm, decay_hbm, sems, own_sems
):
    count, _, width = outs.shape
    copies = []
    for group in range(count):
        slot = bands[group]
        lanes = pl.ds(group * width, width)
        for side, (source, target) in enumerate(((outs, out_hbm), (grads, grad_hbm))):
            copies.append(
                pltpu.make_async_copy(
                    source.at[slot], target.at[:, lanes], sems.at[side, group]
                )
            )
    for row, target in enumerate((skip_hbm, residue_hbm, decay_hbm)):
        copies.append(pltpu.make_async_copy(own.at[row], target, own_sems.at[row]))
    for copy in copies:
        copy.start()
    for copy in copies:
        copy.wait()


def in_hbm(*arrays):
    return [pltpu.with_memory_space_constraint(one, pltpu.HBM) for one in arrays]


def place(bands, outs, grads, own):
    count, rows, width = outs.shape
    inside = pl.BlockSpec(memory_space=pltpu.VMEM)
    anywhere = pl.BlockSpec(memory_space=pl.ANY)
    whole = jax.ShapeDtypeStruct((rows, count * width), outs.dtype)
    small = jax.ShapeDtypeStruct((1, width), own.dtype)
    return pl.pallas_call(
        place_kernel,
        in_specs=[pl.BlockSpec(memory_space=pltpu.SMEM), inside, inside, inside],
        out_specs=[anywhere] * 5,
        out_shape=(whole, whole, small, small, small),
        scratch_shapes=[
            pltpu.SemaphoreType.DMA((2, count)),
            pltpu.SemaphoreType.DMA((3,)),
        ],
        compiler_params=pltpu.CompilerParams(vmem_limit_bytes=SCOPED),
        name="place",
    )(bands, outs, grads, own)


def banded(count, inputs, cotangent, residue, decay, skip_gain, band_blocks):
    rows, channels = inputs.shape
    width = channels // count
    first = rows * 2 // PIECES
    bands = band_blocks[0]
    anywhere = pl.BlockSpec(memory_space=pl.ANY)
    inside = pl.BlockSpec(memory_space=pltpu.VMEM)
    x_flows = pltpu.SemaphoreType.DMA((flow_count(count, False),))
    c_flows = pltpu.SemaphoreType.DMA((flow_count(count, True),))
    few = pltpu.SemaphoreType.DMA((count - 1,))
    kind = inputs.dtype
    packed = pltpu.VMEM((count, rows, width), kind)
    far = pltpu.VMEM((count - 1, rows, width), kind)
    row = pltpu.VMEM((count, 1, width), jnp.float32)
    ends = pltpu.SemaphoreType.DMA((2, count - 1))
    outs, grads, own, order = pl.pallas_call(
        functools.partial(banded_kernel, count),
        in_specs=[anywhere] * 6,
        out_specs=[inside, inside, inside, pl.BlockSpec(memory_space=pltpu.SMEM)],
        out_shape=(
            pltpu.VMEM((count, rows, width), kind),
            pltpu.VMEM((count, rows, width), kind),
            pltpu.VMEM((3, 1, width), jnp.float32),
            pltpu.SMEM((count,), jnp.int32),
        ),
        scratch_shapes=[
            pltpu.SMEM((count,), jnp.int32),
            row,
            row,
            row,
            pltpu.VMEM((count, first, width), kind),
            pltpu.VMEM((count, rows - first, width), kind),
            pltpu.VMEM((count, first, width), kind),
            pltpu.VMEM((count, rows - first, width), kind),
            packed,
            packed,
            far,
            far,
            pltpu.VMEM((2, count + 1, 1, width), jnp.float32),
            pltpu.VMEM((2, count - 1, count + 1, 1, width), jnp.float32),
            pltpu.VMEM((count, 3, 1, width), jnp.float32),
            pltpu.VMEM((count - 1, 3, 1, width), jnp.float32),
            pltpu.VMEM((count - 1, 3, 1, width), jnp.float32),
            pltpu.VMEM((ROWS, width), jnp.float32),
            pltpu.SemaphoreType.DMA((4,)),
            pltpu.SemaphoreType.DMA((4, count)),
            x_flows,
            x_flows,
            c_flows,
            c_flows,
            ends,
            ends,
            few,
            few,
        ],
        compiler_params=pltpu.CompilerParams(
            collective_id=0, has_side_effects=True, vmem_limit_bytes=SCOPED
        ),
        name="banded",
    )(
        *in_hbm(
            bands,
            inputs,
            cotangent,
            *(part.reshape(count, 1, width) for part in (residue, decay, skip_gain)),
        )
    )
    layer_out, input_grad, *sums = place(order, outs, grads, own)
    return (layer_out, input_grad, *(part.reshape(width) for part in sums))


def local_body(count, inputs, cotangent, residue, decay, skip_gain, band_blocks):
    rows, channels = inputs.shape
    groups = band_blocks.shape[1]
    fits = groups == count and count > 2 and rows % (PAIR * PIECES * UNROLL) == 0
    if fits and channels % (groups * LANES) == 0:
        return banded(count, inputs, cotangent, residue, decay, skip_gain, band_blocks)
    return body(inputs, cotangent, residue, decay, skip_gain, band_blocks)


def solution(mesh):
    placed = (P("ctx", "dp"), P("ctx", "dp"), P("dp"), P("dp"), P("dp"), P("dp", None))
    return jax.shard_map(
        functools.partial(local_body, mesh.shape["ctx"]),
        mesh=mesh,
        in_specs=placed,
        out_specs=(
            P("ctx", "dp"),
            P("ctx", "dp"),
            P(("dp", "ctx")),
            P(("dp", "ctx")),
            P(("dp", "ctx")),
        ),
        check_vma=False,
    )
```

```python
import functools
import jax
import jax.numpy as jnp
from jax import lax
from jax.experimental import pallas as pl
from jax.experimental.pallas import tpu as pltpu
from jax.sharding import PartitionSpec as P


def prefix(value, axis, join, neutral, backward):
    count, mine = (lax.axis_size(axis), lax.axis_index(axis))
    pieces = jax.tree.map(lambda part: lax.all_gather(part, axis), value)
    if backward:
        pieces = jax.tree.map(lambda part: part[::-1], pieces)
        mine = count - 1 - mine
    total = jax.tree.map(
        lambda part, zero: jnp.full_like(part, 0) + jnp.asarray(zero, part.dtype), value, neutral
    )

    def turn(position, total):
        longer = join(total, jax.tree.map(lambda part: part[position], pieces))
        return jax.tree.map(lambda new, old: jnp.where(position < mine, new, old), longer, total)

    return lax.fori_loop(0, count - 1, turn, total)


def compose(earlier_pair, later_pair):
    return (earlier_pair[0] * later_pair[0], earlier_pair[1] * later_pair[0] + later_pair[1])


def chain_step(earlier_pair, later_pair):
    return (earlier_pair[0] * later_pair[1] + later_pair[0], earlier_pair[1] * later_pair[1])


def local_scan(values, decay_rate, backward):
    factors = jnp.broadcast_to(jnp.exp(-decay_rate)[None, :], values.shape)
    return lax.associative_scan(compose, (factors, values), reverse=backward)[1]


def slot_groups(bands, ctx_rank, direction):
    group_count = bands.shape[0]
    slot_index = jnp.arange(group_count, dtype=jnp.int32)
    distance = (slot_index - ctx_rank) * direction
    matches = bands[None, :] + 1 == distance[:, None]
    return jnp.sum(jnp.where(matches, slot_index[None, :], 0), axis=1)


def pick(shaped, order):
    blocks = [
        lax.dynamic_index_in_dim(shaped, order[at], 1, keepdims=True)
        for at in range(order.shape[0])
    ]
    return jnp.concatenate(blocks, axis=1)


def outgoing(values, slot_group, group_count, group_width):
    shaped = values.reshape(values.shape[0], group_count, group_width)
    return pick(shaped, slot_group)


def incoming(received, source, in_range):
    picked = pick(received, source)
    picked = jnp.where(in_range[None, :, None], picked, jnp.zeros((), picked.dtype))
    return picked.reshape(picked.shape[0], -1)


def body(inputs, cotangent, residue, decay, skip_gain, band_blocks):
    values = inputs.astype(jnp.float32)
    upstream = cotangent.astype(jnp.float32)
    bands = band_blocks[0]
    block_rows, channels = values.shape
    group_count = bands.shape[0]
    group_width = channels // group_count
    ctx_rank = lax.axis_index("ctx")
    offsets = jnp.arange(block_rows, dtype=jnp.float32)[:, None]
    lengths = jnp.repeat(
        (bands + 1) * block_rows, group_width, total_repeat_length=channels
    ).astype(jnp.float32)
    band_tail = jnp.exp(-decay * lengths)[None, :]
    block_decay = jnp.exp(-decay * block_rows)
    lead_decay = jnp.exp(-decay[None, :] * (offsets + 1.0))
    trail_decay = jnp.exp(-decay[None, :] * (block_rows - offsets))
    zero_state = jnp.zeros_like(decay)
    unit_state = jnp.ones_like(decay)
    inside = local_scan(values, decay, False)
    before, _ = prefix(
        (inside[-1], block_decay), "ctx", chain_step, (zero_state, unit_state), False
    )
    carried = inside + lead_decay * before[None, :]
    send_fwd = slot_groups(bands, ctx_rank, 1)
    source_fwd = ctx_rank - bands - 1
    valid_fwd = source_fwd >= 0
    source_fwd = jnp.clip(source_fwd, 0, group_count - 1)
    inside_back = local_scan(upstream, decay, True)
    after, _ = prefix(
        (inside_back[0], block_decay), "ctx", chain_step, (zero_state, unit_state), True
    )
    back_carried = inside_back + trail_decay * after[None, :]
    send_bwd = slot_groups(bands, ctx_rank, -1)
    source_bwd = ctx_rank + bands + 1
    valid_bwd = source_bwd < group_count
    source_bwd = jnp.clip(source_bwd, 0, group_count - 1)
    received = lax.all_to_all(
        outgoing(carried, send_fwd, group_count, group_width),
        "ctx",
        split_axis=1,
        concat_axis=1,
        tiled=True,
    )
    far_state = incoming(received, source_fwd, valid_fwd)
    received_back = lax.all_to_all(
        outgoing(back_carried, send_bwd, group_count, group_width),
        "ctx",
        split_axis=1,
        concat_axis=1,
        tiled=True,
    )
    near_state = incoming(received_back, source_bwd, valid_bwd)
    truncated = carried - band_tail * far_state
    layer_out = (skip_gain[None, :] * values + residue[None, :] * truncated).astype(jnp.bfloat16)
    back_truncated = back_carried - band_tail * near_state
    input_grad = (skip_gain[None, :] * upstream + residue[None, :] * back_truncated).astype(
        jnp.bfloat16
    )
    position = ctx_rank.astype(jnp.float32) * block_rows + offsets
    weighted = upstream * truncated
    moment = jnp.sum(position * weighted, axis=0) - jnp.sum(
        position * values * back_truncated, axis=0
    )
    grad_terms = jnp.stack(
        [jnp.sum(values * upstream, axis=0), jnp.sum(weighted, axis=0), -decay * residue * moment]
    )
    share_width = channels // lax.axis_size("ctx")
    summed = lax.psum(grad_terms, "ctx")
    own_share = lax.dynamic_slice_in_dim(summed, ctx_rank * share_width, share_width, 1)
    return (layer_out, input_grad, own_share[0], own_share[1], own_share[2])


MESH = pl.DeviceIdType.MESH
LANES = 128
ROWS = 8
PAIR = 2 * ROWS
PIECES = 8
UNROLL = 4
SCOPED = 48_000_000


def greet(count, me):
    barrier = pltpu.get_barrier_semaphore()
    for step in range(1, count):
        pl.semaphore_signal(
            barrier,
            inc=1,
            device_id={"ctx": lax.rem(me + step, count)},
            device_id_type=MESH,
        )
    return lambda: pl.semaphore_wait(barrier, count - 1)


def parts_of(slot, backward):
    if backward:
        return {0: (4, 3, 1), 1: (2, 6)}.get(slot, (8,))
    return {0: (2, 6), 1: (7, 1)}.get(slot, (8,))


def kept_back(slot, backward):
    if backward:
        return 2 if slot == 0 else 0
    return 1 if slot == 1 else 0


def piece_rows(rows, slot, backward, piece):
    parts = parts_of(slot, backward)
    size = rows * parts[piece] // PIECES
    start = rows * sum(parts[:piece]) // PIECES
    return (rows - start - size if backward else start, size)


def piece_at(slot, backward, piece):
    return sum(len(parts_of(before, backward)) for before in range(slot)) + piece


def flow_count(count, backward):
    return sum(len(parts_of(slot, backward)) for slot in range(count - 1))


def end_row(slot, backward):
    return 0 if backward and slot == 0 else slot + 1


def pair_at(step):
    return pl.ds(pl.multiple_of(step * PAIR, PAIR), PAIR)


def banded_kernel(
    count,
    bands_hbm,
    x_hbm,
    c_hbm,
    residue_hbm,
    decay_hbm,
    skip_hbm,
    outs,
    grads,
    own_ref,
    order_ref,
    bands,
    residue_ref,
    decay_ref,
    skip_ref,
    x_first,
    x_rest,
    c_first,
    c_rest,
    xs,
    cs,
    far_x,
    far_c,
    ends,
    far_ends,
    sums,
    shares,
    got,
    blank,
    small_sem,
    load_sem,
    x_send,
    x_recv,
    c_send,
    c_recv,
    e_send,
    e_recv,
    s_send,
    s_recv,
):
    me = lax.axis_index("ctx")
    _, rows, width = xs.shape
    shape = (ROWS, width)
    first = x_first.shape[1]

    all_here = greet(count, me)

    small = [
        pltpu.make_async_copy(source, target, small_sem.at[at])
        for at, (source, target) in enumerate(
            (
                (bands_hbm, bands),
                (decay_hbm, decay_ref),
                (residue_hbm, residue_ref),
                (skip_hbm, skip_ref),
            )
        )
    ]
    small[0].start()
    chunks = (
        (c_hbm, rows - first, c_first, cs),
        (x_hbm, 0, x_first, xs),
        (c_hbm, 0, c_rest, cs),
        (x_hbm, first, x_rest, xs),
    )

    def load(chunk, group):
        source, start, target, _ = chunks[chunk]
        lanes = pl.ds(group * width, width)
        return pltpu.make_async_copy(
            source.at[pl.ds(start, target.shape[1]), lanes],
            target.at[group],
            load_sem.at[chunk, group],
        )

    for chunk in range(len(chunks)):
        for group in range(count):
            load(chunk, group).start()
    for copy in small[1:]:
        copy.start()
    small[0].wait()
    groups = []
    for slot in range(count):
        group = jnp.int32(0)
        for other in range(count):
            group = jnp.where(bands[other] == slot, other, group)
        groups.append(group)

    def pack(chunk):
        _, start, whole, packed = chunks[chunk]
        for group in range(count):
            load(chunk, group).wait()

        def turn(step, _):
            to = pl.ds(pl.multiple_of(start + step * PAIR, PAIR), PAIR)
            for slot in range(count):
                packed[slot, to, :] = whole[groups[slot], pair_at(step), :]
            return 0

        lax.fori_loop(0, whole.shape[1] // PAIR, turn, 0, unroll=UNROLL)

    def has_source(slot, backward):
        return me + slot + 1 < count if backward else me >= slot + 1

    def flow(slot, backward, piece):
        start, size = piece_rows(rows, slot, backward, piece)
        at = pl.ds(start, size)
        sem = piece_at(slot, backward, piece)
        source, target, sends, recvs = (
            (cs, far_c, c_send, c_recv) if backward else (xs, far_x, x_send, x_recv)
        )
        to = me + count - slot - 1 if backward else me + slot + 1
        return pltpu.make_async_remote_copy(
            src_ref=source.at[slot, at],
            dst_ref=target.at[slot, at],
            send_sem=sends.at[sem],
            recv_sem=recvs.at[sem],
            device_id={"ctx": lax.rem(to, count)},
            device_id_type=MESH,
        )

    def send(slot, backward, pieces, asked=True):
        sends_it = jnp.logical_and(has_source(slot, not backward), asked)
        for piece in pieces:
            pl.when(sends_it)(lambda: flow(slot, backward, piece).start())

    def pieces_of(slot, backward):
        return tuple(range(len(parts_of(slot, backward))))

    def end_copy(far, backward):
        first_row = end_row(far - 1, backward)
        if far == 1 or far == 2 and backward:
            first_row = far - 1
        at = pl.ds(first_row, count + 1 - first_row)
        side = int(backward)
        to = me + count - far if backward else me + far
        return pltpu.make_async_remote_copy(
            src_ref=ends.at[side, at],
            dst_ref=far_ends.at[side, far - 1, at],
            send_sem=e_send.at[side, far - 1],
            recv_sem=e_recv.at[side, far - 1],
            device_id={"ctx": lax.rem(to, count)},
            device_id_type=MESH,
        )

    def each_end(act_send, act_receive):
        for far in range(1, count):
            for backward in (False, True):
                if act_send is not None:
                    pl.when(has_source(far - 1, not backward))(
                        lambda: act_send(end_copy(far, backward))
                    )
                if act_receive is not None:
                    pl.when(has_source(far - 1, backward))(
                        lambda: act_receive(end_copy(far, backward))
                    )

    def share_copy(step):
        to = lax.rem(me + step + 1, count)
        return pltpu.make_async_remote_copy(
            src_ref=shares.at[step],
            dst_ref=got.at[step],
            send_sem=s_send.at[step],
            recv_sem=s_recv.at[step],
            device_id={"ctx": to},
            device_id_type=MESH,
        )

    middle = tuple(range(2, count - 1))
    lowest, highest = me == 0, me == count - 1
    outer = jnp.logical_or(lowest, highest)
    keeps_up, keeps_down = me == 1, me == count - 2
    pack(0)
    all_here()
    send(1, True, (0,), jnp.logical_not(highest))
    pack(1)
    send(0, False, (0,))
    pack(2)
    pack(3)
    for copy in small[1:]:
        copy.wait()

    level = lax.broadcasted_iota(jnp.int32, shape, 0)
    depth = level.astype(jnp.float32)
    blank[...] = jnp.zeros(shape, jnp.float32)
    zero = blank[...]
    steps = rows // PAIR
    for slot in range(count):
        rate = decay_ref[groups[slot]]
        leap_pair = jnp.broadcast_to(jnp.exp(-rate * PAIR), shape)
        wide_pair = leap_pair * float(PAIR)
        weighted = {0: (0, 1), 1: (2, 3)}.get(slot, ())

        def turn(step, state):
            held, moments = state
            ahead = xs[slot, pair_at(step), :].astype(jnp.float32)
            back = cs[slot, pair_at(steps - 1 - step), :].astype(jnp.float32)
            parts = (ahead[:ROWS], ahead[ROWS:], back[:ROWS], back[ROWS:])
            moments = tuple(
                moment * leap_pair + held[at] * wide_pair
                for moment, at in zip(moments, weighted)
            )
            return (
                tuple(old * leap_pair + new for old, new in zip(held, parts)),
                moments,
            )

        held, moments = lax.fori_loop(
            0, steps, turn, ((zero,) * 4, (zero,) * len(weighted)), unroll=UNROLL
        )
        apart = (PAIR - 1 - depth, ROWS - 1 - depth, depth, ROWS + depth)
        factors = [jnp.exp(-rate * far) for far in apart]
        scaled = [one * factor for one, factor in zip(held, factors)]
        for side in range(2):
            both = scaled[2 * side] + scaled[2 * side + 1]
            ends[side, end_row(slot, side)] = jnp.sum(both, axis=0, keepdims=True)
        if weighted:
            both = zero
            for moment, at in zip(moments, weighted):
                both = both + factors[at] * moment + apart[at] * scaled[at]
            ends[slot, slot] = jnp.sum(both, axis=0, keepdims=True)
    each_end(lambda copy: copy.start(), None)

    def ends_here():
        each_end(lambda copy: copy.wait_send(), lambda copy: copy.wait_recv())

    pl.when(outer)(ends_here)
    last_up = pieces_of(1, False)[-kept_back(1, False) :]
    last_down = pieces_of(0, True)[-kept_back(0, True) :]
    send(1, True, (0,), highest)
    send(1, True, pieces_of(1, True)[1:])
    for slot in middle:
        send(slot, True, pieces_of(slot, True))
    send(0, True, pieces_of(0, True)[: -len(last_down)])
    send(0, True, last_down, jnp.logical_not(keeps_down))
    for slot in middle[::-1]:
        send(slot, False, pieces_of(slot, False))
    send(0, False, pieces_of(0, False)[1:])
    send(1, False, pieces_of(1, False)[: -len(last_up)])
    send(1, False, last_up, jnp.logical_not(keeps_up))

    for slot in range(count - 1):
        for backward, far in ((False, far_x), (True, far_c)):

            @pl.when(jnp.logical_not(has_source(slot, backward)))
            def _():
                def clear(step, _):
                    far[slot, pair_at(step), :] = jnp.zeros((PAIR, width), far.dtype)
                    return 0

                lax.fori_loop(0, steps, clear, 0, unroll=UNROLL)

    pl.when(jnp.logical_not(outer))(ends_here)

    def scan(tile, hops):
        for hop, turn, factor in hops:
            tile = tile + factor * pltpu.roll(tile, turn, 0)
        return tile

    def scan_both(tile, moment, hops):
        for hop, turn, factor in hops:
            moved = pltpu.roll(tile, turn, 0)
            moment = moment + factor * (pltpu.roll(moment, turn, 0) + float(hop) * moved)
            tile = tile + factor * moved
        return tile, moment

    def run(slot, backward, mode):
        band = slot + 1
        reach = slot < count - 1
        one = mode == "one"
        rate = decay_ref[groups[slot]]
        start = jnp.zeros((1, width), jnp.float32)
        start_moment = start
        side = int(backward)
        for apart in range(min(band, count - 1)):
            kept = has_source(apart, backward)
            span = float(apart * rows)
            factor = jnp.exp(-rate * span)
            end = far_ends[side, apart, end_row(slot, backward)]
            start = start + jnp.where(kept, factor * end, 0.0)
            if one:
                moment = far_ends[side, apart, slot] + span * end
                start_moment = start_moment + jnp.where(kept, factor * moment, 0.0)
        tail_row = jnp.exp(-rate * float(band * rows))
        tail = jnp.broadcast_to(tail_row, shape)
        far_tail = jnp.broadcast_to(tail_row * float(band * rows), shape)
        leap = jnp.broadcast_to(jnp.exp(-rate * ROWS), shape)
        wide = leap * float(ROWS)
        residue = jnp.broadcast_to(residue_ref[groups[slot]], shape)
        skip = jnp.broadcast_to(skip_ref[groups[slot]], shape)
        ahead = ROWS - depth if backward else depth + 1.0
        lead = jnp.exp(-rate * ahead)
        lead_moment = lead * ahead
        hops = []
        for hop in (1, 2, 4):
            inside = level < ROWS - hop if backward else level >= hop
            factor = jnp.where(inside, jnp.exp(-rate * hop), 0.0)
            hops.append((hop, ROWS - hop if backward else hop, factor))
        source, other_side = (cs, xs) if backward else (xs, cs)
        target = grads if backward else outs
        far_ref = far_c if backward else far_x
        edge = slice(0, 1) if backward else slice(ROWS - 1, ROWS)

        def turn(step, state):
            carry, moment_carry, s_skip, s_w, s_m = state
            if backward:
                step = steps - 1 - step
            at = pair_at(step)
            base = (step * PAIR).astype(jnp.float32)
            values = source[slot, at, :].astype(jnp.float32)
            if mode != "none":
                others = other_side[slot, at, :].astype(jnp.float32)
            if reach:
                far = far_ref[slot, at, :].astype(jnp.float32)
            made = [None, None]
            for half in (1, 0) if backward else (0, 1):
                part = slice(half * ROWS, (half + 1) * ROWS)
                fresh = values[part]
                if reach:
                    fresh = fresh - tail * far[part]
                if one:
                    local, local_moment = scan_both(fresh, -far_tail * far[part], hops)
                    moment = local_moment + lead * moment_carry + lead_moment * carry
                    moment_carry = (
                        leap * moment_carry
                        + wide * carry
                        + jnp.broadcast_to(local_moment[edge], shape)
                    )
                else:
                    local = scan(fresh, hops)
                truncated = local + lead * carry
                carry = leap * carry + jnp.broadcast_to(local[edge], shape)
                made[half] = skip * values[part] + residue * truncated
                if mode != "none":
                    w = others[part] * truncated
                    s_w = s_w + w
                if one:
                    s_m = s_m + others[part] * moment
                elif mode == "two":
                    s_m = s_m + (base + half * ROWS) * w
                if one or mode == "two" and not backward:
                    s_skip = s_skip + values[part] * others[part]
            target[slot, at, :] = jnp.concatenate(made, axis=0).astype(target.dtype)
            return carry, moment_carry, s_skip, s_w, s_m

        state = (
            zero + jnp.broadcast_to(start, shape),
            zero + jnp.broadcast_to(start_moment, shape),
            zero,
            zero,
            zero,
        )
        done = 0
        parts = parts_of(slot, backward) if reach else (PIECES,)
        for piece, part in enumerate(parts):
            if reach:
                pl.when(has_source(slot, backward))(
                    lambda: flow(slot, backward, piece).wait_recv()
                )
            span = (done * steps // PIECES, (done + part) * steps // PIECES)
            state = lax.fori_loop(*span, turn, state, unroll=UNROLL)
            done += part
        return state[2:]

    def close(slot, s_skip, s_w, moment):
        scale = -decay_ref[groups[slot]] * residue_ref[groups[slot]]
        sums[slot, 0] = jnp.sum(s_skip, axis=0, keepdims=True)
        sums[slot, 1] = jnp.sum(s_w, axis=0, keepdims=True)
        sums[slot, 2] = scale * jnp.sum(moment, axis=0, keepdims=True)

    def both_sides(slot):
        s_skip, s_w, s_tw = run(slot, False, "two")
        _, s_v, s_tv = run(slot, True, "two")
        offset = depth + (me * rows).astype(jnp.float32)
        close(slot, s_skip, s_w, (s_tw - s_tv) + offset * (s_w - s_v))

    both_sides(count - 1)
    for slot in middle[::-1]:
        both_sides(slot)

    @pl.when(has_source(0, False))
    def _():
        close(1, *run(1, True, "one"))
        close(0, *run(0, False, "one"))

    @pl.when(jnp.logical_not(has_source(0, False)))
    def _():
        close(0, *run(0, False, "one"))
        close(1, *run(1, True, "one"))

    for step in range(count - 1):
        share = sums[bands[lax.rem(me + step + 1, count)]]
        shares[step] = share
        share_copy(step).start()
    send(0, True, last_down, keeps_down)
    send(1, False, last_up, keeps_up)

    @pl.when(has_source(0, True))
    def _():
        run(1, False, "none")
        run(0, True, "none")

    @pl.when(jnp.logical_not(has_source(0, True)))
    def _():
        run(0, True, "none")
        run(1, False, "none")

    for step in range(count - 1):
        share_copy(step).wait()
    total = sums[bands[me]]
    for step in range(count - 1):
        total = total + got[step]
    own_ref[...] = total
    for group in range(count):
        order_ref[group] = bands[group]
    for backward in (False, True):
        for slot in range(count - 1):
            for piece in pieces_of(slot, backward):
                pl.when(has_source(slot, not backward))(
                    lambda: flow(slot, backward, piece).wait_send()
                )


def place_kernel(
    bands, outs, grads, own, out_hbm, grad_hbm, skip_hbm, residue_hbm, decay_hbm, sems, own_sems
):
    count, _, width = outs.shape
    copies = []
    for group in range(count):
        slot = bands[group]
        lanes = pl.ds(group * width, width)
        for side, (source, target) in enumerate(((outs, out_hbm), (grads, grad_hbm))):
            copies.append(
                pltpu.make_async_copy(
                    source.at[slot], target.at[:, lanes], sems.at[side, group]
                )
            )
    for row, target in enumerate((skip_hbm, residue_hbm, decay_hbm)):
        copies.append(pltpu.make_async_copy(own.at[row], target, own_sems.at[row]))
    for copy in copies:
        copy.start()
    for copy in copies:
        copy.wait()


def in_hbm(*arrays):
    return [pltpu.with_memory_space_constraint(one, pltpu.HBM) for one in arrays]


def place(bands, outs, grads, own):
    count, rows, width = outs.shape
    inside = pl.BlockSpec(memory_space=pltpu.VMEM)
    anywhere = pl.BlockSpec(memory_space=pl.ANY)
    whole = jax.ShapeDtypeStruct((rows, count * width), outs.dtype)
    small = jax.ShapeDtypeStruct((1, width), own.dtype)
    return pl.pallas_call(
        place_kernel,
        in_specs=[pl.BlockSpec(memory_space=pltpu.SMEM), inside, inside, inside],
        out_specs=[anywhere] * 5,
        out_shape=(whole, whole, small, small, small),
        scratch_shapes=[
            pltpu.SemaphoreType.DMA((2, count)),
            pltpu.SemaphoreType.DMA((3,)),
        ],
        compiler_params=pltpu.CompilerParams(vmem_limit_bytes=SCOPED),
        name="place",
    )(bands, outs, grads, own)


def banded(count, inputs, cotangent, residue, decay, skip_gain, band_blocks):
    rows, channels = inputs.shape
    width = channels // count
    first = rows * 2 // PIECES
    bands = band_blocks[0]
    anywhere = pl.BlockSpec(memory_space=pl.ANY)
    inside = pl.BlockSpec(memory_space=pltpu.VMEM)
    x_flows = pltpu.SemaphoreType.DMA((flow_count(count, False),))
    c_flows = pltpu.SemaphoreType.DMA((flow_count(count, True),))
    few = pltpu.SemaphoreType.DMA((count - 1,))
    kind = inputs.dtype
    packed = pltpu.VMEM((count, rows, width), kind)
    far = pltpu.VMEM((count - 1, rows, width), kind)
    row = pltpu.VMEM((count, 1, width), jnp.float32)
    ends = pltpu.SemaphoreType.DMA((2, count - 1))
    outs, grads, own, order = pl.pallas_call(
        functools.partial(banded_kernel, count),
        in_specs=[anywhere] * 6,
        out_specs=[inside, inside, inside, pl.BlockSpec(memory_space=pltpu.SMEM)],
        out_shape=(
            pltpu.VMEM((count, rows, width), kind),
            pltpu.VMEM((count, rows, width), kind),
            pltpu.VMEM((3, 1, width), jnp.float32),
            pltpu.SMEM((count,), jnp.int32),
        ),
        scratch_shapes=[
            pltpu.SMEM((count,), jnp.int32),
            row,
            row,
            row,
            pltpu.VMEM((count, first, width), kind),
            pltpu.VMEM((count, rows - first, width), kind),
            pltpu.VMEM((count, first, width), kind),
            pltpu.VMEM((count, rows - first, width), kind),
            packed,
            packed,
            far,
            far,
            pltpu.VMEM((2, count + 1, 1, width), jnp.float32),
            pltpu.VMEM((2, count - 1, count + 1, 1, width), jnp.float32),
            pltpu.VMEM((count, 3, 1, width), jnp.float32),
            pltpu.VMEM((count - 1, 3, 1, width), jnp.float32),
            pltpu.VMEM((count - 1, 3, 1, width), jnp.float32),
            pltpu.VMEM((ROWS, width), jnp.float32),
            pltpu.SemaphoreType.DMA((4,)),
            pltpu.SemaphoreType.DMA((4, count)),
            x_flows,
            x_flows,
            c_flows,
            c_flows,
            ends,
            ends,
            few,
            few,
        ],
        compiler_params=pltpu.CompilerParams(
            collective_id=0, has_side_effects=True, vmem_limit_bytes=SCOPED
        ),
        name="banded",
    )(
        *in_hbm(
            bands,
            inputs,
            cotangent,
            *(part.reshape(count, 1, width) for part in (residue, decay, skip_gain)),
        )
    )
    layer_out, input_grad, *sums = place(order, outs, grads, own)
    return (layer_out, input_grad, *(part.reshape(width) for part in sums))


def local_body(count, inputs, cotangent, residue, decay, skip_gain, band_blocks):
    rows, channels = inputs.shape
    groups = band_blocks.shape[1]
    fits = groups == count and count > 2 and rows % (PAIR * PIECES * UNROLL) == 0
    if fits and channels % (groups * LANES) == 0:
        return banded(count, inputs, cotangent, residue, decay, skip_gain, band_blocks)
    return body(inputs, cotangent, residue, decay, skip_gain, band_blocks)


def solution(mesh):
    placed = (P("ctx", "dp"), P("ctx", "dp"), P("dp"), P("dp"), P("dp"), P("dp", None))
    return jax.shard_map(
        functools.partial(local_body, mesh.shape["ctx"]),
        mesh=mesh,
        in_specs=placed,
        out_specs=(
            P("ctx", "dp"),
            P("ctx", "dp"),
            P(("dp", "ctx")),
            P(("dp", "ctx")),
            P(("dp", "ctx")),
        ),
        check_vma=False,
    )
```

```python
import functools
import jax
import jax.numpy as jnp
from jax import lax
from jax.experimental import pallas as pl
from jax.experimental.pallas import tpu as pltpu
from jax.sharding import PartitionSpec as P


def prefix(value, axis, join, neutral, backward):
    count, mine = (lax.axis_size(axis), lax.axis_index(axis))
    pieces = jax.tree.map(lambda part: lax.all_gather(part, axis), value)
    if backward:
        pieces = jax.tree.map(lambda part: part[::-1], pieces)
        mine = count - 1 - mine
    total = jax.tree.map(
        lambda part, zero: jnp.full_like(part, 0) + jnp.asarray(zero, part.dtype), value, neutral
    )

    def turn(position, total):
        longer = join(total, jax.tree.map(lambda part: part[position], pieces))
        return jax.tree.map(lambda new, old: jnp.where(position < mine, new, old), longer, total)

    return lax.fori_loop(0, count - 1, turn, total)


def compose(earlier_pair, later_pair):
    return (earlier_pair[0] * later_pair[0], earlier_pair[1] * later_pair[0] + later_pair[1])


def chain_step(earlier_pair, later_pair):
    return (earlier_pair[0] * later_pair[1] + later_pair[0], earlier_pair[1] * later_pair[1])


def local_scan(values, decay_rate, backward):
    factors = jnp.broadcast_to(jnp.exp(-decay_rate)[None, :], values.shape)
    return lax.associative_scan(compose, (factors, values), reverse=backward)[1]


def slot_groups(bands, ctx_rank, direction):
    group_count = bands.shape[0]
    slot_index = jnp.arange(group_count, dtype=jnp.int32)
    distance = (slot_index - ctx_rank) * direction
    matches = bands[None, :] + 1 == distance[:, None]
    return jnp.sum(jnp.where(matches, slot_index[None, :], 0), axis=1)


def pick(shaped, order):
    blocks = [
        lax.dynamic_index_in_dim(shaped, order[at], 1, keepdims=True)
        for at in range(order.shape[0])
    ]
    return jnp.concatenate(blocks, axis=1)


def outgoing(values, slot_group, group_count, group_width):
    shaped = values.reshape(values.shape[0], group_count, group_width)
    return pick(shaped, slot_group)


def incoming(received, source, in_range):
    picked = pick(received, source)
    picked = jnp.where(in_range[None, :, None], picked, jnp.zeros((), picked.dtype))
    return picked.reshape(picked.shape[0], -1)


def body(inputs, cotangent, residue, decay, skip_gain, band_blocks):
    values = inputs.astype(jnp.float32)
    upstream = cotangent.astype(jnp.float32)
    bands = band_blocks[0]
    block_rows, channels = values.shape
    group_count = bands.shape[0]
    group_width = channels // group_count
    ctx_rank = lax.axis_index("ctx")
    offsets = jnp.arange(block_rows, dtype=jnp.float32)[:, None]
    lengths = jnp.repeat(
        (bands + 1) * block_rows, group_width, total_repeat_length=channels
    ).astype(jnp.float32)
    band_tail = jnp.exp(-decay * lengths)[None, :]
    block_decay = jnp.exp(-decay * block_rows)
    lead_decay = jnp.exp(-decay[None, :] * (offsets + 1.0))
    trail_decay = jnp.exp(-decay[None, :] * (block_rows - offsets))
    zero_state = jnp.zeros_like(decay)
    unit_state = jnp.ones_like(decay)
    inside = local_scan(values, decay, False)
    before, _ = prefix(
        (inside[-1], block_decay), "ctx", chain_step, (zero_state, unit_state), False
    )
    carried = inside + lead_decay * before[None, :]
    send_fwd = slot_groups(bands, ctx_rank, 1)
    source_fwd = ctx_rank - bands - 1
    valid_fwd = source_fwd >= 0
    source_fwd = jnp.clip(source_fwd, 0, group_count - 1)
    inside_back = local_scan(upstream, decay, True)
    after, _ = prefix(
        (inside_back[0], block_decay), "ctx", chain_step, (zero_state, unit_state), True
    )
    back_carried = inside_back + trail_decay * after[None, :]
    send_bwd = slot_groups(bands, ctx_rank, -1)
    source_bwd = ctx_rank + bands + 1
    valid_bwd = source_bwd < group_count
    source_bwd = jnp.clip(source_bwd, 0, group_count - 1)
    received = lax.all_to_all(
        outgoing(carried, send_fwd, group_count, group_width),
        "ctx",
        split_axis=1,
        concat_axis=1,
        tiled=True,
    )
    far_state = incoming(received, source_fwd, valid_fwd)
    received_back = lax.all_to_all(
        outgoing(back_carried, send_bwd, group_count, group_width),
        "ctx",
        split_axis=1,
        concat_axis=1,
        tiled=True,
    )
    near_state = incoming(received_back, source_bwd, valid_bwd)
    truncated = carried - band_tail * far_state
    layer_out = (skip_gain[None, :] * values + residue[None, :] * truncated).astype(jnp.bfloat16)
    back_truncated = back_carried - band_tail * near_state
    input_grad = (skip_gain[None, :] * upstream + residue[None, :] * back_truncated).astype(
        jnp.bfloat16
    )
    position = ctx_rank.astype(jnp.float32) * block_rows + offsets
    weighted = upstream * truncated
    moment = jnp.sum(position * weighted, axis=0) - jnp.sum(
        position * values * back_truncated, axis=0
    )
    grad_terms = jnp.stack(
        [jnp.sum(values * upstream, axis=0), jnp.sum(weighted, axis=0), -decay * residue * moment]
    )
    share_width = channels // lax.axis_size("ctx")
    summed = lax.psum(grad_terms, "ctx")
    own_share = lax.dynamic_slice_in_dim(summed, ctx_rank * share_width, share_width, 1)
    return (layer_out, input_grad, own_share[0], own_share[1], own_share[2])


MESH = pl.DeviceIdType.MESH
LANES = 128
ROWS = 8
PAIR = 2 * ROWS
PIECES = 8
UNROLL = 4
SCOPED = 48_000_000


def greet(count, me):
    barrier = pltpu.get_barrier_semaphore()
    for step in range(1, count):
        pl.semaphore_signal(
            barrier,
            inc=1,
            device_id={"ctx": lax.rem(me + step, count)},
            device_id_type=MESH,
        )
    return lambda: pl.semaphore_wait(barrier, count - 1)


def parts_of(slot, backward):
    if backward:
        return {0: (4, 3, 1), 1: (2, 6)}.get(slot, (8,))
    return {0: (2, 6), 1: (7, 1)}.get(slot, (8,))


def kept_back(slot, backward):
    if backward:
        return 2 if slot == 0 else 0
    return 1 if slot == 1 else 0


def piece_rows(rows, slot, backward, piece):
    parts = parts_of(slot, backward)
    size = rows * parts[piece] // PIECES
    start = rows * sum(parts[:piece]) // PIECES
    return (rows - start - size if backward else start, size)


def piece_at(slot, backward, piece):
    return sum(len(parts_of(before, backward)) for before in range(slot)) + piece


def flow_count(count, backward):
    return sum(len(parts_of(slot, backward)) for slot in range(count - 1))


def end_row(slot, backward):
    return 0 if backward and slot == 0 else slot + 1


def pair_at(step):
    return pl.ds(pl.multiple_of(step * PAIR, PAIR), PAIR)


def banded_kernel(
    count,
    bands_hbm,
    x_hbm,
    c_hbm,
    residue_hbm,
    decay_hbm,
    skip_hbm,
    outs,
    grads,
    own_ref,
    order_ref,
    bands,
    residue_ref,
    decay_ref,
    skip_ref,
    x_first,
    x_rest,
    c_first,
    c_rest,
    xs,
    cs,
    far_x,
    far_c,
    ends,
    far_ends,
    sums,
    shares,
    got,
    blank,
    small_sem,
    load_sem,
    x_send,
    x_recv,
    c_send,
    c_recv,
    e_send,
    e_recv,
    s_send,
    s_recv,
):
    me = lax.axis_index("ctx")
    _, rows, width = xs.shape
    shape = (ROWS, width)
    first = x_first.shape[1]

    all_here = greet(count, me)

    small = [
        pltpu.make_async_copy(source, target, small_sem.at[at])
        for at, (source, target) in enumerate(
            (
                (bands_hbm, bands),
                (decay_hbm, decay_ref),
                (residue_hbm, residue_ref),
                (skip_hbm, skip_ref),
            )
        )
    ]
    small[0].start()
    chunks = (
        (c_hbm, rows - first, c_first, cs),
        (x_hbm, 0, x_first, xs),
        (c_hbm, 0, c_rest, cs),
        (x_hbm, first, x_rest, xs),
    )

    def load(chunk, group):
        source, start, target, _ = chunks[chunk]
        lanes = pl.ds(group * width, width)
        return pltpu.make_async_copy(
            source.at[pl.ds(start, target.shape[1]), lanes],
            target.at[group],
            load_sem.at[chunk, group],
        )

    for chunk in range(len(chunks)):
        for group in range(count):
            load(chunk, group).start()
    for copy in small[1:]:
        copy.start()
    small[0].wait()
    groups = []
    for slot in range(count):
        group = jnp.int32(0)
        for other in range(count):
            group = jnp.where(bands[other] == slot, other, group)
        groups.append(group)

    def pack(chunk):
        _, start, whole, packed = chunks[chunk]
        for group in range(count):
            load(chunk, group).wait()

        def turn(step, _):
            to = pl.ds(pl.multiple_of(start + step * PAIR, PAIR), PAIR)
            for slot in range(count):
                packed[slot, to, :] = whole[groups[slot], pair_at(step), :]
            return 0

        lax.fori_loop(0, whole.shape[1] // PAIR, turn, 0, unroll=UNROLL)

    def has_source(slot, backward):
        return me + slot + 1 < count if backward else me >= slot + 1

    def flow(slot, backward, piece):
        start, size = piece_rows(rows, slot, backward, piece)
        at = pl.ds(start, size)
        sem = piece_at(slot, backward, piece)
        source, target, sends, recvs = (
            (cs, far_c, c_send, c_recv) if backward else (xs, far_x, x_send, x_recv)
        )
        to = me + count - slot - 1 if backward else me + slot + 1
        return pltpu.make_async_remote_copy(
            src_ref=source.at[slot, at],
            dst_ref=target.at[slot, at],
            send_sem=sends.at[sem],
            recv_sem=recvs.at[sem],
            device_id={"ctx": lax.rem(to, count)},
            device_id_type=MESH,
        )

    def send(slot, backward, pieces, asked=True):
        sends_it = jnp.logical_and(has_source(slot, not backward), asked)
        for piece in pieces:
            pl.when(sends_it)(lambda: flow(slot, backward, piece).start())

    def pieces_of(slot, backward):
        return tuple(range(len(parts_of(slot, backward))))

    def end_copy(far, backward, passed_on=False):
        first_row = end_row(far - 1, backward)
        if far == 1 or far == 2 and backward:
            first_row = far - 1
        at = pl.ds(first_row, count + 1 - first_row)
        side = int(backward)
        away = 1 if passed_on else far
        to = me + count - away if backward else me + away
        source = far_ends.at[side, far - 2, at] if passed_on else ends.at[side, at]
        return pltpu.make_async_remote_copy(
            src_ref=source,
            dst_ref=far_ends.at[side, far - 1, at],
            send_sem=e_send.at[side, far - 1],
            recv_sem=e_recv.at[side, far - 1],
            device_id={"ctx": lax.rem(to, count)},
            device_id_type=MESH,
        )

    def sends_end(far, backward):
        outermost = me == far if backward else me + far == count - 1
        reached = has_source(far - 1, not backward)
        return reached if far == 1 else jnp.logical_and(reached, jnp.logical_not(outermost))

    def each_end(fars, may, act):
        for far in fars:
            for backward in (False, True):
                pl.when(may(far, backward))(lambda: act(far, backward))

    def passes_on(far, backward):
        return me == 1 if backward else me == count - 2

    def share_copy(step):
        to = lax.rem(me + step + 1, count)
        return pltpu.make_async_remote_copy(
            src_ref=shares.at[step],
            dst_ref=got.at[step],
            send_sem=s_send.at[step],
            recv_sem=s_recv.at[step],
            device_id={"ctx": to},
            device_id_type=MESH,
        )

    middle = tuple(range(2, count - 1))
    lowest, highest = me == 0, me == count - 1
    outer = jnp.logical_or(lowest, highest)
    keeps_up, keeps_down = me == 1, me == count - 2
    pack(0)
    all_here()
    send(1, True, (0,), jnp.logical_not(highest))
    pack(1)
    send(0, False, (0,))
    pack(2)
    pack(3)
    for copy in small[1:]:
        copy.wait()

    level = lax.broadcasted_iota(jnp.int32, shape, 0)
    depth = level.astype(jnp.float32)
    blank[...] = jnp.zeros(shape, jnp.float32)
    zero = blank[...]
    steps = rows // PAIR
    for slot in range(count):
        rate = decay_ref[groups[slot]]
        leap_pair = jnp.broadcast_to(jnp.exp(-rate * PAIR), shape)
        wide_pair = leap_pair * float(PAIR)
        weighted = {0: (0, 1), 1: (2, 3)}.get(slot, ())

        def turn(step, state):
            held, moments = state
            ahead = xs[slot, pair_at(step), :].astype(jnp.float32)
            back = cs[slot, pair_at(steps - 1 - step), :].astype(jnp.float32)
            parts = (ahead[:ROWS], ahead[ROWS:], back[:ROWS], back[ROWS:])
            moments = tuple(
                moment * leap_pair + held[at] * wide_pair
                for moment, at in zip(moments, weighted)
            )
            return (
                tuple(old * leap_pair + new for old, new in zip(held, parts)),
                moments,
            )

        held, moments = lax.fori_loop(
            0, steps, turn, ((zero,) * 4, (zero,) * len(weighted)), unroll=UNROLL
        )
        apart = (PAIR - 1 - depth, ROWS - 1 - depth, depth, ROWS + depth)
        factors = [jnp.exp(-rate * far) for far in apart]
        scaled = [one * factor for one, factor in zip(held, factors)]
        for side in range(2):
            both = scaled[2 * side] + scaled[2 * side + 1]
            ends[side, end_row(slot, side)] = jnp.sum(both, axis=0, keepdims=True)
        if weighted:
            both = zero
            for moment, at in zip(moments, weighted):
                both = both + factors[at] * moment + apart[at] * scaled[at]
            ends[slot, slot] = jnp.sum(both, axis=0, keepdims=True)
    every, others = range(1, count), range(2, count)
    each_end(every, sends_end, lambda *which: end_copy(*which).start())

    def receives(far, backward):
        return has_source(far - 1, backward)

    def wait_for_ends(fars):
        each_end(fars, receives, lambda *which: end_copy(*which).wait_recv())

    pl.when(outer)(lambda: wait_for_ends((1,)))
    last_up = pieces_of(1, False)[-kept_back(1, False) :]
    last_down = pieces_of(0, True)[-kept_back(0, True) :]
    send(1, True, (0,), highest)
    send(1, True, pieces_of(1, True)[1:])
    for slot in middle:
        send(slot, True, pieces_of(slot, True))
    send(0, True, pieces_of(0, True)[: -len(last_down)])
    send(0, True, last_down, jnp.logical_not(keeps_down))
    for slot in middle[::-1]:
        send(slot, False, pieces_of(slot, False))
    send(0, False, pieces_of(0, False)[1:])
    send(1, False, pieces_of(1, False)[: -len(last_up)])
    send(1, False, last_up, jnp.logical_not(keeps_up))

    for slot in range(count - 1):
        for backward, far in ((False, far_x), (True, far_c)):

            @pl.when(jnp.logical_not(has_source(slot, backward)))
            def _():
                def clear(step, _):
                    far[slot, pair_at(step), :] = jnp.zeros((PAIR, width), far.dtype)
                    return 0

                lax.fori_loop(0, steps, clear, 0, unroll=UNROLL)

    @pl.when(jnp.logical_not(outer))
    def _():
        wait_for_ends(every)
        each_end(others, passes_on, lambda *which: end_copy(*which, True).start())

    pl.when(outer)(lambda: wait_for_ends(others))
    each_end(every, sends_end, lambda *which: end_copy(*which).wait_send())

    def scan(tile, hops):
        for hop, turn, factor in hops:
            tile = tile + factor * pltpu.roll(tile, turn, 0)
        return tile

    def scan_both(tile, moment, hops):
        for hop, turn, factor in hops:
            moved = pltpu.roll(tile, turn, 0)
            moment = moment + factor * (pltpu.roll(moment, turn, 0) + float(hop) * moved)
            tile = tile + factor * moved
        return tile, moment

    def run(slot, backward, mode):
        band = slot + 1
        reach = slot < count - 1
        one = mode == "one"
        rate = decay_ref[groups[slot]]
        start = jnp.zeros((1, width), jnp.float32)
        start_moment = start
        side = int(backward)
        for apart in range(min(band, count - 1)):
            kept = has_source(apart, backward)
            span = float(apart * rows)
            factor = jnp.exp(-rate * span)
            end = far_ends[side, apart, end_row(slot, backward)]
            start = start + jnp.where(kept, factor * end, 0.0)
            if one:
                moment = far_ends[side, apart, slot] + span * end
                start_moment = start_moment + jnp.where(kept, factor * moment, 0.0)
        tail_row = jnp.exp(-rate * float(band * rows))
        tail = jnp.broadcast_to(tail_row, shape)
        far_tail = jnp.broadcast_to(tail_row * float(band * rows), shape)
        leap = jnp.broadcast_to(jnp.exp(-rate * ROWS), shape)
        wide = leap * float(ROWS)
        residue = jnp.broadcast_to(residue_ref[groups[slot]], shape)
        skip = jnp.broadcast_to(skip_ref[groups[slot]], shape)
        ahead = ROWS - depth if backward else depth + 1.0
        lead = jnp.exp(-rate * ahead)
        lead_moment = lead * ahead
        hops = []
        for hop in (1, 2, 4):
            inside = level < ROWS - hop if backward else level >= hop
            factor = jnp.where(inside, jnp.exp(-rate * hop), 0.0)
            hops.append((hop, ROWS - hop if backward else hop, factor))
        source, other_side = (cs, xs) if backward else (xs, cs)
        target = grads if backward else outs
        far_ref = far_c if backward else far_x
        edge = slice(0, 1) if backward else slice(ROWS - 1, ROWS)

        def turn(step, state):
            carry, moment_carry, s_skip, s_w, s_m = state
            if backward:
                step = steps - 1 - step
            at = pair_at(step)
            base = (step * PAIR).astype(jnp.float32)
            values = source[slot, at, :].astype(jnp.float32)
            if mode != "none":
                others = other_side[slot, at, :].astype(jnp.float32)
            if reach:
                far = far_ref[slot, at, :].astype(jnp.float32)
            made = [None, None]
            for half in (1, 0) if backward else (0, 1):
                part = slice(half * ROWS, (half + 1) * ROWS)
                fresh = values[part]
                if reach:
                    fresh = fresh - tail * far[part]
                if one:
                    local, local_moment = scan_both(fresh, -far_tail * far[part], hops)
                    moment = local_moment + lead * moment_carry + lead_moment * carry
                    moment_carry = (
                        leap * moment_carry
                        + wide * carry
                        + jnp.broadcast_to(local_moment[edge], shape)
                    )
                else:
                    local = scan(fresh, hops)
                truncated = local + lead * carry
                carry = leap * carry + jnp.broadcast_to(local[edge], shape)
                made[half] = skip * values[part] + residue * truncated
                if mode != "none":
                    w = others[part] * truncated
                    s_w = s_w + w
                if one:
                    s_m = s_m + others[part] * moment
                elif mode == "two":
                    s_m = s_m + (base + half * ROWS) * w
                if one or mode == "two" and not backward:
                    s_skip = s_skip + values[part] * others[part]
            target[slot, at, :] = jnp.concatenate(made, axis=0).astype(target.dtype)
            return carry, moment_carry, s_skip, s_w, s_m

        state = (
            zero + jnp.broadcast_to(start, shape),
            zero + jnp.broadcast_to(start_moment, shape),
            zero,
            zero,
            zero,
        )
        done = 0
        parts = parts_of(slot, backward) if reach else (PIECES,)
        for piece, part in enumerate(parts):
            if reach:
                pl.when(has_source(slot, backward))(
                    lambda: flow(slot, backward, piece).wait_recv()
                )
            span = (done * steps // PIECES, (done + part) * steps // PIECES)
            state = lax.fori_loop(*span, turn, state, unroll=UNROLL)
            done += part
        return state[2:]

    def close(slot, s_skip, s_w, moment):
        scale = -decay_ref[groups[slot]] * residue_ref[groups[slot]]
        sums[slot, 0] = jnp.sum(s_skip, axis=0, keepdims=True)
        sums[slot, 1] = jnp.sum(s_w, axis=0, keepdims=True)
        sums[slot, 2] = scale * jnp.sum(moment, axis=0, keepdims=True)

    def both_sides(slot):
        s_skip, s_w, s_tw = run(slot, False, "two")
        _, s_v, s_tv = run(slot, True, "two")
        offset = depth + (me * rows).astype(jnp.float32)
        close(slot, s_skip, s_w, (s_tw - s_tv) + offset * (s_w - s_v))

    both_sides(count - 1)
    for slot in middle[::-1]:
        both_sides(slot)

    @pl.when(has_source(0, False))
    def _():
        close(1, *run(1, True, "one"))
        close(0, *run(0, False, "one"))

    @pl.when(jnp.logical_not(has_source(0, False)))
    def _():
        close(0, *run(0, False, "one"))
        close(1, *run(1, True, "one"))

    for step in range(count - 1):
        share = sums[bands[lax.rem(me + step + 1, count)]]
        shares[step] = share
        share_copy(step).start()
    send(0, True, last_down, keeps_down)
    send(1, False, last_up, keeps_up)

    @pl.when(has_source(0, True))
    def _():
        run(1, False, "none")
        run(0, True, "none")

    @pl.when(jnp.logical_not(has_source(0, True)))
    def _():
        run(0, True, "none")
        run(1, False, "none")

    for step in range(count - 1):
        share_copy(step).wait()
    total = sums[bands[me]]
    for step in range(count - 1):
        total = total + got[step]
    own_ref[...] = total
    for group in range(count):
        order_ref[group] = bands[group]
    each_end(others, passes_on, lambda *which: end_copy(*which, True).wait_send())
    for backward in (False, True):
        for slot in range(count - 1):
            for piece in pieces_of(slot, backward):
                pl.when(has_source(slot, not backward))(
                    lambda: flow(slot, backward, piece).wait_send()
                )


def place_kernel(
    bands, outs, grads, own, out_hbm, grad_hbm, skip_hbm, residue_hbm, decay_hbm, sems, own_sems
):
    count, _, width = outs.shape
    copies = [
        pltpu.make_async_copy(own.at[row], target, own_sems.at[row])
        for row, target in enumerate((skip_hbm, residue_hbm, decay_hbm))
    ]
    for group in range(count):
        slot = bands[group]
        lanes = pl.ds(group * width, width)
        for side, (source, target) in enumerate(((outs, out_hbm), (grads, grad_hbm))):
            copies.append(
                pltpu.make_async_copy(
                    source.at[slot], target.at[:, lanes], sems.at[side, group]
                )
            )
    for copy in copies:
        copy.start()
    for copy in copies:
        copy.wait()


def in_hbm(*arrays):
    return [pltpu.with_memory_space_constraint(one, pltpu.HBM) for one in arrays]


def place(bands, outs, grads, own):
    count, rows, width = outs.shape
    inside = pl.BlockSpec(memory_space=pltpu.VMEM)
    anywhere = pl.BlockSpec(memory_space=pl.ANY)
    whole = jax.ShapeDtypeStruct((rows, count * width), outs.dtype)
    small = jax.ShapeDtypeStruct((1, width), own.dtype)
    return pl.pallas_call(
        place_kernel,
        in_specs=[pl.BlockSpec(memory_space=pltpu.SMEM), inside, inside, inside],
        out_specs=[anywhere] * 5,
        out_shape=(whole, whole, small, small, small),
        scratch_shapes=[
            pltpu.SemaphoreType.DMA((2, count)),
            pltpu.SemaphoreType.DMA((3,)),
        ],
        compiler_params=pltpu.CompilerParams(vmem_limit_bytes=SCOPED),
        name="place",
    )(bands, outs, grads, own)


def banded(count, inputs, cotangent, residue, decay, skip_gain, band_blocks):
    rows, channels = inputs.shape
    width = channels // count
    first = rows * 2 // PIECES
    bands = band_blocks[0]
    anywhere = pl.BlockSpec(memory_space=pl.ANY)
    inside = pl.BlockSpec(memory_space=pltpu.VMEM)
    x_flows = pltpu.SemaphoreType.DMA((flow_count(count, False),))
    c_flows = pltpu.SemaphoreType.DMA((flow_count(count, True),))
    few = pltpu.SemaphoreType.DMA((count - 1,))
    kind = inputs.dtype
    packed = pltpu.VMEM((count, rows, width), kind)
    far = pltpu.VMEM((count - 1, rows, width), kind)
    row = pltpu.VMEM((count, 1, width), jnp.float32)
    ends = pltpu.SemaphoreType.DMA((2, count - 1))
    outs, grads, own, order = pl.pallas_call(
        functools.partial(banded_kernel, count),
        in_specs=[anywhere] * 6,
        out_specs=[inside, inside, inside, pl.BlockSpec(memory_space=pltpu.SMEM)],
        out_shape=(
            pltpu.VMEM((count, rows, width), kind),
            pltpu.VMEM((count, rows, width), kind),
            pltpu.VMEM((3, 1, width), jnp.float32),
            pltpu.SMEM((count,), jnp.int32),
        ),
        scratch_shapes=[
            pltpu.SMEM((count,), jnp.int32),
            row,
            row,
            row,
            pltpu.VMEM((count, first, width), kind),
            pltpu.VMEM((count, rows - first, width), kind),
            pltpu.VMEM((count, first, width), kind),
            pltpu.VMEM((count, rows - first, width), kind),
            packed,
            packed,
            far,
            far,
            pltpu.VMEM((2, count + 1, 1, width), jnp.float32),
            pltpu.VMEM((2, count - 1, count + 1, 1, width), jnp.float32),
            pltpu.VMEM((count, 3, 1, width), jnp.float32),
            pltpu.VMEM((count - 1, 3, 1, width), jnp.float32),
            pltpu.VMEM((count - 1, 3, 1, width), jnp.float32),
            pltpu.VMEM((ROWS, width), jnp.float32),
            pltpu.SemaphoreType.DMA((4,)),
            pltpu.SemaphoreType.DMA((4, count)),
            x_flows,
            x_flows,
            c_flows,
            c_flows,
            ends,
            ends,
            few,
            few,
        ],
        compiler_params=pltpu.CompilerParams(
            collective_id=0, has_side_effects=True, vmem_limit_bytes=SCOPED
        ),
        name="banded",
    )(
        *in_hbm(
            bands,
            inputs,
            cotangent,
            *(part.reshape(count, 1, width) for part in (residue, decay, skip_gain)),
        )
    )
    layer_out, input_grad, *sums = place(order, outs, grads, own)
    return (layer_out, input_grad, *(part.reshape(width) for part in sums))


def local_body(count, inputs, cotangent, residue, decay, skip_gain, band_blocks):
    rows, channels = inputs.shape
    groups = band_blocks.shape[1]
    fits = groups == count and count > 2 and rows % (PAIR * PIECES * UNROLL) == 0
    if fits and channels % (groups * LANES) == 0:
        return banded(count, inputs, cotangent, residue, decay, skip_gain, band_blocks)
    return body(inputs, cotangent, residue, decay, skip_gain, band_blocks)


def solution(mesh):
    placed = (P("ctx", "dp"), P("ctx", "dp"), P("dp"), P("dp"), P("dp"), P("dp", None))
    return jax.shard_map(
        functools.partial(local_body, mesh.shape["ctx"]),
        mesh=mesh,
        in_specs=placed,
        out_specs=(
            P("ctx", "dp"),
            P("ctx", "dp"),
            P(("dp", "ctx")),
            P(("dp", "ctx")),
            P(("dp", "ctx")),
        ),
        check_vma=False,
    )
```

```python
import functools
import jax
import jax.numpy as jnp
from jax import lax
from jax.experimental import pallas as pl
from jax.experimental.pallas import tpu as pltpu
from jax.sharding import PartitionSpec as P


def prefix(value, axis, join, neutral, backward):
    count, mine = (lax.axis_size(axis), lax.axis_index(axis))
    pieces = jax.tree.map(lambda part: lax.all_gather(part, axis), value)
    if backward:
        pieces = jax.tree.map(lambda part: part[::-1], pieces)
        mine = count - 1 - mine
    total = jax.tree.map(
        lambda part, zero: jnp.full_like(part, 0) + jnp.asarray(zero, part.dtype), value, neutral
    )

    def turn(position, total):
        longer = join(total, jax.tree.map(lambda part: part[position], pieces))
        return jax.tree.map(lambda new, old: jnp.where(position < mine, new, old), longer, total)

    return lax.fori_loop(0, count - 1, turn, total)


def compose(earlier_pair, later_pair):
    return (earlier_pair[0] * later_pair[0], earlier_pair[1] * later_pair[0] + later_pair[1])


def chain_step(earlier_pair, later_pair):
    return (earlier_pair[0] * later_pair[1] + later_pair[0], earlier_pair[1] * later_pair[1])


def local_scan(values, decay_rate, backward):
    factors = jnp.broadcast_to(jnp.exp(-decay_rate)[None, :], values.shape)
    return lax.associative_scan(compose, (factors, values), reverse=backward)[1]


def slot_groups(bands, ctx_rank, direction):
    group_count = bands.shape[0]
    slot_index = jnp.arange(group_count, dtype=jnp.int32)
    distance = (slot_index - ctx_rank) * direction
    matches = bands[None, :] + 1 == distance[:, None]
    return jnp.sum(jnp.where(matches, slot_index[None, :], 0), axis=1)


def pick(shaped, order):
    blocks = [
        lax.dynamic_index_in_dim(shaped, order[at], 1, keepdims=True)
        for at in range(order.shape[0])
    ]
    return jnp.concatenate(blocks, axis=1)


def outgoing(values, slot_group, group_count, group_width):
    shaped = values.reshape(values.shape[0], group_count, group_width)
    return pick(shaped, slot_group)


def incoming(received, source, in_range):
    picked = pick(received, source)
    picked = jnp.where(in_range[None, :, None], picked, jnp.zeros((), picked.dtype))
    return picked.reshape(picked.shape[0], -1)


def body(inputs, cotangent, residue, decay, skip_gain, band_blocks):
    values = inputs.astype(jnp.float32)
    upstream = cotangent.astype(jnp.float32)
    bands = band_blocks[0]
    block_rows, channels = values.shape
    group_count = bands.shape[0]
    group_width = channels // group_count
    ctx_rank = lax.axis_index("ctx")
    offsets = jnp.arange(block_rows, dtype=jnp.float32)[:, None]
    lengths = jnp.repeat(
        (bands + 1) * block_rows, group_width, total_repeat_length=channels
    ).astype(jnp.float32)
    band_tail = jnp.exp(-decay * lengths)[None, :]
    block_decay = jnp.exp(-decay * block_rows)
    lead_decay = jnp.exp(-decay[None, :] * (offsets + 1.0))
    trail_decay = jnp.exp(-decay[None, :] * (block_rows - offsets))
    zero_state = jnp.zeros_like(decay)
    unit_state = jnp.ones_like(decay)
    inside = local_scan(values, decay, False)
    before, _ = prefix(
        (inside[-1], block_decay), "ctx", chain_step, (zero_state, unit_state), False
    )
    carried = inside + lead_decay * before[None, :]
    send_fwd = slot_groups(bands, ctx_rank, 1)
    source_fwd = ctx_rank - bands - 1
    valid_fwd = source_fwd >= 0
    source_fwd = jnp.clip(source_fwd, 0, group_count - 1)
    inside_back = local_scan(upstream, decay, True)
    after, _ = prefix(
        (inside_back[0], block_decay), "ctx", chain_step, (zero_state, unit_state), True
    )
    back_carried = inside_back + trail_decay * after[None, :]
    send_bwd = slot_groups(bands, ctx_rank, -1)
    source_bwd = ctx_rank + bands + 1
    valid_bwd = source_bwd < group_count
    source_bwd = jnp.clip(source_bwd, 0, group_count - 1)
    received = lax.all_to_all(
        outgoing(carried, send_fwd, group_count, group_width),
        "ctx",
        split_axis=1,
        concat_axis=1,
        tiled=True,
    )
    far_state = incoming(received, source_fwd, valid_fwd)
    received_back = lax.all_to_all(
        outgoing(back_carried, send_bwd, group_count, group_width),
        "ctx",
        split_axis=1,
        concat_axis=1,
        tiled=True,
    )
    near_state = incoming(received_back, source_bwd, valid_bwd)
    truncated = carried - band_tail * far_state
    layer_out = (skip_gain[None, :] * values + residue[None, :] * truncated).astype(jnp.bfloat16)
    back_truncated = back_carried - band_tail * near_state
    input_grad = (skip_gain[None, :] * upstream + residue[None, :] * back_truncated).astype(
        jnp.bfloat16
    )
    position = ctx_rank.astype(jnp.float32) * block_rows + offsets
    weighted = upstream * truncated
    moment = jnp.sum(position * weighted, axis=0) - jnp.sum(
        position * values * back_truncated, axis=0
    )
    grad_terms = jnp.stack(
        [jnp.sum(values * upstream, axis=0), jnp.sum(weighted, axis=0), -decay * residue * moment]
    )
    share_width = channels // lax.axis_size("ctx")
    summed = lax.psum(grad_terms, "ctx")
    own_share = lax.dynamic_slice_in_dim(summed, ctx_rank * share_width, share_width, 1)
    return (layer_out, input_grad, own_share[0], own_share[1], own_share[2])


MESH = pl.DeviceIdType.MESH
LANES = 128
ROWS = 8
PAIR = 2 * ROWS
PIECES = 8
UNROLL = 4
SCOPED = 48_000_000


def greet(count, me):
    barrier = pltpu.get_barrier_semaphore()
    for step in range(1, count):
        pl.semaphore_signal(
            barrier,
            inc=1,
            device_id={"ctx": lax.rem(me + step, count)},
            device_id_type=MESH,
        )
    return lambda: pl.semaphore_wait(barrier, count - 1)


def parts_of(slot, backward):
    if backward:
        return {0: (4, 3, 1), 1: (2, 6)}.get(slot, (8,))
    return {0: (2, 6), 1: (7, 1)}.get(slot, (8,))


def kept_back(slot, backward):
    if backward:
        return 2 if slot == 0 else 0
    return 1 if slot == 1 else 0


def piece_rows(rows, slot, backward, piece):
    parts = parts_of(slot, backward)
    size = rows * parts[piece] // PIECES
    start = rows * sum(parts[:piece]) // PIECES
    return (rows - start - size if backward else start, size)


def piece_at(slot, backward, piece):
    return sum(len(parts_of(before, backward)) for before in range(slot)) + piece


def flow_count(count, backward):
    return sum(len(parts_of(slot, backward)) for slot in range(count - 1))


def end_row(slot, backward):
    return 0 if backward and slot == 0 else slot + 1


def pair_at(step):
    return pl.ds(pl.multiple_of(step * PAIR, PAIR), PAIR)


def banded_kernel(
    count,
    bands_hbm,
    x_hbm,
    c_hbm,
    residue_hbm,
    decay_hbm,
    skip_hbm,
    outs,
    grads,
    own_ref,
    order_ref,
    bands,
    residue_ref,
    decay_ref,
    skip_ref,
    x_first,
    x_rest,
    c_first,
    c_rest,
    xs,
    cs,
    far_x,
    far_c,
    ends,
    far_ends,
    sums,
    shares,
    got,
    blank,
    small_sem,
    load_sem,
    x_send,
    x_recv,
    c_send,
    c_recv,
    e_send,
    e_recv,
    s_send,
    s_recv,
):
    me = lax.axis_index("ctx")
    _, rows, width = xs.shape
    shape = (ROWS, width)
    first = x_first.shape[1]

    all_here = greet(count, me)

    small = [
        pltpu.make_async_copy(source, target, small_sem.at[at])
        for at, (source, target) in enumerate(
            (
                (bands_hbm, bands),
                (decay_hbm, decay_ref),
                (residue_hbm, residue_ref),
                (skip_hbm, skip_ref),
            )
        )
    ]
    small[0].start()
    chunks = (
        (c_hbm, rows - first, c_first, cs),
        (x_hbm, 0, x_first, xs),
        (c_hbm, 0, c_rest, cs),
        (x_hbm, first, x_rest, xs),
    )

    def load(chunk, group):
        source, start, target, _ = chunks[chunk]
        lanes = pl.ds(group * width, width)
        return pltpu.make_async_copy(
            source.at[pl.ds(start, target.shape[1]), lanes],
            target.at[group],
            load_sem.at[chunk, group],
        )

    for chunk in range(len(chunks)):
        for group in range(count):
            load(chunk, group).start()
    for copy in small[1:]:
        copy.start()
    small[0].wait()
    groups = []
    for slot in range(count):
        group = jnp.int32(0)
        for other in range(count):
            group = jnp.where(bands[other] == slot, other, group)
        groups.append(group)

    def pack(chunk):
        _, start, whole, packed = chunks[chunk]
        for group in range(count):
            load(chunk, group).wait()

        def turn(step, _):
            to = pl.ds(pl.multiple_of(start + step * PAIR, PAIR), PAIR)
            for slot in range(count):
                packed[slot, to, :] = whole[groups[slot], pair_at(step), :]
            return 0

        lax.fori_loop(0, whole.shape[1] // PAIR, turn, 0, unroll=UNROLL)

    def has_source(slot, backward):
        return me + slot + 1 < count if backward else me >= slot + 1

    def flow(slot, backward, piece):
        start, size = piece_rows(rows, slot, backward, piece)
        at = pl.ds(start, size)
        sem = piece_at(slot, backward, piece)
        source, target, sends, recvs = (
            (cs, far_c, c_send, c_recv) if backward else (xs, far_x, x_send, x_recv)
        )
        to = me + count - slot - 1 if backward else me + slot + 1
        return pltpu.make_async_remote_copy(
            src_ref=source.at[slot, at],
            dst_ref=target.at[slot, at],
            send_sem=sends.at[sem],
            recv_sem=recvs.at[sem],
            device_id={"ctx": lax.rem(to, count)},
            device_id_type=MESH,
        )

    def send(slot, backward, pieces, asked=True):
        sends_it = jnp.logical_and(has_source(slot, not backward), asked)
        for piece in pieces:
            pl.when(sends_it)(lambda: flow(slot, backward, piece).start())

    def pieces_of(slot, backward):
        return tuple(range(len(parts_of(slot, backward))))

    def end_copy(far, backward, passed_on=False):
        first_row = end_row(far - 1, backward)
        if far == 1 or far == 2 and backward:
            first_row = far - 1
        at = pl.ds(first_row, count + 1 - first_row)
        side = int(backward)
        away = 1 if passed_on else far
        to = me + count - away if backward else me + away
        source = far_ends.at[side, far - 2, at] if passed_on else ends.at[side, at]
        return pltpu.make_async_remote_copy(
            src_ref=source,
            dst_ref=far_ends.at[side, far - 1, at],
            send_sem=e_send.at[side, far - 1],
            recv_sem=e_recv.at[side, far - 1],
            device_id={"ctx": lax.rem(to, count)},
            device_id_type=MESH,
        )

    def sends_end(far, backward):
        outermost = me == far if backward else me + far == count - 1
        reached = has_source(far - 1, not backward)
        return reached if far == 1 else jnp.logical_and(reached, jnp.logical_not(outermost))

    def each_end(fars, may, act):
        for far in fars:
            for backward in (False, True):
                pl.when(may(far, backward))(lambda: act(far, backward))

    def passes_on(far, backward):
        return me == 1 if backward else me == count - 2

    def share_copy(step):
        to = lax.rem(me + step + 1, count)
        return pltpu.make_async_remote_copy(
            src_ref=shares.at[step],
            dst_ref=got.at[step],
            send_sem=s_send.at[step],
            recv_sem=s_recv.at[step],
            device_id={"ctx": to},
            device_id_type=MESH,
        )

    middle = tuple(range(2, count - 1))
    lowest, highest = me == 0, me == count - 1
    outer = jnp.logical_or(lowest, highest)
    keeps_up, keeps_down = me == 1, me == count - 2
    pack(0)
    all_here()
    send(1, True, (0,), jnp.logical_not(highest))
    pack(1)
    send(0, False, (0,))
    pack(2)
    pack(3)
    for copy in small[1:]:
        copy.wait()

    level = lax.broadcasted_iota(jnp.int32, shape, 0)
    depth = level.astype(jnp.float32)
    blank[...] = jnp.zeros(shape, jnp.float32)
    zero = blank[...]
    steps = rows // PAIR
    for slot in range(count):
        rate = decay_ref[groups[slot]]
        leap_pair = jnp.broadcast_to(jnp.exp(-rate * PAIR), shape)
        wide_pair = leap_pair * float(PAIR)
        weighted = {0: (0, 1), 1: (2, 3)}.get(slot, ())

        def turn(step, state):
            held, moments = state
            ahead = xs[slot, pair_at(step), :].astype(jnp.float32)
            back = cs[slot, pair_at(steps - 1 - step), :].astype(jnp.float32)
            parts = (ahead[:ROWS], ahead[ROWS:], back[:ROWS], back[ROWS:])
            moments = tuple(
                moment * leap_pair + held[at] * wide_pair
                for moment, at in zip(moments, weighted)
            )
            return (
                tuple(old * leap_pair + new for old, new in zip(held, parts)),
                moments,
            )

        held, moments = lax.fori_loop(
            0, steps, turn, ((zero,) * 4, (zero,) * len(weighted)), unroll=UNROLL
        )
        apart = (PAIR - 1 - depth, ROWS - 1 - depth, depth, ROWS + depth)
        factors = [jnp.exp(-rate * far) for far in apart]
        scaled = [one * factor for one, factor in zip(held, factors)]
        for side in range(2):
            both = scaled[2 * side] + scaled[2 * side + 1]
            ends[side, end_row(slot, side)] = jnp.sum(both, axis=0, keepdims=True)
        if weighted:
            both = zero
            for moment, at in zip(moments, weighted):
                both = both + factors[at] * moment + apart[at] * scaled[at]
            ends[slot, slot] = jnp.sum(both, axis=0, keepdims=True)
    every, others = range(1, count), range(2, count)
    each_end(every, sends_end, lambda *which: end_copy(*which).start())

    def receives(far, backward):
        return has_source(far - 1, backward)

    def wait_for_ends(fars):
        each_end(fars, receives, lambda *which: end_copy(*which).wait_recv())

    pl.when(outer)(lambda: wait_for_ends((1,)))
    last_up = pieces_of(1, False)[-kept_back(1, False) :]
    last_down = pieces_of(0, True)[-kept_back(0, True) :]
    send(1, True, (0,), highest)
    send(1, True, pieces_of(1, True)[1:])
    for slot in middle:
        send(slot, True, pieces_of(slot, True))
    send(0, True, pieces_of(0, True)[: -len(last_down)])
    send(0, True, last_down, jnp.logical_not(keeps_down))
    for slot in middle[::-1]:
        send(slot, False, pieces_of(slot, False))
    send(0, False, pieces_of(0, False)[1:])
    send(1, False, pieces_of(1, False)[: -len(last_up)])
    send(1, False, last_up, jnp.logical_not(keeps_up))

    for slot in range(count - 1):
        for backward, far in ((False, far_x), (True, far_c)):

            @pl.when(jnp.logical_not(has_source(slot, backward)))
            def _():
                def clear(step, _):
                    far[slot, pair_at(step), :] = jnp.zeros((PAIR, width), far.dtype)
                    return 0

                lax.fori_loop(0, steps, clear, 0, unroll=UNROLL)

    @pl.when(jnp.logical_not(outer))
    def _():
        wait_for_ends(every)
        each_end(others, passes_on, lambda *which: end_copy(*which, True).start())

    pl.when(outer)(lambda: wait_for_ends(others))
    each_end(every, sends_end, lambda *which: end_copy(*which).wait_send())

    def scan(tile, hops):
        for hop, turn, factor in hops:
            tile = tile + factor * pltpu.roll(tile, turn, 0)
        return tile

    def scan_both(tile, moment, hops):
        for hop, turn, factor in hops:
            moved = pltpu.roll(tile, turn, 0)
            moment = moment + factor * (pltpu.roll(moment, turn, 0) + float(hop) * moved)
            tile = tile + factor * moved
        return tile, moment

    def run(slot, backward, mode):
        band = slot + 1
        reach = slot < count - 1
        one = mode == "one"
        rate = decay_ref[groups[slot]]
        start = jnp.zeros((1, width), jnp.float32)
        start_moment = start
        side = int(backward)
        for apart in range(min(band, count - 1)):
            kept = has_source(apart, backward)
            span = float(apart * rows)
            factor = jnp.exp(-rate * span)
            end = far_ends[side, apart, end_row(slot, backward)]
            start = start + jnp.where(kept, factor * end, 0.0)
            if one:
                moment = far_ends[side, apart, slot] + span * end
                start_moment = start_moment + jnp.where(kept, factor * moment, 0.0)
        tail_row = jnp.exp(-rate * float(band * rows))
        tail = jnp.broadcast_to(tail_row, shape)
        far_tail = jnp.broadcast_to(tail_row * float(band * rows), shape)
        leap = jnp.broadcast_to(jnp.exp(-rate * ROWS), shape)
        wide = leap * float(ROWS)
        residue = jnp.broadcast_to(residue_ref[groups[slot]], shape)
        skip = jnp.broadcast_to(skip_ref[groups[slot]], shape)
        ahead = ROWS - depth if backward else depth + 1.0
        lead = jnp.exp(-rate * ahead)
        lead_moment = lead * ahead
        hops = []
        for hop in (1, 2, 4):
            inside = level < ROWS - hop if backward else level >= hop
            factor = jnp.where(inside, jnp.exp(-rate * hop), 0.0)
            hops.append((hop, ROWS - hop if backward else hop, factor))
        source, other_side = (cs, xs) if backward else (xs, cs)
        target = grads if backward else outs
        far_ref = far_c if backward else far_x
        edge = slice(0, 1) if backward else slice(ROWS - 1, ROWS)

        def turn(step, state):
            carry, moment_carry, s_skip, s_w, s_m = state
            if backward:
                step = steps - 1 - step
            at = pair_at(step)
            base = (step * PAIR).astype(jnp.float32)
            values = source[slot, at, :].astype(jnp.float32)
            if mode != "none":
                others = other_side[slot, at, :].astype(jnp.float32)
            if reach:
                far = far_ref[slot, at, :].astype(jnp.float32)
            made = [None, None]
            for half in (1, 0) if backward else (0, 1):
                part = slice(half * ROWS, (half + 1) * ROWS)
                fresh = values[part]
                if reach:
                    fresh = fresh - tail * far[part]
                if one:
                    local, local_moment = scan_both(fresh, -far_tail * far[part], hops)
                    moment = local_moment + lead * moment_carry + lead_moment * carry
                    moment_carry = (
                        leap * moment_carry
                        + wide * carry
                        + jnp.broadcast_to(local_moment[edge], shape)
                    )
                else:
                    local = scan(fresh, hops)
                truncated = local + lead * carry
                carry = leap * carry + jnp.broadcast_to(local[edge], shape)
                made[half] = skip * values[part] + residue * truncated
                if mode != "none":
                    w = others[part] * truncated
                    s_w = s_w + w
                if one:
                    s_m = s_m + others[part] * moment
                elif mode == "two":
                    s_m = s_m + (base + half * ROWS) * w
                if one or mode == "two" and not backward:
                    s_skip = s_skip + values[part] * others[part]
            target[slot, at, :] = jnp.concatenate(made, axis=0).astype(target.dtype)
            return carry, moment_carry, s_skip, s_w, s_m

        state = (
            zero + jnp.broadcast_to(start, shape),
            zero + jnp.broadcast_to(start_moment, shape),
            zero,
            zero,
            zero,
        )
        done = 0
        parts = parts_of(slot, backward) if reach else (PIECES,)
        for piece, part in enumerate(parts):
            if reach:
                pl.when(has_source(slot, backward))(
                    lambda: flow(slot, backward, piece).wait_recv()
                )
            span = (done * steps // PIECES, (done + part) * steps // PIECES)
            state = lax.fori_loop(*span, turn, state, unroll=UNROLL)
            done += part
        return state[2:]

    def close(slot, s_skip, s_w, moment):
        scale = -decay_ref[groups[slot]] * residue_ref[groups[slot]]
        sums[slot, 0] = jnp.sum(s_skip, axis=0, keepdims=True)
        sums[slot, 1] = jnp.sum(s_w, axis=0, keepdims=True)
        sums[slot, 2] = scale * jnp.sum(moment, axis=0, keepdims=True)

    def both_sides(slot):
        s_skip, s_w, s_tw = run(slot, False, "two")
        _, s_v, s_tv = run(slot, True, "two")
        offset = depth + (me * rows).astype(jnp.float32)
        close(slot, s_skip, s_w, (s_tw - s_tv) + offset * (s_w - s_v))

    both_sides(count - 1)
    for slot in middle[::-1]:
        both_sides(slot)

    @pl.when(has_source(0, False))
    def _():
        close(1, *run(1, True, "one"))
        close(0, *run(0, False, "one"))

    @pl.when(jnp.logical_not(has_source(0, False)))
    def _():
        close(0, *run(0, False, "one"))
        close(1, *run(1, True, "one"))

    for step in range(count - 1):
        share = sums[bands[lax.rem(me + step + 1, count)]]
        shares[step] = share
        share_copy(step).start()
    send(0, True, last_down, keeps_down)
    send(1, False, last_up, keeps_up)

    def wait_sent(which):
        for backward in (False, True):
            for slot in range(count - 1):
                for piece in pieces_of(slot, backward) if which(slot, backward) else ():
                    pl.when(has_source(slot, not backward))(
                        lambda: flow(slot, backward, piece).wait_send()
                    )

    def early_sent():
        each_end(others, passes_on, lambda *which: end_copy(*which, True).wait_send())
        wait_sent(lambda slot, backward: slot != int(not backward))

    @pl.when(has_source(0, True))
    def _():
        run(1, False, "none")
        early_sent()
        run(0, True, "none")

    @pl.when(jnp.logical_not(has_source(0, True)))
    def _():
        run(0, True, "none")
        early_sent()
        run(1, False, "none")

    for step in range(count - 1):
        share_copy(step).wait()
    total = sums[bands[me]]
    for step in range(count - 1):
        total = total + got[step]
    own_ref[...] = total
    for group in range(count):
        order_ref[group] = bands[group]
    wait_sent(lambda slot, backward: slot == int(not backward))


def place_kernel(
    bands, outs, grads, own, out_hbm, grad_hbm, skip_hbm, residue_hbm, decay_hbm, sems, own_sems
):
    count, _, width = outs.shape
    copies = [
        pltpu.make_async_copy(own.at[row], target, own_sems.at[row])
        for row, target in enumerate((skip_hbm, residue_hbm, decay_hbm))
    ]
    for group in range(count):
        slot = bands[group]
        lanes = pl.ds(group * width, width)
        for side, (source, target) in enumerate(((outs, out_hbm), (grads, grad_hbm))):
            copies.append(
                pltpu.make_async_copy(
                    source.at[slot], target.at[:, lanes], sems.at[side, group]
                )
            )
    for copy in copies:
        copy.start()
    for copy in copies:
        copy.wait()


def in_hbm(*arrays):
    return [pltpu.with_memory_space_constraint(one, pltpu.HBM) for one in arrays]


def place(bands, outs, grads, own):
    count, rows, width = outs.shape
    inside = pl.BlockSpec(memory_space=pltpu.VMEM)
    anywhere = pl.BlockSpec(memory_space=pl.ANY)
    whole = jax.ShapeDtypeStruct((rows, count * width), outs.dtype)
    small = jax.ShapeDtypeStruct((1, width), own.dtype)
    return pl.pallas_call(
        place_kernel,
        in_specs=[pl.BlockSpec(memory_space=pltpu.SMEM), inside, inside, inside],
        out_specs=[anywhere] * 5,
        out_shape=(whole, whole, small, small, small),
        scratch_shapes=[
            pltpu.SemaphoreType.DMA((2, count)),
            pltpu.SemaphoreType.DMA((3,)),
        ],
        compiler_params=pltpu.CompilerParams(vmem_limit_bytes=SCOPED),
        name="place",
    )(bands, outs, grads, own)


def banded(count, inputs, cotangent, residue, decay, skip_gain, band_blocks):
    rows, channels = inputs.shape
    width = channels // count
    first = rows * 2 // PIECES
    bands = band_blocks[0]
    anywhere = pl.BlockSpec(memory_space=pl.ANY)
    inside = pl.BlockSpec(memory_space=pltpu.VMEM)
    x_flows = pltpu.SemaphoreType.DMA((flow_count(count, False),))
    c_flows = pltpu.SemaphoreType.DMA((flow_count(count, True),))
    few = pltpu.SemaphoreType.DMA((count - 1,))
    kind = inputs.dtype
    packed = pltpu.VMEM((count, rows, width), kind)
    far = pltpu.VMEM((count - 1, rows, width), kind)
    row = pltpu.VMEM((count, 1, width), jnp.float32)
    ends = pltpu.SemaphoreType.DMA((2, count - 1))
    outs, grads, own, order = pl.pallas_call(
        functools.partial(banded_kernel, count),
        in_specs=[anywhere] * 6,
        out_specs=[inside, inside, inside, pl.BlockSpec(memory_space=pltpu.SMEM)],
        out_shape=(
            pltpu.VMEM((count, rows, width), kind),
            pltpu.VMEM((count, rows, width), kind),
            pltpu.VMEM((3, 1, width), jnp.float32),
            pltpu.SMEM((count,), jnp.int32),
        ),
        scratch_shapes=[
            pltpu.SMEM((count,), jnp.int32),
            row,
            row,
            row,
            pltpu.VMEM((count, first, width), kind),
            pltpu.VMEM((count, rows - first, width), kind),
            pltpu.VMEM((count, first, width), kind),
            pltpu.VMEM((count, rows - first, width), kind),
            packed,
            packed,
            far,
            far,
            pltpu.VMEM((2, count + 1, 1, width), jnp.float32),
            pltpu.VMEM((2, count - 1, count + 1, 1, width), jnp.float32),
            pltpu.VMEM((count, 3, 1, width), jnp.float32),
            pltpu.VMEM((count - 1, 3, 1, width), jnp.float32),
            pltpu.VMEM((count - 1, 3, 1, width), jnp.float32),
            pltpu.VMEM((ROWS, width), jnp.float32),
            pltpu.SemaphoreType.DMA((4,)),
            pltpu.SemaphoreType.DMA((4, count)),
            x_flows,
            x_flows,
            c_flows,
            c_flows,
            ends,
            ends,
            few,
            few,
        ],
        compiler_params=pltpu.CompilerParams(
            collective_id=0, has_side_effects=True, vmem_limit_bytes=SCOPED
        ),
        name="banded",
    )(
        *in_hbm(
            bands,
            inputs,
            cotangent,
            *(part.reshape(count, 1, width) for part in (residue, decay, skip_gain)),
        )
    )
    layer_out, input_grad, *sums = place(order, outs, grads, own)
    return (layer_out, input_grad, *(part.reshape(width) for part in sums))


def local_body(count, inputs, cotangent, residue, decay, skip_gain, band_blocks):
    rows, channels = inputs.shape
    groups = band_blocks.shape[1]
    fits = groups == count and count > 2 and rows % (PAIR * PIECES * UNROLL) == 0
    if fits and channels % (groups * LANES) == 0:
        return banded(count, inputs, cotangent, residue, decay, skip_gain, band_blocks)
    return body(inputs, cotangent, residue, decay, skip_gain, band_blocks)


def solution(mesh):
    placed = (P("ctx", "dp"), P("ctx", "dp"), P("dp"), P("dp"), P("dp"), P("dp", None))
    return jax.shard_map(
        functools.partial(local_body, mesh.shape["ctx"]),
        mesh=mesh,
        in_specs=placed,
        out_specs=(
            P("ctx", "dp"),
            P("ctx", "dp"),
            P(("dp", "ctx")),
            P(("dp", "ctx")),
            P(("dp", "ctx")),
        ),
        check_vma=False,
    )
```

```python
import functools
import jax
import jax.numpy as jnp
from jax import lax
from jax.experimental import pallas as pl
from jax.experimental.pallas import tpu as pltpu
from jax.sharding import PartitionSpec as P


def prefix(value, axis, join, neutral, backward):
    count, mine = (lax.axis_size(axis), lax.axis_index(axis))
    pieces = jax.tree.map(lambda part: lax.all_gather(part, axis), value)
    if backward:
        pieces = jax.tree.map(lambda part: part[::-1], pieces)
        mine = count - 1 - mine
    total = jax.tree.map(
        lambda part, zero: jnp.full_like(part, 0) + jnp.asarray(zero, part.dtype), value, neutral
    )

    def turn(position, total):
        longer = join(total, jax.tree.map(lambda part: part[position], pieces))
        return jax.tree.map(lambda new, old: jnp.where(position < mine, new, old), longer, total)

    return lax.fori_loop(0, count - 1, turn, total)


def compose(earlier_pair, later_pair):
    return (earlier_pair[0] * later_pair[0], earlier_pair[1] * later_pair[0] + later_pair[1])


def chain_step(earlier_pair, later_pair):
    return (earlier_pair[0] * later_pair[1] + later_pair[0], earlier_pair[1] * later_pair[1])


def local_scan(values, decay_rate, backward):
    factors = jnp.broadcast_to(jnp.exp(-decay_rate)[None, :], values.shape)
    return lax.associative_scan(compose, (factors, values), reverse=backward)[1]


def slot_groups(bands, ctx_rank, direction):
    group_count = bands.shape[0]
    slot_index = jnp.arange(group_count, dtype=jnp.int32)
    distance = (slot_index - ctx_rank) * direction
    matches = bands[None, :] + 1 == distance[:, None]
    return jnp.sum(jnp.where(matches, slot_index[None, :], 0), axis=1)


def pick(shaped, order):
    blocks = [
        lax.dynamic_index_in_dim(shaped, order[at], 1, keepdims=True)
        for at in range(order.shape[0])
    ]
    return jnp.concatenate(blocks, axis=1)


def outgoing(values, slot_group, group_count, group_width):
    shaped = values.reshape(values.shape[0], group_count, group_width)
    return pick(shaped, slot_group)


def incoming(received, source, in_range):
    picked = pick(received, source)
    picked = jnp.where(in_range[None, :, None], picked, jnp.zeros((), picked.dtype))
    return picked.reshape(picked.shape[0], -1)


def body(inputs, cotangent, residue, decay, skip_gain, band_blocks):
    values = inputs.astype(jnp.float32)
    upstream = cotangent.astype(jnp.float32)
    bands = band_blocks[0]
    block_rows, channels = values.shape
    group_count = bands.shape[0]
    group_width = channels // group_count
    ctx_rank = lax.axis_index("ctx")
    offsets = jnp.arange(block_rows, dtype=jnp.float32)[:, None]
    lengths = jnp.repeat(
        (bands + 1) * block_rows, group_width, total_repeat_length=channels
    ).astype(jnp.float32)
    band_tail = jnp.exp(-decay * lengths)[None, :]
    block_decay = jnp.exp(-decay * block_rows)
    lead_decay = jnp.exp(-decay[None, :] * (offsets + 1.0))
    trail_decay = jnp.exp(-decay[None, :] * (block_rows - offsets))
    zero_state = jnp.zeros_like(decay)
    unit_state = jnp.ones_like(decay)
    inside = local_scan(values, decay, False)
    before, _ = prefix(
        (inside[-1], block_decay), "ctx", chain_step, (zero_state, unit_state), False
    )
    carried = inside + lead_decay * before[None, :]
    send_fwd = slot_groups(bands, ctx_rank, 1)
    source_fwd = ctx_rank - bands - 1
    valid_fwd = source_fwd >= 0
    source_fwd = jnp.clip(source_fwd, 0, group_count - 1)
    inside_back = local_scan(upstream, decay, True)
    after, _ = prefix(
        (inside_back[0], block_decay), "ctx", chain_step, (zero_state, unit_state), True
    )
    back_carried = inside_back + trail_decay * after[None, :]
    send_bwd = slot_groups(bands, ctx_rank, -1)
    source_bwd = ctx_rank + bands + 1
    valid_bwd = source_bwd < group_count
    source_bwd = jnp.clip(source_bwd, 0, group_count - 1)
    received = lax.all_to_all(
        outgoing(carried, send_fwd, group_count, group_width),
        "ctx",
        split_axis=1,
        concat_axis=1,
        tiled=True,
    )
    far_state = incoming(received, source_fwd, valid_fwd)
    received_back = lax.all_to_all(
        outgoing(back_carried, send_bwd, group_count, group_width),
        "ctx",
        split_axis=1,
        concat_axis=1,
        tiled=True,
    )
    near_state = incoming(received_back, source_bwd, valid_bwd)
    truncated = carried - band_tail * far_state
    layer_out = (skip_gain[None, :] * values + residue[None, :] * truncated).astype(jnp.bfloat16)
    back_truncated = back_carried - band_tail * near_state
    input_grad = (skip_gain[None, :] * upstream + residue[None, :] * back_truncated).astype(
        jnp.bfloat16
    )
    position = ctx_rank.astype(jnp.float32) * block_rows + offsets
    weighted = upstream * truncated
    moment = jnp.sum(position * weighted, axis=0) - jnp.sum(
        position * values * back_truncated, axis=0
    )
    grad_terms = jnp.stack(
        [jnp.sum(values * upstream, axis=0), jnp.sum(weighted, axis=0), -decay * residue * moment]
    )
    share_width = channels // lax.axis_size("ctx")
    summed = lax.psum(grad_terms, "ctx")
    own_share = lax.dynamic_slice_in_dim(summed, ctx_rank * share_width, share_width, 1)
    return (layer_out, input_grad, own_share[0], own_share[1], own_share[2])


MESH = pl.DeviceIdType.MESH
LANES = 128
ROWS = 8
PAIR = 2 * ROWS
PIECES = 16
UNROLL = 4
SCOPED = 48_000_000


def greet(count, me):
    barrier = pltpu.get_barrier_semaphore()
    for step in range(1, count):
        pl.semaphore_signal(
            barrier,
            inc=1,
            device_id={"ctx": lax.rem(me + step, count)},
            device_id_type=MESH,
        )
    return lambda: pl.semaphore_wait(barrier, count - 1)


def parts_of(slot, backward):
    if backward:
        return {0: (8, 7, 1), 1: (4, 12)}.get(slot, (PIECES,))
    return {0: (4, 12), 1: (14, 2)}.get(slot, (PIECES,))


def kept_back(slot, backward):
    if backward:
        return 2 if slot == 0 else 0
    return 1 if slot == 1 else 0


def piece_rows(rows, slot, backward, piece):
    parts = parts_of(slot, backward)
    size = rows * parts[piece] // PIECES
    start = rows * sum(parts[:piece]) // PIECES
    return (rows - start - size if backward else start, size)


def piece_at(slot, backward, piece):
    return sum(len(parts_of(before, backward)) for before in range(slot)) + piece


def flow_count(count, backward):
    return sum(len(parts_of(slot, backward)) for slot in range(count - 1))


def end_row(slot, backward):
    return 0 if backward and slot == 0 else slot + 1


def pair_at(step):
    return pl.ds(pl.multiple_of(step * PAIR, PAIR), PAIR)


def banded_kernel(
    count,
    bands_hbm,
    x_hbm,
    c_hbm,
    residue_hbm,
    decay_hbm,
    skip_hbm,
    outs,
    grads,
    own_ref,
    order_ref,
    bands,
    residue_ref,
    decay_ref,
    skip_ref,
    x_first,
    x_rest,
    c_first,
    c_rest,
    xs,
    cs,
    far_x,
    far_c,
    ends,
    far_ends,
    sums,
    shares,
    got,
    blank,
    small_sem,
    load_sem,
    x_send,
    x_recv,
    c_send,
    c_recv,
    e_send,
    e_recv,
    s_send,
    s_recv,
):
    me = lax.axis_index("ctx")
    _, rows, width = xs.shape
    shape = (ROWS, width)
    first = x_first.shape[1]

    all_here = greet(count, me)

    small = [
        pltpu.make_async_copy(source, target, small_sem.at[at])
        for at, (source, target) in enumerate(
            (
                (bands_hbm, bands),
                (decay_hbm, decay_ref),
                (residue_hbm, residue_ref),
                (skip_hbm, skip_ref),
            )
        )
    ]
    small[0].start()
    chunks = (
        (c_hbm, rows - first, c_first, cs),
        (x_hbm, 0, x_first, xs),
        (c_hbm, 0, c_rest, cs),
        (x_hbm, first, x_rest, xs),
    )

    def load(chunk, group):
        source, start, target, _ = chunks[chunk]
        lanes = pl.ds(group * width, width)
        return pltpu.make_async_copy(
            source.at[pl.ds(start, target.shape[1]), lanes],
            target.at[group],
            load_sem.at[chunk, group],
        )

    for chunk in range(len(chunks)):
        for group in range(count):
            load(chunk, group).start()
    for copy in small[1:]:
        copy.start()
    small[0].wait()
    groups = []
    for slot in range(count):
        group = jnp.int32(0)
        for other in range(count):
            group = jnp.where(bands[other] == slot, other, group)
        groups.append(group)

    def pack(chunk):
        _, start, whole, packed = chunks[chunk]
        for group in range(count):
            load(chunk, group).wait()

        def turn(step, _):
            to = pl.ds(pl.multiple_of(start + step * PAIR, PAIR), PAIR)
            for slot in range(count):
                packed[slot, to, :] = whole[groups[slot], pair_at(step), :]
            return 0

        lax.fori_loop(0, whole.shape[1] // PAIR, turn, 0, unroll=UNROLL)

    def has_source(slot, backward):
        return me + slot + 1 < count if backward else me >= slot + 1

    def flow(slot, backward, piece):
        start, size = piece_rows(rows, slot, backward, piece)
        at = pl.ds(start, size)
        sem = piece_at(slot, backward, piece)
        source, target, sends, recvs = (
            (cs, far_c, c_send, c_recv) if backward else (xs, far_x, x_send, x_recv)
        )
        to = me + count - slot - 1 if backward else me + slot + 1
        return pltpu.make_async_remote_copy(
            src_ref=source.at[slot, at],
            dst_ref=target.at[slot, at],
            send_sem=sends.at[sem],
            recv_sem=recvs.at[sem],
            device_id={"ctx": lax.rem(to, count)},
            device_id_type=MESH,
        )

    def send(slot, backward, pieces, asked=True):
        sends_it = jnp.logical_and(has_source(slot, not backward), asked)
        for piece in pieces:
            pl.when(sends_it)(lambda: flow(slot, backward, piece).start())

    def pieces_of(slot, backward):
        return tuple(range(len(parts_of(slot, backward))))

    def end_copy(far, backward, passed_on=False):
        first_row = end_row(far - 1, backward)
        if far == 1 or far == 2 and backward:
            first_row = far - 1
        at = pl.ds(first_row, count + 1 - first_row)
        side = int(backward)
        away = 1 if passed_on else far
        to = me + count - away if backward else me + away
        source = far_ends.at[side, far - 2, at] if passed_on else ends.at[side, at]
        return pltpu.make_async_remote_copy(
            src_ref=source,
            dst_ref=far_ends.at[side, far - 1, at],
            send_sem=e_send.at[side, far - 1],
            recv_sem=e_recv.at[side, far - 1],
            device_id={"ctx": lax.rem(to, count)},
            device_id_type=MESH,
        )

    def sends_end(far, backward):
        outermost = me == far if backward else me + far == count - 1
        reached = has_source(far - 1, not backward)
        return reached if far == 1 else jnp.logical_and(reached, jnp.logical_not(outermost))

    def each_end(fars, may, act):
        for far in fars:
            for backward in (False, True):
                pl.when(may(far, backward))(lambda: act(far, backward))

    def passes_on(far, backward):
        return me == 1 if backward else me == count - 2

    def share_copy(step):
        to = lax.rem(me + step + 1, count)
        return pltpu.make_async_remote_copy(
            src_ref=shares.at[step],
            dst_ref=got.at[step],
            send_sem=s_send.at[step],
            recv_sem=s_recv.at[step],
            device_id={"ctx": to},
            device_id_type=MESH,
        )

    middle = tuple(range(2, count - 1))
    lowest, highest = me == 0, me == count - 1
    outer = jnp.logical_or(lowest, highest)
    keeps_up, keeps_down = me == 1, me == count - 2
    pack(0)
    all_here()
    send(1, True, (0,), jnp.logical_not(highest))
    pack(1)
    send(0, False, (0,))
    pack(2)
    pack(3)
    for copy in small[1:]:
        copy.wait()

    level = lax.broadcasted_iota(jnp.int32, shape, 0)
    depth = level.astype(jnp.float32)
    blank[...] = jnp.zeros(shape, jnp.float32)
    zero = blank[...]
    steps = rows // PAIR
    for slot in range(count):
        rate = decay_ref[groups[slot]]
        leap_pair = jnp.broadcast_to(jnp.exp(-rate * PAIR), shape)
        wide_pair = leap_pair * float(PAIR)
        weighted = {0: (0, 1), 1: (2, 3)}.get(slot, ())

        def turn(step, state):
            held, moments = state
            ahead = xs[slot, pair_at(step), :].astype(jnp.float32)
            back = cs[slot, pair_at(steps - 1 - step), :].astype(jnp.float32)
            parts = (ahead[:ROWS], ahead[ROWS:], back[:ROWS], back[ROWS:])
            moments = tuple(
                moment * leap_pair + held[at] * wide_pair
                for moment, at in zip(moments, weighted)
            )
            return (
                tuple(old * leap_pair + new for old, new in zip(held, parts)),
                moments,
            )

        held, moments = lax.fori_loop(
            0, steps, turn, ((zero,) * 4, (zero,) * len(weighted)), unroll=UNROLL
        )
        apart = (PAIR - 1 - depth, ROWS - 1 - depth, depth, ROWS + depth)
        factors = [jnp.exp(-rate * far) for far in apart]
        scaled = [one * factor for one, factor in zip(held, factors)]
        for side in range(2):
            both = scaled[2 * side] + scaled[2 * side + 1]
            ends[side, end_row(slot, side)] = jnp.sum(both, axis=0, keepdims=True)
        if weighted:
            both = zero
            for moment, at in zip(moments, weighted):
                both = both + factors[at] * moment + apart[at] * scaled[at]
            ends[slot, slot] = jnp.sum(both, axis=0, keepdims=True)
    every, others = range(1, count), range(2, count)
    each_end(every, sends_end, lambda *which: end_copy(*which).start())

    def receives(far, backward):
        return has_source(far - 1, backward)

    def wait_for_ends(fars):
        each_end(fars, receives, lambda *which: end_copy(*which).wait_recv())

    pl.when(outer)(lambda: wait_for_ends((1,)))
    last_up = pieces_of(1, False)[-kept_back(1, False) :]
    last_down = pieces_of(0, True)[-kept_back(0, True) :]
    send(1, True, (0,), highest)
    send(1, True, pieces_of(1, True)[1:])
    for slot in middle:
        send(slot, True, pieces_of(slot, True))
    send(0, True, pieces_of(0, True)[: -len(last_down)])
    send(0, True, last_down, jnp.logical_not(keeps_down))
    for slot in middle[::-1]:
        send(slot, False, pieces_of(slot, False))
    send(0, False, pieces_of(0, False)[1:])
    send(1, False, pieces_of(1, False)[: -len(last_up)])
    send(1, False, last_up, jnp.logical_not(keeps_up))

    for slot in range(count - 1):
        for backward, far in ((False, far_x), (True, far_c)):

            @pl.when(jnp.logical_not(has_source(slot, backward)))
            def _():
                def clear(step, _):
                    far[slot, pair_at(step), :] = jnp.zeros((PAIR, width), far.dtype)
                    return 0

                lax.fori_loop(0, steps, clear, 0, unroll=UNROLL)

    @pl.when(jnp.logical_not(outer))
    def _():
        wait_for_ends(every)
        each_end(others, passes_on, lambda *which: end_copy(*which, True).start())

    pl.when(outer)(lambda: wait_for_ends(others))
    each_end(every, sends_end, lambda *which: end_copy(*which).wait_send())

    def scan(tile, hops):
        for hop, turn, factor in hops:
            tile = tile + factor * pltpu.roll(tile, turn, 0)
        return tile

    def scan_both(tile, moment, hops):
        for hop, turn, factor in hops:
            moved = pltpu.roll(tile, turn, 0)
            moment = moment + factor * (pltpu.roll(moment, turn, 0) + float(hop) * moved)
            tile = tile + factor * moved
        return tile, moment

    def run(slot, backward, mode):
        band = slot + 1
        reach = slot < count - 1
        one = mode == "one"
        rate = decay_ref[groups[slot]]
        start = jnp.zeros((1, width), jnp.float32)
        start_moment = start
        side = int(backward)
        for apart in range(min(band, count - 1)):
            kept = has_source(apart, backward)
            span = float(apart * rows)
            factor = jnp.exp(-rate * span)
            end = far_ends[side, apart, end_row(slot, backward)]
            start = start + jnp.where(kept, factor * end, 0.0)
            if one:
                moment = far_ends[side, apart, slot] + span * end
                start_moment = start_moment + jnp.where(kept, factor * moment, 0.0)
        tail_row = jnp.exp(-rate * float(band * rows))
        tail = jnp.broadcast_to(tail_row, shape)
        far_tail = jnp.broadcast_to(tail_row * float(band * rows), shape)
        leap = jnp.broadcast_to(jnp.exp(-rate * ROWS), shape)
        wide = leap * float(ROWS)
        residue = jnp.broadcast_to(residue_ref[groups[slot]], shape)
        skip = jnp.broadcast_to(skip_ref[groups[slot]], shape)
        ahead = ROWS - depth if backward else depth + 1.0
        lead = jnp.exp(-rate * ahead)
        lead_moment = lead * ahead
        hops = []
        for hop in (1, 2, 4):
            inside = level < ROWS - hop if backward else level >= hop
            factor = jnp.where(inside, jnp.exp(-rate * hop), 0.0)
            hops.append((hop, ROWS - hop if backward else hop, factor))
        source, other_side = (cs, xs) if backward else (xs, cs)
        target = grads if backward else outs
        far_ref = far_c if backward else far_x
        edge = slice(0, 1) if backward else slice(ROWS - 1, ROWS)

        def turn(step, state):
            carry, moment_carry, s_skip, s_w, s_m = state
            if backward:
                step = steps - 1 - step
            at = pair_at(step)
            base = (step * PAIR).astype(jnp.float32)
            values = source[slot, at, :].astype(jnp.float32)
            if mode != "none":
                others = other_side[slot, at, :].astype(jnp.float32)
            if reach:
                far = far_ref[slot, at, :].astype(jnp.float32)
            made = [None, None]
            for half in (1, 0) if backward else (0, 1):
                part = slice(half * ROWS, (half + 1) * ROWS)
                fresh = values[part]
                if reach:
                    fresh = fresh - tail * far[part]
                if one:
                    local, local_moment = scan_both(fresh, -far_tail * far[part], hops)
                    moment = local_moment + lead * moment_carry + lead_moment * carry
                    moment_carry = (
                        leap * moment_carry
                        + wide * carry
                        + jnp.broadcast_to(local_moment[edge], shape)
                    )
                else:
                    local = scan(fresh, hops)
                truncated = local + lead * carry
                carry = leap * carry + jnp.broadcast_to(local[edge], shape)
                made[half] = skip * values[part] + residue * truncated
                if mode != "none":
                    w = others[part] * truncated
                    s_w = s_w + w
                if one:
                    s_m = s_m + others[part] * moment
                elif mode == "two":
                    s_m = s_m + (base + half * ROWS) * w
                if one or mode == "two" and not backward:
                    s_skip = s_skip + values[part] * others[part]
            target[slot, at, :] = jnp.concatenate(made, axis=0).astype(target.dtype)
            return carry, moment_carry, s_skip, s_w, s_m

        state = (
            zero + jnp.broadcast_to(start, shape),
            zero + jnp.broadcast_to(start_moment, shape),
            zero,
            zero,
            zero,
        )
        done = 0
        parts = parts_of(slot, backward) if reach else (PIECES,)
        for piece, part in enumerate(parts):
            if reach:
                pl.when(has_source(slot, backward))(
                    lambda: flow(slot, backward, piece).wait_recv()
                )
            span = (done * steps // PIECES, (done + part) * steps // PIECES)
            state = lax.fori_loop(*span, turn, state, unroll=UNROLL)
            done += part
        return state[2:]

    def close(slot, s_skip, s_w, moment):
        scale = -decay_ref[groups[slot]] * residue_ref[groups[slot]]
        sums[slot, 0] = jnp.sum(s_skip, axis=0, keepdims=True)
        sums[slot, 1] = jnp.sum(s_w, axis=0, keepdims=True)
        sums[slot, 2] = scale * jnp.sum(moment, axis=0, keepdims=True)

    def both_sides(slot):
        s_skip, s_w, s_tw = run(slot, False, "two")
        _, s_v, s_tv = run(slot, True, "two")
        offset = depth + (me * rows).astype(jnp.float32)
        close(slot, s_skip, s_w, (s_tw - s_tv) + offset * (s_w - s_v))

    both_sides(count - 1)
    for slot in middle[::-1]:
        both_sides(slot)

    @pl.when(has_source(0, False))
    def _():
        close(1, *run(1, True, "one"))
        close(0, *run(0, False, "one"))

    @pl.when(jnp.logical_not(has_source(0, False)))
    def _():
        close(0, *run(0, False, "one"))
        close(1, *run(1, True, "one"))

    for step in range(count - 1):
        share = sums[bands[lax.rem(me + step + 1, count)]]
        shares[step] = share
        share_copy(step).start()
    send(0, True, last_down, keeps_down)
    send(1, False, last_up, keeps_up)

    def wait_sent(which):
        for backward in (False, True):
            for slot in range(count - 1):
                for piece in pieces_of(slot, backward) if which(slot, backward) else ():
                    pl.when(has_source(slot, not backward))(
                        lambda: flow(slot, backward, piece).wait_send()
                    )

    def early_sent():
        each_end(others, passes_on, lambda *which: end_copy(*which, True).wait_send())
        wait_sent(lambda slot, backward: slot != int(not backward))

    @pl.when(has_source(0, True))
    def _():
        run(1, False, "none")
        early_sent()
        run(0, True, "none")

    @pl.when(jnp.logical_not(has_source(0, True)))
    def _():
        run(0, True, "none")
        early_sent()
        run(1, False, "none")

    for step in range(count - 1):
        share_copy(step).wait()
    total = sums[bands[me]]
    for step in range(count - 1):
        total = total + got[step]
    own_ref[...] = total
    for group in range(count):
        order_ref[group] = bands[group]
    wait_sent(lambda slot, backward: slot == int(not backward))


def place_kernel(
    bands, outs, grads, own, out_hbm, grad_hbm, skip_hbm, residue_hbm, decay_hbm, sems, own_sems
):
    count, _, width = outs.shape
    copies = [
        pltpu.make_async_copy(own.at[row], target, own_sems.at[row])
        for row, target in enumerate((skip_hbm, residue_hbm, decay_hbm))
    ]
    for group in range(count):
        slot = bands[group]
        lanes = pl.ds(group * width, width)
        for side, (source, target) in enumerate(((outs, out_hbm), (grads, grad_hbm))):
            copies.append(
                pltpu.make_async_copy(
                    source.at[slot], target.at[:, lanes], sems.at[side, group]
                )
            )
    for copy in copies:
        copy.start()
    for copy in copies:
        copy.wait()


def in_hbm(*arrays):
    return [pltpu.with_memory_space_constraint(one, pltpu.HBM) for one in arrays]


def place(bands, outs, grads, own):
    count, rows, width = outs.shape
    inside = pl.BlockSpec(memory_space=pltpu.VMEM)
    anywhere = pl.BlockSpec(memory_space=pl.ANY)
    whole = jax.ShapeDtypeStruct((rows, count * width), outs.dtype)
    small = jax.ShapeDtypeStruct((1, width), own.dtype)
    return pl.pallas_call(
        place_kernel,
        in_specs=[pl.BlockSpec(memory_space=pltpu.SMEM), inside, inside, inside],
        out_specs=[anywhere] * 5,
        out_shape=(whole, whole, small, small, small),
        scratch_shapes=[
            pltpu.SemaphoreType.DMA((2, count)),
            pltpu.SemaphoreType.DMA((3,)),
        ],
        compiler_params=pltpu.CompilerParams(vmem_limit_bytes=SCOPED),
        name="place",
    )(bands, outs, grads, own)


def banded(count, inputs, cotangent, residue, decay, skip_gain, band_blocks):
    rows, channels = inputs.shape
    width = channels // count
    first = rows * 4 // PIECES
    bands = band_blocks[0]
    anywhere = pl.BlockSpec(memory_space=pl.ANY)
    inside = pl.BlockSpec(memory_space=pltpu.VMEM)
    x_flows = pltpu.SemaphoreType.DMA((flow_count(count, False),))
    c_flows = pltpu.SemaphoreType.DMA((flow_count(count, True),))
    few = pltpu.SemaphoreType.DMA((count - 1,))
    kind = inputs.dtype
    packed = pltpu.VMEM((count, rows, width), kind)
    far = pltpu.VMEM((count - 1, rows, width), kind)
    row = pltpu.VMEM((count, 1, width), jnp.float32)
    ends = pltpu.SemaphoreType.DMA((2, count - 1))
    outs, grads, own, order = pl.pallas_call(
        functools.partial(banded_kernel, count),
        in_specs=[anywhere] * 6,
        out_specs=[inside, inside, inside, pl.BlockSpec(memory_space=pltpu.SMEM)],
        out_shape=(
            pltpu.VMEM((count, rows, width), kind),
            pltpu.VMEM((count, rows, width), kind),
            pltpu.VMEM((3, 1, width), jnp.float32),
            pltpu.SMEM((count,), jnp.int32),
        ),
        scratch_shapes=[
            pltpu.SMEM((count,), jnp.int32),
            row,
            row,
            row,
            pltpu.VMEM((count, first, width), kind),
            pltpu.VMEM((count, rows - first, width), kind),
            pltpu.VMEM((count, first, width), kind),
            pltpu.VMEM((count, rows - first, width), kind),
            packed,
            packed,
            far,
            far,
            pltpu.VMEM((2, count + 1, 1, width), jnp.float32),
            pltpu.VMEM((2, count - 1, count + 1, 1, width), jnp.float32),
            pltpu.VMEM((count, 3, 1, width), jnp.float32),
            pltpu.VMEM((count - 1, 3, 1, width), jnp.float32),
            pltpu.VMEM((count - 1, 3, 1, width), jnp.float32),
            pltpu.VMEM((ROWS, width), jnp.float32),
            pltpu.SemaphoreType.DMA((4,)),
            pltpu.SemaphoreType.DMA((4, count)),
            x_flows,
            x_flows,
            c_flows,
            c_flows,
            ends,
            ends,
            few,
            few,
        ],
        compiler_params=pltpu.CompilerParams(
            collective_id=0, has_side_effects=True, vmem_limit_bytes=SCOPED
        ),
        name="banded",
    )(
        *in_hbm(
            bands,
            inputs,
            cotangent,
            *(part.reshape(count, 1, width) for part in (residue, decay, skip_gain)),
        )
    )
    layer_out, input_grad, *sums = place(order, outs, grads, own)
    return (layer_out, input_grad, *(part.reshape(width) for part in sums))


def local_body(count, inputs, cotangent, residue, decay, skip_gain, band_blocks):
    rows, channels = inputs.shape
    groups = band_blocks.shape[1]
    fits = groups == count and count > 2 and rows % (PAIR * PIECES * UNROLL) == 0
    if fits and channels % (groups * LANES) == 0:
        return banded(count, inputs, cotangent, residue, decay, skip_gain, band_blocks)
    return body(inputs, cotangent, residue, decay, skip_gain, band_blocks)


def solution(mesh):
    placed = (P("ctx", "dp"), P("ctx", "dp"), P("dp"), P("dp"), P("dp"), P("dp", None))
    return jax.shard_map(
        functools.partial(local_body, mesh.shape["ctx"]),
        mesh=mesh,
        in_specs=placed,
        out_specs=(
            P("ctx", "dp"),
            P("ctx", "dp"),
            P(("dp", "ctx")),
            P(("dp", "ctx")),
            P(("dp", "ctx")),
        ),
        check_vma=False,
    )
```

```python
import functools
import jax
import jax.numpy as jnp
from jax import lax
from jax.experimental import pallas as pl
from jax.experimental.pallas import tpu as pltpu
from jax.sharding import PartitionSpec as P


def prefix(value, axis, join, neutral, backward):
    count, mine = (lax.axis_size(axis), lax.axis_index(axis))
    pieces = jax.tree.map(lambda part: lax.all_gather(part, axis), value)
    if backward:
        pieces = jax.tree.map(lambda part: part[::-1], pieces)
        mine = count - 1 - mine
    total = jax.tree.map(
        lambda part, zero: jnp.full_like(part, 0) + jnp.asarray(zero, part.dtype), value, neutral
    )

    def turn(position, total):
        longer = join(total, jax.tree.map(lambda part: part[position], pieces))
        return jax.tree.map(lambda new, old: jnp.where(position < mine, new, old), longer, total)

    return lax.fori_loop(0, count - 1, turn, total)


def compose(earlier_pair, later_pair):
    return (earlier_pair[0] * later_pair[0], earlier_pair[1] * later_pair[0] + later_pair[1])


def chain_step(earlier_pair, later_pair):
    return (earlier_pair[0] * later_pair[1] + later_pair[0], earlier_pair[1] * later_pair[1])


def local_scan(values, decay_rate, backward):
    factors = jnp.broadcast_to(jnp.exp(-decay_rate)[None, :], values.shape)
    return lax.associative_scan(compose, (factors, values), reverse=backward)[1]


def slot_groups(bands, ctx_rank, direction):
    group_count = bands.shape[0]
    slot_index = jnp.arange(group_count, dtype=jnp.int32)
    distance = (slot_index - ctx_rank) * direction
    matches = bands[None, :] + 1 == distance[:, None]
    return jnp.sum(jnp.where(matches, slot_index[None, :], 0), axis=1)


def pick(shaped, order):
    blocks = [
        lax.dynamic_index_in_dim(shaped, order[at], 1, keepdims=True)
        for at in range(order.shape[0])
    ]
    return jnp.concatenate(blocks, axis=1)


def outgoing(values, slot_group, group_count, group_width):
    shaped = values.reshape(values.shape[0], group_count, group_width)
    return pick(shaped, slot_group)


def incoming(received, source, in_range):
    picked = pick(received, source)
    picked = jnp.where(in_range[None, :, None], picked, jnp.zeros((), picked.dtype))
    return picked.reshape(picked.shape[0], -1)


def body(inputs, cotangent, residue, decay, skip_gain, band_blocks):
    values = inputs.astype(jnp.float32)
    upstream = cotangent.astype(jnp.float32)
    bands = band_blocks[0]
    block_rows, channels = values.shape
    group_count = bands.shape[0]
    group_width = channels // group_count
    ctx_rank = lax.axis_index("ctx")
    offsets = jnp.arange(block_rows, dtype=jnp.float32)[:, None]
    lengths = jnp.repeat(
        (bands + 1) * block_rows, group_width, total_repeat_length=channels
    ).astype(jnp.float32)
    band_tail = jnp.exp(-decay * lengths)[None, :]
    block_decay = jnp.exp(-decay * block_rows)
    lead_decay = jnp.exp(-decay[None, :] * (offsets + 1.0))
    trail_decay = jnp.exp(-decay[None, :] * (block_rows - offsets))
    zero_state = jnp.zeros_like(decay)
    unit_state = jnp.ones_like(decay)
    inside = local_scan(values, decay, False)
    before, _ = prefix(
        (inside[-1], block_decay), "ctx", chain_step, (zero_state, unit_state), False
    )
    carried = inside + lead_decay * before[None, :]
    send_fwd = slot_groups(bands, ctx_rank, 1)
    source_fwd = ctx_rank - bands - 1
    valid_fwd = source_fwd >= 0
    source_fwd = jnp.clip(source_fwd, 0, group_count - 1)
    inside_back = local_scan(upstream, decay, True)
    after, _ = prefix(
        (inside_back[0], block_decay), "ctx", chain_step, (zero_state, unit_state), True
    )
    back_carried = inside_back + trail_decay * after[None, :]
    send_bwd = slot_groups(bands, ctx_rank, -1)
    source_bwd = ctx_rank + bands + 1
    valid_bwd = source_bwd < group_count
    source_bwd = jnp.clip(source_bwd, 0, group_count - 1)
    received = lax.all_to_all(
        outgoing(carried, send_fwd, group_count, group_width),
        "ctx",
        split_axis=1,
        concat_axis=1,
        tiled=True,
    )
    far_state = incoming(received, source_fwd, valid_fwd)
    received_back = lax.all_to_all(
        outgoing(back_carried, send_bwd, group_count, group_width),
        "ctx",
        split_axis=1,
        concat_axis=1,
        tiled=True,
    )
    near_state = incoming(received_back, source_bwd, valid_bwd)
    truncated = carried - band_tail * far_state
    layer_out = (skip_gain[None, :] * values + residue[None, :] * truncated).astype(jnp.bfloat16)
    back_truncated = back_carried - band_tail * near_state
    input_grad = (skip_gain[None, :] * upstream + residue[None, :] * back_truncated).astype(
        jnp.bfloat16
    )
    position = ctx_rank.astype(jnp.float32) * block_rows + offsets
    weighted = upstream * truncated
    moment = jnp.sum(position * weighted, axis=0) - jnp.sum(
        position * values * back_truncated, axis=0
    )
    grad_terms = jnp.stack(
        [jnp.sum(values * upstream, axis=0), jnp.sum(weighted, axis=0), -decay * residue * moment]
    )
    share_width = channels // lax.axis_size("ctx")
    summed = lax.psum(grad_terms, "ctx")
    own_share = lax.dynamic_slice_in_dim(summed, ctx_rank * share_width, share_width, 1)
    return (layer_out, input_grad, own_share[0], own_share[1], own_share[2])


MESH = pl.DeviceIdType.MESH
LANES = 128
ROWS = 8
PAIR = 2 * ROWS
PIECES = 16
UNROLL = 4
SCOPED = 48_000_000


def greet(count, me):
    barrier = pltpu.get_barrier_semaphore()
    for step in range(1, count):
        pl.semaphore_signal(
            barrier,
            inc=1,
            device_id={"ctx": lax.rem(me + step, count)},
            device_id_type=MESH,
        )
    return lambda: pl.semaphore_wait(barrier, count - 1)


def parts_of(slot, backward):
    if backward:
        return {0: (8, 7, 1), 1: (4, 12)}.get(slot, (PIECES,))
    return {0: (4, 12), 1: (12, 3, 1)}.get(slot, (PIECES,))


def kept_back(slot, backward):
    if backward:
        return 2 if slot == 0 else 0
    return 2 if slot == 1 else 0


def piece_rows(rows, slot, backward, piece):
    parts = parts_of(slot, backward)
    size = rows * parts[piece] // PIECES
    start = rows * sum(parts[:piece]) // PIECES
    return (rows - start - size if backward else start, size)


def piece_at(slot, backward, piece):
    return sum(len(parts_of(before, backward)) for before in range(slot)) + piece


def flow_count(count, backward):
    return sum(len(parts_of(slot, backward)) for slot in range(count - 1))


def end_row(slot, backward):
    return 0 if backward and slot == 0 else slot + 1


def pair_at(step):
    return pl.ds(pl.multiple_of(step * PAIR, PAIR), PAIR)


def banded_kernel(
    count,
    bands_hbm,
    x_hbm,
    c_hbm,
    residue_hbm,
    decay_hbm,
    skip_hbm,
    outs,
    grads,
    own_ref,
    order_ref,
    bands,
    residue_ref,
    decay_ref,
    skip_ref,
    x_first,
    x_rest,
    c_first,
    c_rest,
    xs,
    cs,
    far_x,
    far_c,
    ends,
    far_ends,
    sums,
    shares,
    got,
    blank,
    small_sem,
    load_sem,
    x_send,
    x_recv,
    c_send,
    c_recv,
    e_send,
    e_recv,
    s_send,
    s_recv,
):
    me = lax.axis_index("ctx")
    _, rows, width = xs.shape
    shape = (ROWS, width)
    first = x_first.shape[1]

    all_here = greet(count, me)

    small = [
        pltpu.make_async_copy(source, target, small_sem.at[at])
        for at, (source, target) in enumerate(
            (
                (bands_hbm, bands),
                (decay_hbm, decay_ref),
                (residue_hbm, residue_ref),
                (skip_hbm, skip_ref),
            )
        )
    ]
    small[0].start()
    chunks = (
        (c_hbm, rows - first, c_first, cs),
        (x_hbm, 0, x_first, xs),
        (c_hbm, 0, c_rest, cs),
        (x_hbm, first, x_rest, xs),
    )

    def load(chunk, group):
        source, start, target, _ = chunks[chunk]
        lanes = pl.ds(group * width, width)
        return pltpu.make_async_copy(
            source.at[pl.ds(start, target.shape[1]), lanes],
            target.at[group],
            load_sem.at[chunk, group],
        )

    for chunk in range(len(chunks)):
        for group in range(count):
            load(chunk, group).start()
    for copy in small[1:]:
        copy.start()
    small[0].wait()
    groups = []
    for slot in range(count):
        group = jnp.int32(0)
        for other in range(count):
            group = jnp.where(bands[other] == slot, other, group)
        groups.append(group)

    def pack(chunk):
        _, start, whole, packed = chunks[chunk]
        for group in range(count):
            load(chunk, group).wait()

        def turn(step, _):
            to = pl.ds(pl.multiple_of(start + step * PAIR, PAIR), PAIR)
            for slot in range(count):
                packed[slot, to, :] = whole[groups[slot], pair_at(step), :]
            return 0

        lax.fori_loop(0, whole.shape[1] // PAIR, turn, 0, unroll=UNROLL)

    def has_source(slot, backward):
        return me + slot + 1 < count if backward else me >= slot + 1

    def flow(slot, backward, piece):
        start, size = piece_rows(rows, slot, backward, piece)
        at = pl.ds(start, size)
        sem = piece_at(slot, backward, piece)
        source, target, sends, recvs = (
            (cs, far_c, c_send, c_recv) if backward else (xs, far_x, x_send, x_recv)
        )
        to = me + count - slot - 1 if backward else me + slot + 1
        return pltpu.make_async_remote_copy(
            src_ref=source.at[slot, at],
            dst_ref=target.at[slot, at],
            send_sem=sends.at[sem],
            recv_sem=recvs.at[sem],
            device_id={"ctx": lax.rem(to, count)},
            device_id_type=MESH,
        )

    def send(slot, backward, pieces, asked=True):
        sends_it = jnp.logical_and(has_source(slot, not backward), asked)
        for piece in pieces:
            pl.when(sends_it)(lambda: flow(slot, backward, piece).start())

    def pieces_of(slot, backward):
        return tuple(range(len(parts_of(slot, backward))))

    def end_copy(far, backward, passed_on=False):
        first_row = end_row(far - 1, backward)
        if far == 1 or far == 2 and backward:
            first_row = far - 1
        at = pl.ds(first_row, count + 1 - first_row)
        side = int(backward)
        away = 1 if passed_on else far
        to = me + count - away if backward else me + away
        source = far_ends.at[side, far - 2, at] if passed_on else ends.at[side, at]
        return pltpu.make_async_remote_copy(
            src_ref=source,
            dst_ref=far_ends.at[side, far - 1, at],
            send_sem=e_send.at[side, far - 1],
            recv_sem=e_recv.at[side, far - 1],
            device_id={"ctx": lax.rem(to, count)},
            device_id_type=MESH,
        )

    def sends_end(far, backward):
        outermost = me == far if backward else me + far == count - 1
        reached = has_source(far - 1, not backward)
        return reached if far == 1 else jnp.logical_and(reached, jnp.logical_not(outermost))

    def each_end(fars, may, act):
        for far in fars:
            for backward in (False, True):
                pl.when(may(far, backward))(lambda: act(far, backward))

    def passes_on(far, backward):
        return me == 1 if backward else me == count - 2

    def share_copy(step):
        to = lax.rem(me + step + 1, count)
        return pltpu.make_async_remote_copy(
            src_ref=shares.at[step],
            dst_ref=got.at[step],
            send_sem=s_send.at[step],
            recv_sem=s_recv.at[step],
            device_id={"ctx": to},
            device_id_type=MESH,
        )

    middle = tuple(range(2, count - 1))
    lowest, highest = me == 0, me == count - 1
    outer = jnp.logical_or(lowest, highest)
    keeps_up, keeps_down = me == 1, me == count - 2
    pack(0)
    all_here()
    send(1, True, (0,), jnp.logical_not(highest))
    pack(1)
    send(0, False, (0,))
    pack(2)
    pack(3)
    for copy in small[1:]:
        copy.wait()

    level = lax.broadcasted_iota(jnp.int32, shape, 0)
    depth = level.astype(jnp.float32)
    blank[...] = jnp.zeros(shape, jnp.float32)
    zero = blank[...]
    steps = rows // PAIR
    for slot in range(count):
        rate = decay_ref[groups[slot]]
        leap_pair = jnp.broadcast_to(jnp.exp(-rate * PAIR), shape)
        wide_pair = leap_pair * float(PAIR)
        weighted = {0: (0, 1), 1: (2, 3)}.get(slot, ())

        def turn(step, state):
            held, moments = state
            ahead = xs[slot, pair_at(step), :].astype(jnp.float32)
            back = cs[slot, pair_at(steps - 1 - step), :].astype(jnp.float32)
            parts = (ahead[:ROWS], ahead[ROWS:], back[:ROWS], back[ROWS:])
            moments = tuple(
                moment * leap_pair + held[at] * wide_pair
                for moment, at in zip(moments, weighted)
            )
            return (
                tuple(old * leap_pair + new for old, new in zip(held, parts)),
                moments,
            )

        held, moments = lax.fori_loop(
            0, steps, turn, ((zero,) * 4, (zero,) * len(weighted)), unroll=UNROLL
        )
        apart = (PAIR - 1 - depth, ROWS - 1 - depth, depth, ROWS + depth)
        factors = [jnp.exp(-rate * far) for far in apart]
        scaled = [one * factor for one, factor in zip(held, factors)]
        for side in range(2):
            both = scaled[2 * side] + scaled[2 * side + 1]
            ends[side, end_row(slot, side)] = jnp.sum(both, axis=0, keepdims=True)
        if weighted:
            both = zero
            for moment, at in zip(moments, weighted):
                both = both + factors[at] * moment + apart[at] * scaled[at]
            ends[slot, slot] = jnp.sum(both, axis=0, keepdims=True)
    every, others = range(1, count), range(2, count)
    each_end(every, sends_end, lambda *which: end_copy(*which).start())

    def receives(far, backward):
        return has_source(far - 1, backward)

    def wait_for_ends(fars):
        each_end(fars, receives, lambda *which: end_copy(*which).wait_recv())

    pl.when(outer)(lambda: wait_for_ends((1,)))
    last_up = pieces_of(1, False)[-kept_back(1, False) :]
    last_down = pieces_of(0, True)[-kept_back(0, True) :]
    send(1, True, (0,), highest)
    send(1, True, pieces_of(1, True)[1:])
    for slot in middle:
        send(slot, True, pieces_of(slot, True))
    send(0, True, pieces_of(0, True)[: -len(last_down)])
    send(0, True, last_down, jnp.logical_not(keeps_down))
    for slot in middle[::-1]:
        send(slot, False, pieces_of(slot, False))
    send(0, False, pieces_of(0, False)[1:])
    send(1, False, pieces_of(1, False)[: -len(last_up)])
    send(1, False, last_up, jnp.logical_not(keeps_up))

    for slot in range(count - 1):
        for backward, far in ((False, far_x), (True, far_c)):

            @pl.when(jnp.logical_not(has_source(slot, backward)))
            def _():
                def clear(step, _):
                    far[slot, pair_at(step), :] = jnp.zeros((PAIR, width), far.dtype)
                    return 0

                lax.fori_loop(0, steps, clear, 0, unroll=UNROLL)

    @pl.when(jnp.logical_not(outer))
    def _():
        wait_for_ends(every)
        each_end(others, passes_on, lambda *which: end_copy(*which, True).start())

    pl.when(outer)(lambda: wait_for_ends(others))
    each_end(every, sends_end, lambda *which: end_copy(*which).wait_send())

    def scan(tile, hops):
        for hop, turn, factor in hops:
            tile = tile + factor * pltpu.roll(tile, turn, 0)
        return tile

    def scan_both(tile, moment, hops):
        for hop, turn, factor in hops:
            moved = pltpu.roll(tile, turn, 0)
            moment = moment + factor * (pltpu.roll(moment, turn, 0) + float(hop) * moved)
            tile = tile + factor * moved
        return tile, moment

    def run(slot, backward, mode):
        band = slot + 1
        reach = slot < count - 1
        one = mode == "one"
        rate = decay_ref[groups[slot]]
        start = jnp.zeros((1, width), jnp.float32)
        start_moment = start
        side = int(backward)
        for apart in range(min(band, count - 1)):
            kept = has_source(apart, backward)
            span = float(apart * rows)
            factor = jnp.exp(-rate * span)
            end = far_ends[side, apart, end_row(slot, backward)]
            start = start + jnp.where(kept, factor * end, 0.0)
            if one:
                moment = far_ends[side, apart, slot] + span * end
                start_moment = start_moment + jnp.where(kept, factor * moment, 0.0)
        tail_row = jnp.exp(-rate * float(band * rows))
        tail = jnp.broadcast_to(tail_row, shape)
        far_tail = jnp.broadcast_to(tail_row * float(band * rows), shape)
        leap = jnp.broadcast_to(jnp.exp(-rate * ROWS), shape)
        wide = leap * float(ROWS)
        residue = jnp.broadcast_to(residue_ref[groups[slot]], shape)
        skip = jnp.broadcast_to(skip_ref[groups[slot]], shape)
        ahead = ROWS - depth if backward else depth + 1.0
        lead = jnp.exp(-rate * ahead)
        lead_moment = lead * ahead
        hops = []
        for hop in (1, 2, 4):
            inside = level < ROWS - hop if backward else level >= hop
            factor = jnp.where(inside, jnp.exp(-rate * hop), 0.0)
            hops.append((hop, ROWS - hop if backward else hop, factor))
        source, other_side = (cs, xs) if backward else (xs, cs)
        target = grads if backward else outs
        far_ref = far_c if backward else far_x
        edge = slice(0, 1) if backward else slice(ROWS - 1, ROWS)

        def turn(step, state):
            carry, moment_carry, s_skip, s_w, s_m = state
            if backward:
                step = steps - 1 - step
            at = pair_at(step)
            base = (step * PAIR).astype(jnp.float32)
            values = source[slot, at, :].astype(jnp.float32)
            if mode != "none":
                others = other_side[slot, at, :].astype(jnp.float32)
            if reach:
                far = far_ref[slot, at, :].astype(jnp.float32)
            made = [None, None]
            for half in (1, 0) if backward else (0, 1):
                part = slice(half * ROWS, (half + 1) * ROWS)
                fresh = values[part]
                if reach:
                    fresh = fresh - tail * far[part]
                if one:
                    local, local_moment = scan_both(fresh, -far_tail * far[part], hops)
                    moment = local_moment + lead * moment_carry + lead_moment * carry
                    moment_carry = (
                        leap * moment_carry
                        + wide * carry
                        + jnp.broadcast_to(local_moment[edge], shape)
                    )
                else:
                    local = scan(fresh, hops)
                truncated = local + lead * carry
                carry = leap * carry + jnp.broadcast_to(local[edge], shape)
                made[half] = skip * values[part] + residue * truncated
                if mode != "none":
                    w = others[part] * truncated
                    s_w = s_w + w
                if one:
                    s_m = s_m + others[part] * moment
                elif mode == "two":
                    s_m = s_m + (base + half * ROWS) * w
                if one or mode == "two" and not backward:
                    s_skip = s_skip + values[part] * others[part]
            target[slot, at, :] = jnp.concatenate(made, axis=0).astype(target.dtype)
            return carry, moment_carry, s_skip, s_w, s_m

        state = (
            zero + jnp.broadcast_to(start, shape),
            zero + jnp.broadcast_to(start_moment, shape),
            zero,
            zero,
            zero,
        )
        done = 0
        parts = parts_of(slot, backward) if reach else (PIECES,)
        for piece, part in enumerate(parts):
            if reach:
                pl.when(has_source(slot, backward))(
                    lambda: flow(slot, backward, piece).wait_recv()
                )
            span = (done * steps // PIECES, (done + part) * steps // PIECES)
            state = lax.fori_loop(*span, turn, state, unroll=UNROLL)
            done += part
        return state[2:]

    def close(slot, s_skip, s_w, moment):
        scale = -decay_ref[groups[slot]] * residue_ref[groups[slot]]
        sums[slot, 0] = jnp.sum(s_skip, axis=0, keepdims=True)
        sums[slot, 1] = jnp.sum(s_w, axis=0, keepdims=True)
        sums[slot, 2] = scale * jnp.sum(moment, axis=0, keepdims=True)

    def both_sides(slot):
        s_skip, s_w, s_tw = run(slot, False, "two")
        _, s_v, s_tv = run(slot, True, "two")
        offset = depth + (me * rows).astype(jnp.float32)
        close(slot, s_skip, s_w, (s_tw - s_tv) + offset * (s_w - s_v))

    both_sides(count - 1)
    for slot in middle[::-1]:
        both_sides(slot)

    @pl.when(has_source(0, False))
    def _():
        close(1, *run(1, True, "one"))
        close(0, *run(0, False, "one"))

    @pl.when(jnp.logical_not(has_source(0, False)))
    def _():
        close(0, *run(0, False, "one"))
        close(1, *run(1, True, "one"))

    for step in range(count - 1):
        share = sums[bands[lax.rem(me + step + 1, count)]]
        shares[step] = share
        share_copy(step).start()
    send(0, True, last_down, keeps_down)
    send(1, False, last_up, keeps_up)

    def wait_sent(which):
        for backward in (False, True):
            for slot in range(count - 1):
                for piece in pieces_of(slot, backward) if which(slot, backward) else ():
                    pl.when(has_source(slot, not backward))(
                        lambda: flow(slot, backward, piece).wait_send()
                    )

    def early_sent():
        each_end(others, passes_on, lambda *which: end_copy(*which, True).wait_send())
        wait_sent(lambda slot, backward: slot != int(not backward))

    @pl.when(has_source(0, True))
    def _():
        run(1, False, "none")
        early_sent()
        run(0, True, "none")

    @pl.when(jnp.logical_not(has_source(0, True)))
    def _():
        run(0, True, "none")
        early_sent()
        run(1, False, "none")

    for step in range(count - 1):
        share_copy(step).wait()
    total = sums[bands[me]]
    for step in range(count - 1):
        total = total + got[step]
    own_ref[...] = total
    for group in range(count):
        order_ref[group] = bands[group]
    wait_sent(lambda slot, backward: slot == int(not backward))


def place_kernel(
    bands, outs, grads, own, out_hbm, grad_hbm, skip_hbm, residue_hbm, decay_hbm, sems, own_sems
):
    count, _, width = outs.shape
    copies = [
        pltpu.make_async_copy(own.at[row], target, own_sems.at[row])
        for row, target in enumerate((skip_hbm, residue_hbm, decay_hbm))
    ]
    for group in range(count):
        slot = bands[group]
        lanes = pl.ds(group * width, width)
        for side, (source, target) in enumerate(((outs, out_hbm), (grads, grad_hbm))):
            copies.append(
                pltpu.make_async_copy(
                    source.at[slot], target.at[:, lanes], sems.at[side, group]
                )
            )
    for copy in copies:
        copy.start()
    for copy in copies:
        copy.wait()


def in_hbm(*arrays):
    return [pltpu.with_memory_space_constraint(one, pltpu.HBM) for one in arrays]


def place(bands, outs, grads, own):
    count, rows, width = outs.shape
    inside = pl.BlockSpec(memory_space=pltpu.VMEM)
    anywhere = pl.BlockSpec(memory_space=pl.ANY)
    whole = jax.ShapeDtypeStruct((rows, count * width), outs.dtype)
    small = jax.ShapeDtypeStruct((1, width), own.dtype)
    return pl.pallas_call(
        place_kernel,
        in_specs=[pl.BlockSpec(memory_space=pltpu.SMEM), inside, inside, inside],
        out_specs=[anywhere] * 5,
        out_shape=(whole, whole, small, small, small),
        scratch_shapes=[
            pltpu.SemaphoreType.DMA((2, count)),
            pltpu.SemaphoreType.DMA((3,)),
        ],
        compiler_params=pltpu.CompilerParams(vmem_limit_bytes=SCOPED),
        name="place",
    )(bands, outs, grads, own)


def banded(count, inputs, cotangent, residue, decay, skip_gain, band_blocks):
    rows, channels = inputs.shape
    width = channels // count
    first = rows * 4 // PIECES
    bands = band_blocks[0]
    anywhere = pl.BlockSpec(memory_space=pl.ANY)
    inside = pl.BlockSpec(memory_space=pltpu.VMEM)
    x_flows = pltpu.SemaphoreType.DMA((flow_count(count, False),))
    c_flows = pltpu.SemaphoreType.DMA((flow_count(count, True),))
    few = pltpu.SemaphoreType.DMA((count - 1,))
    kind = inputs.dtype
    packed = pltpu.VMEM((count, rows, width), kind)
    far = pltpu.VMEM((count - 1, rows, width), kind)
    row = pltpu.VMEM((count, 1, width), jnp.float32)
    ends = pltpu.SemaphoreType.DMA((2, count - 1))
    outs, grads, own, order = pl.pallas_call(
        functools.partial(banded_kernel, count),
        in_specs=[anywhere] * 6,
        out_specs=[inside, inside, inside, pl.BlockSpec(memory_space=pltpu.SMEM)],
        out_shape=(
            pltpu.VMEM((count, rows, width), kind),
            pltpu.VMEM((count, rows, width), kind),
            pltpu.VMEM((3, 1, width), jnp.float32),
            pltpu.SMEM((count,), jnp.int32),
        ),
        scratch_shapes=[
            pltpu.SMEM((count,), jnp.int32),
            row,
            row,
            row,
            pltpu.VMEM((count, first, width), kind),
            pltpu.VMEM((count, rows - first, width), kind),
            pltpu.VMEM((count, first, width), kind),
            pltpu.VMEM((count, rows - first, width), kind),
            packed,
            packed,
            far,
            far,
            pltpu.VMEM((2, count + 1, 1, width), jnp.float32),
            pltpu.VMEM((2, count - 1, count + 1, 1, width), jnp.float32),
            pltpu.VMEM((count, 3, 1, width), jnp.float32),
            pltpu.VMEM((count - 1, 3, 1, width), jnp.float32),
            pltpu.VMEM((count - 1, 3, 1, width), jnp.float32),
            pltpu.VMEM((ROWS, width), jnp.float32),
            pltpu.SemaphoreType.DMA((4,)),
            pltpu.SemaphoreType.DMA((4, count)),
            x_flows,
            x_flows,
            c_flows,
            c_flows,
            ends,
            ends,
            few,
            few,
        ],
        compiler_params=pltpu.CompilerParams(
            collective_id=0, has_side_effects=True, vmem_limit_bytes=SCOPED
        ),
        name="banded",
    )(
        *in_hbm(
            bands,
            inputs,
            cotangent,
            *(part.reshape(count, 1, width) for part in (residue, decay, skip_gain)),
        )
    )
    layer_out, input_grad, *sums = place(order, outs, grads, own)
    return (layer_out, input_grad, *(part.reshape(width) for part in sums))


def local_body(count, inputs, cotangent, residue, decay, skip_gain, band_blocks):
    rows, channels = inputs.shape
    groups = band_blocks.shape[1]
    fits = groups == count and count > 2 and rows % (PAIR * PIECES * UNROLL) == 0
    if fits and channels % (groups * LANES) == 0:
        return banded(count, inputs, cotangent, residue, decay, skip_gain, band_blocks)
    return body(inputs, cotangent, residue, decay, skip_gain, band_blocks)


def solution(mesh):
    placed = (P("ctx", "dp"), P("ctx", "dp"), P("dp"), P("dp"), P("dp"), P("dp", None))
    return jax.shard_map(
        functools.partial(local_body, mesh.shape["ctx"]),
        mesh=mesh,
        in_specs=placed,
        out_specs=(
            P("ctx", "dp"),
            P("ctx", "dp"),
            P(("dp", "ctx")),
            P(("dp", "ctx")),
            P(("dp", "ctx")),
        ),
        check_vma=False,
    )
```
